256 devices in a mesh: tm: 64 (over y, z, core), chan: 4 (over x).
Axes of the slice: x: 4, y: 4, z: 8, core: 2. Of those that a mesh axis runs over, the one named last changes fastest.
Arguments:
- signals: bfloat16 [262144, 2048], P('tm', 'chan')
- channel_node: int32 [2048], P('chan'), may hold values from 0 to 127, as said below
- lag_offsets: int32 [8], replicated, may hold values from 0 to 512, as said below
Outputs:
- r_factor: float32 [1024, 1024], replicated
The draws below stay inside these ranges and needn't reach their ends.
Inputs may be any that keep to these rules, and one draw needn't show every extreme that they name: `channel_node`: every node is named by exactly 16 channels; which channels, and so which channel groups, is drawn. `lag_offsets`: strictly increasing; the first is 0 and the last is 512.
All inputs are finite; a program needn't handle non-finite values.
Results may differ from the reference program's by a relative error of at most 0.0003.
Values sent between devices are 32-bit elements; how exact they have to be, the bound alone decides.
A program may use at most 64 MiB of HBM per device.

```python
import math
import jax
import jax.numpy as jnp
from jax import lax

K = 1024
NODES = 128
CH = 2048
MAXLAG = 512
MODES = 6
TR = 4096
LAGS = 8
TIME = 262144
N_CHAN = 4


def draw_signals(key, part):
    keys = jax.random.split(key, 5)
    period = 4096
    times = jnp.arange(TIME, dtype=jnp.int32)[:, None] % period
    freqs = jax.random.randint(keys[0], (MODES,), 1, 1024)
    phases = jax.random.uniform(keys[1], (MODES,), jnp.float32, 0.0, 2.0 * math.pi)
    shapes = jax.random.normal(keys[2], (MODES, CH), jnp.float32) * 0.35
    scales = jnp.exp(jax.random.uniform(keys[3], (1, CH), jnp.float32, 0.0, math.log(10.0)))
    rows = jnp.arange(TIME, dtype=jnp.int32)[:, None].astype(jnp.float32)
    modal = jnp.zeros((TIME, CH), jnp.float32)
    for mode in range(MODES):
        index = times * freqs[mode] % period
        wave = jnp.sin(index.astype(jnp.float32) * (2.0 * math.pi / period) + phases[mode])
        modal = modal + wave * shapes[mode][None, :]
    noise = jax.random.normal(keys[4], (TIME, CH), jnp.float32)
    envelope = 1.0 + 2.0 * rows / TIME
    base = noise + modal
    return (base * envelope * scales * 0.3).astype(jnp.bfloat16)


def draw_channel_node(key, part):
    order = jax.random.permutation(key, CH)
    return (order % NODES).astype(jnp.int32)


def draw_lag_offsets(key, part):
    inner = jax.random.permutation(key, MAXLAG - 1)[:LAGS - 2] + 1
    inner = jnp.sort(inner.astype(jnp.int32))
    return jnp.concatenate([jnp.zeros((1,), jnp.int32), inner, jnp.full((1,), MAXLAG, jnp.int32)])


def setup_inputs(seed: int = 0) -> dict:
    arg_keys = jax.random.split(jax.random.key(seed), 4)
    return {
        "signals": draw_signals(jax.random.fold_in(arg_keys[3], 71), 0),
        "channel_node": draw_channel_node(jax.random.fold_in(arg_keys[3], 71), 0),
        "lag_offsets": draw_lag_offsets(jax.random.fold_in(arg_keys[3], 71), 0),
    }


def reference(signals, channel_node, lag_offsets):
    group_width = NODES // N_CHAN
    lag_count = K // NODES
    block_rows = TR // N_CHAN
    block_total = TIME // block_rows
    onehot = (channel_node[:, None] == jnp.arange(NODES, dtype=jnp.int32)[None, :]).astype(jnp.float32)
    node_scale = 1.0 / math.sqrt(CH // NODES)

    def node_block(rows_in):
        return jnp.dot(rows_in.astype(jnp.float32), onehot.astype(jnp.float32), precision=lax.Precision.HIGHEST, preferred_element_type=jnp.float32)
    node_signals = lax.map(node_block, signals.reshape(block_total, block_rows, CH)).reshape(TIME, NODES) * node_scale
    padded = jnp.concatenate([node_signals, jnp.zeros((MAXLAG, NODES), jnp.float32)], axis=0)

    def add_block(block_index, gram_matrix):
        row_start = (block_index * block_rows).astype(jnp.int32)
        columns = []
        for group in range(N_CHAN):
            for lag_index in range(lag_count):
                first = (row_start + lag_offsets[lag_index]).astype(jnp.int32)
                columns.append(lax.dynamic_slice(padded, (first, jnp.int32(group * group_width)), (block_rows, group_width)))
        hankel = jnp.concatenate(columns, axis=1)
        return gram_matrix + lax.dot_general(hankel.astype(jnp.float32), hankel.astype(jnp.float32), (((0,), (0,)), ((), ())), precision=lax.Precision.HIGHEST, preferred_element_type=jnp.float32)
    gram_matrix = lax.fori_loop(0, block_total, add_block, jnp.zeros((K, K), jnp.float32))
    gram_matrix = gram_matrix / TIME
    return jnp.linalg.cholesky(gram_matrix).T
```

```python
import functools
import math

import jax
import jax.numpy as jnp
from jax import lax
from jax.experimental import pallas as pl
from jax.experimental.pallas import tpu as pltpu
from jax.sharding import PartitionSpec as P

NODES = 128
CH = 2048
MAXLAG = 512

def lanes(x, c):
    return jnp.broadcast_to(x[:, c:c+1], x.shape)

def subs(x, r):
    return jnp.broadcast_to(x[r:r+1, :], x.shape)

def factor_block(rows, nb):
    count = nb // 8
    lane = lax.broadcasted_iota(jnp.int32, (8, nb), 1)
    sub = lax.broadcasted_iota(jnp.int32, (8, nb), 0)
    rows = list(rows)
    inv = [jnp.where(lane == sub + 8 * i, 1.0, 0.0).astype(jnp.float32) for i in range(count)]
    for p in range(count):
        r0 = 8 * p
        col = [[None] * count for _ in range(8)]
        for j in range(8):
            for b in range(p, count):
                col[j][b] = lanes(rows[b], r0 + j)
        e = [[None] * 8 for _ in range(8)]
        for i in range(8):
            for j in range(i, 8):
                e[i][j] = subs(col[i][p], j)
        rinv = [None] * 8
        for j in range(8):
            rinv[j] = 1.0 / e[j][j]
            for i in range(j + 1, 8):
                for k in range(i, 8):
                    e[i][k] = e[i][k] - (e[j][i] * e[j][k]) * rinv[j]
        diag = e[7][7]
        for j in range(7):
            diag = jnp.where(sub == j, e[j][j], diag)
        rs = lax.rsqrt(diag)
        for b in range(p, count):
            for j in range(8):
                v = col[j][b]
                for i in range(j):
                    v = v - col[i][b] * e[i][j]
                v = v * rinv[j]
                if b == p:
                    v = jnp.where(sub > j, v, 0.0)
                col[j][b] = v
        for j in range(8):
            ra, rw = subs(rows[p], j), subs(inv[p], j)
            for b in range(p, count):
                rows[b] = rows[b] - col[j][b] * ra
                inv[b] = inv[b] - col[j][b] * rw
        rows[p] = jnp.where(lane >= sub + r0, rows[p] * rs, 0.0)
        inv[p] = inv[p] * rs
    return rows, inv

DOT = dict(precision=lax.Precision.HIGHEST, preferred_element_type=jnp.float32)

def chol_body(n, nb, scale, g_ref, r_ref, w_ref, d_ref):
    nblk = n // nb
    r_ref[...] = jnp.zeros_like(r_ref)

    def update(k):
        r0 = k * nb
        if k == 0:
            v = g_ref[0:nb, :] * scale
        else:
            v = g_ref[r0:r0+nb, r0:] * scale - lax.dot_general(
                r_ref[0:r0, r0:r0+nb], r_ref[0:r0, r0:], (((0,), (0,)), ((), ())), **DOT)
        r_ref[r0:r0+nb, r0:] = v
        d_ref[...] = v[:, :nb]

    def panel(k):
        r0 = k * nb
        r_ref[r0:r0+nb, r0:r0+nb] = d_ref[...]
        if k + 1 < nblk:
            r_ref[r0:r0+nb, r0+nb:] = lax.dot_general(
                w_ref[...], r_ref[r0:r0+nb, r0+nb:], (((1,), (0,)), ((), ())), **DOT)

    def step(k, _):
        lax.switch(k, [functools.partial(update, i) for i in range(nblk)])
        rows, inv = factor_block([d_ref[8*i:8*i+8, :] for i in range(nb // 8)], nb)
        for i in range(nb // 8):
            d_ref[8*i:8*i+8, :] = rows[i]
            w_ref[8*i:8*i+8, :] = inv[i]
        lax.switch(k, [functools.partial(panel, i) for i in range(nblk)])
        return 0
    lax.fori_loop(0, nblk, step, 0)

def cholesky_r(g, scale):
    n = g.shape[0]
    nb = 128
    return pl.pallas_call(
        functools.partial(chol_body, n, nb, scale),
        out_shape=jax.ShapeDtypeStruct((n, n), jnp.float32),
        in_specs=[pl.BlockSpec(memory_space=pltpu.VMEM)],
        out_specs=pl.BlockSpec(memory_space=pltpu.VMEM),
        scratch_shapes=[pltpu.VMEM((nb, nb), jnp.float32)] * 2,
        compiler_params=pltpu.CompilerParams(vmem_limit_bytes=48 << 20),
    )(g)


def on_device(signals, channel_node, lag_offsets):
    axes = ("tm", "chan")
    parts = lax.axis_size("tm") * lax.axis_size("chan")
    groups = lax.axis_size("chan")
    lag_count = lag_offsets.shape[0]
    width = NODES // groups
    node_scale = 1.0 / math.sqrt(CH // NODES)
    onehot = (channel_node[:, None] == jnp.arange(NODES, dtype=jnp.int32)[None, :]).astype(
        jnp.bfloat16
    )
    partial_sum = jnp.dot(signals, onehot, preferred_element_type=jnp.float32)
    node_rows = lax.psum_scatter(partial_sum, "chan", scatter_dimension=0, tiled=True) * node_scale
    halo = lax.ppermute(node_rows[:MAXLAG], axes, [(i, i - 1) for i in range(1, parts)])
    extended = jnp.concatenate([node_rows, halo], axis=0)
    rows = node_rows.shape[0]
    columns = []
    for group in range(groups):
        for lag_index in range(lag_count):
            columns.append(
                lax.dynamic_slice(
                    extended, (lag_offsets[lag_index], jnp.int32(group * width)), (rows, width)
                )
            )
    hankel = jnp.concatenate(columns, axis=1)
    local_gram = lax.dot_general(
        hankel,
        hankel,
        (((0,), (0,)), ((), ())),
        precision=lax.Precision.HIGHEST,
        preferred_element_type=jnp.float32,
    )
    gram = lax.psum(local_gram, axes)
    return cholesky_r(gram, 1.0 / (rows * parts))


def solution(mesh):
    in_specs = (P("tm", "chan"), P("chan"), P())
    out_specs = P()
    return jax.shard_map(
        on_device, mesh=mesh, in_specs=in_specs, out_specs=out_specs, check_vma=False
    )
```

```python
import functools
import math

import jax
import jax.numpy as jnp
from jax import lax
from jax.experimental import pallas as pl
from jax.experimental.pallas import tpu as pltpu
from jax.sharding import PartitionSpec as P

NODES = 128
CH = 2048
MAXLAG = 512
F32 = jnp.float32
MESH = pl.DeviceIdType.MESH
VMEM = pl.BlockSpec(memory_space=pltpu.VMEM)
NB = 128


def first_block(i, count):
    return i * count - i * (i - 1) // 2


def gram_body(rows, lag_count, groups, lags_ref, ext_ref, out_ref, rot_ref, hi_ref, lo_ref):
    width = NODES // groups
    per_tile = NB // width
    count = lag_count * NODES // NB
    chunk = 128
    for r in range(1, per_tile):
        rot_ref[r - 1] = pltpu.roll(ext_ref[...], width * r, 1)
    place = lax.broadcasted_iota(jnp.int32, (chunk, NB), 1) // width
    for tile in range(count):
        group, half = tile // (count // groups), tile % (count // groups)

        def build(step, _):
            value = None
            for m in range(per_tile):
                first = lags_ref[half * per_tile + m] + step * chunk
                r = (m - group) % per_tile
                if r == 0:
                    piece = ext_ref[pl.ds(first, chunk), :]
                else:
                    piece = rot_ref[r - 1, pl.ds(first, chunk), :]
                value = piece if value is None else jnp.where(place == m, piece, value)
            high = value.astype(jnp.bfloat16)
            low = (value - high.astype(F32)).astype(jnp.bfloat16)
            at = pl.ds(pl.multiple_of(step * chunk, chunk), chunk)
            hi_ref[at, tile * NB : (tile + 1) * NB] = high
            lo_ref[at, tile * NB : (tile + 1) * NB] = low
            return 0

        lax.fori_loop(0, rows // chunk, build, 0)
    dims = (((0,), (0,)), ((), ()))
    for i in range(count):
        mine = slice(i * NB, (i + 1) * NB)
        rest = slice(i * NB, count * NB)
        a, b = hi_ref[:, mine], lo_ref[:, mine]
        value = lax.dot_general(a, lo_ref[:, rest], dims, preferred_element_type=F32)
        value += lax.dot_general(b, hi_ref[:, rest], dims, preferred_element_type=F32)
        value += lax.dot_general(a, hi_ref[:, rest], dims, preferred_element_type=F32)
        for j in range(i, count):
            out_ref[first_block(i, count) + j - i] = value[:, (j - i) * NB : (j - i + 1) * NB]


def local_gram(lags, extended, rows, groups):
    lag_count = lags.shape[0]
    size = lag_count * NODES
    count = size // NB
    return pl.pallas_call(
        functools.partial(gram_body, rows, lag_count, groups),
        out_shape=jax.ShapeDtypeStruct((count * (count + 1) // 2, NB, NB), F32),
        in_specs=[pl.BlockSpec(memory_space=pltpu.SMEM), VMEM],
        out_specs=VMEM,
        scratch_shapes=[
            pltpu.VMEM((NB // (NODES // groups) - 1,) + extended.shape, F32),
            pltpu.VMEM((rows, size), jnp.bfloat16),
            pltpu.VMEM((rows, size), jnp.bfloat16),
        ],
        compiler_params=pltpu.CompilerParams(vmem_limit_bytes=48 << 20),
    )(lags, extended)


NX, NY, NZ = 4, 4, 8


def place():
    x = lax.axis_index("chan")
    t = lax.axis_index("tm")
    return x, t // (NZ * 2), lax.rem(t // 2, NZ), lax.rem(t, 2)


def device(x, y, z, c):
    return {"tm": (y * NZ + z) * 2 + c, "chan": x}


def remote(src, dst, send, recv, target):
    return pltpu.make_async_remote_copy(
        src_ref=src, dst_ref=dst, send_sem=send, recv_sem=recv,
        device_id=target, device_id_type=MESH,
    )


def sum_body(half, x_ref, out_ref, rc, h, ra, sa, rb, y18, rz, send, recv):
    x, y, z, c = place()
    quarter = half // 2 // 4
    small = quarter // 4
    piece = 2 * small // 6
    barrier = pltpu.get_barrier_semaphore()
    near = [device(x, y, z, 1 - c)]
    near += [device(lax.rem(x + d, NX), y, z, c) for d in range(1, NX)]
    near += [device(x, lax.rem(y + d, NY), z, c) for d in range(1, NY)]
    near += [device(x, y, lax.rem(z + d, NZ), c) for d in range(1, NZ)]
    for dev in near:
        pl.semaphore_signal(barrier, inc=1, device_id=dev, device_id_type=MESH)
    pl.semaphore_wait(barrier, len(near))
    sem = iter(range(64))

    def ring(color, d, first):
        along_x = (color == 0) == first
        if along_x:
            at = lax.rem(x + d, NX)
            return device(at, y, z, c), at
        at = lax.rem(y + d, NY)
        return device(x, at, z, c), at

    work = []
    for color in range(2):
        s = next(sem)
        lo = color * half // 2
        cp = remote(x_ref.at[pl.ds((1 - c) * half + lo, half // 2)], rc.at[pl.ds(lo, half // 2)],
                    send.at[s], recv.at[s], device(x, y, z, 1 - c))
        cp.start()
        work.append(cp)
    for color in range(2):
        work[color].wait_recv()
        lo = color * half // 2
        h[lo : lo + half // 2] = x_ref[pl.ds(c * half + lo, half // 2)] + rc[lo : lo + half // 2]
        for d in range(1, 4):
            s = next(sem)
            dev, at = ring(color, d, True)
            cp = remote(h.at[pl.ds(lo + at * quarter, quarter)], ra.at[color, d - 1],
                        send.at[s], recv.at[s], dev)
            cp.start()
            work.append(cp)
    for color in range(2):
        mine = work[2 + 3 * color : 5 + 3 * color]
        for cp in mine:
            cp.wait_recv()
        _, at = ring(color, 0, True)
        lo = color * half // 2
        sa[color] = ((h[pl.ds(lo + at * quarter, quarter)] + ra[color, 0])
                     + (ra[color, 1] + ra[color, 2]))
        for d in range(1, 4):
            s = next(sem)
            dev, at = ring(color, d, False)
            cp = remote(sa.at[color, pl.ds(at * small, small)], rb.at[color, d - 1],
                        send.at[s], recv.at[s], dev)
            cp.start()
            work.append(cp)
    for color in range(2):
        mine = work[8 + 3 * color : 11 + 3 * color]
        for cp in mine:
            cp.wait_recv()
        _, at = ring(color, 0, False)
        y18[color * small : (color + 1) * small] = (
            (sa[color, pl.ds(at * small, small)] + rb[color, 0]) + (rb[color, 1] + rb[color, 2]))
    for cp in work:
        cp.wait_send()
    zcopies = []
    for d in range(1, NZ):
        s = next(sem)
        to = lax.rem(z + d, NZ)
        own = jnp.minimum(to, 5)
        cp = remote(y18.at[pl.ds(own * piece, piece)], rz.at[d - 1], send.at[s], recv.at[s],
                    device(x, y, to, c))
        pl.when(to < 6)(cp.start)
        zcopies.append((cp, to))
    base = c * half

    def spot(p):
        color = p // 3
        chunk = jnp.where(color == 0, x * 4 + y, y * 4 + x)
        return base + color * (half // 2) + chunk * small + lax.rem(p, 3) * piece

    own = jnp.minimum(z, 5)

    @pl.when(z < 6)
    def _():
        total = y18[pl.ds(own * piece, piece)]
        for d in range(1, NZ):
            zcopies[d - 1][0].wait_recv()
            total = total + rz[d - 1]
        out_ref[pl.ds(spot(own), piece)] = total

    back = []
    for d in range(1, NZ):
        s = next(sem)
        to = lax.rem(z + d, NZ)
        at = pl.ds(spot(own), piece)
        cp = remote(out_ref.at[at], out_ref.at[at], send.at[s], recv.at[s], device(x, y, to, c))
        pl.when(z < 6)(cp.start)
        back.append(cp)
    for d in range(1, NZ):
        source = lax.rem(z - d + NZ, NZ)
        pl.when(source < 6)(back[d - 1].wait_recv)
    work = []
    for color in range(2):
        _, mine = ring(color, 0, True)
        _, sub = ring(color, 0, False)
        at = pl.ds(base + color * (half // 2) + mine * quarter + sub * small, small)
        for d in range(1, 4):
            s = next(sem)
            dev, _ = ring(color, d, False)
            cp = remote(out_ref.at[at], out_ref.at[at], send.at[s], recv.at[s], dev)
            cp.start()
            work.append(cp)
    for color in range(2):
        for cp in work[3 * color : 3 * color + 3]:
            cp.wait_recv()
        _, mine = ring(color, 0, True)
        at = pl.ds(base + color * (half // 2) + mine * quarter, quarter)
        for d in range(1, 4):
            s = next(sem)
            dev, _ = ring(color, d, True)
            cp = remote(out_ref.at[at], out_ref.at[at], send.at[s], recv.at[s], dev)
            cp.start()
            work.append(cp)
    for color in range(2):
        for cp in work[6 + 3 * color : 9 + 3 * color]:
            cp.wait_recv()
        s = next(sem)
        at = pl.ds(base + color * (half // 2), half // 2)
        cp = remote(out_ref.at[at], out_ref.at[at], send.at[s], recv.at[s], device(x, y, z, 1 - c))
        cp.start()
        work.append(cp)
    for cp in work[12:]:
        cp.wait_recv()
    for cp in work:
        cp.wait_send()
    for cp, to in zcopies:
        pl.when(to < 6)(cp.wait_send)
    for cp in back:
        pl.when(z < 6)(cp.wait_send)


def sum_all(value):
    units = value.shape[0]
    half = units // 2
    quarter = half // 8
    small = quarter // 4
    piece = 2 * small // 6
    tile = value.shape[1:]
    buf = lambda *lead: pltpu.VMEM(lead + tile, F32)
    return pl.pallas_call(
        functools.partial(sum_body, half),
        out_shape=jax.ShapeDtypeStruct(value.shape, F32),
        in_specs=[VMEM],
        out_specs=VMEM,
        scratch_shapes=[
            buf(half), buf(half), buf(2, 3, quarter), buf(2, quarter), buf(2, 3, small),
            buf(2 * small), buf(7, piece),
            pltpu.SemaphoreType.DMA((64,)), pltpu.SemaphoreType.DMA((64,)),
        ],
        compiler_params=pltpu.CompilerParams(
            collective_id=1, has_side_effects=True, vmem_limit_bytes=48 << 20),
    )(value)

def lanes(x, c):
    return jnp.broadcast_to(x[:, c : c + 1], x.shape)


def subs(x, r):
    return jnp.broadcast_to(x[r : r + 1, :], x.shape)


def factor_block(rows):
    count = NB // 8
    lane = lax.broadcasted_iota(jnp.int32, (8, NB), 1)
    sub = lax.broadcasted_iota(jnp.int32, (8, NB), 0)
    rows = list(rows)
    inv = [jnp.where(lane == sub + 8 * i, 1.0, 0.0).astype(F32) for i in range(count)]
    for p in range(count):
        r0 = 8 * p
        col = [[None] * count for _ in range(8)]
        for j in range(8):
            for b in range(p, count):
                col[j][b] = lanes(rows[b], r0 + j)
        e = [[None] * 8 for _ in range(8)]
        for i in range(8):
            for j in range(i, 8):
                e[i][j] = subs(col[i][p], j)
        rinv = [None] * 8
        for j in range(8):
            rinv[j] = 1.0 / e[j][j]
            for i in range(j + 1, 8):
                for k in range(i, 8):
                    e[i][k] = e[i][k] - (e[j][i] * e[j][k]) * rinv[j]
        diag = e[7][7]
        for j in range(7):
            diag = jnp.where(sub == j, e[j][j], diag)
        rs = lax.rsqrt(diag)
        for b in range(p, count):
            for j in range(8):
                v = col[j][b]
                for i in range(j):
                    v = v - col[i][b] * e[i][j]
                v = v * rinv[j]
                if b == p:
                    v = jnp.where(sub > j, v, 0.0)
                col[j][b] = v
        for j in range(8):
            ra, rw = subs(rows[p], j), subs(inv[p], j)
            for b in range(p, count):
                rows[b] = rows[b] - col[j][b] * ra
                inv[b] = inv[b] - col[j][b] * rw
        rows[p] = jnp.where(lane >= sub + r0, rows[p] * rs, 0.0)
        inv[p] = inv[p] * rs
    return rows, inv


DOT = dict(precision=lax.Precision.HIGHEST, preferred_element_type=F32)


def factor_body(count, scale, g_ref, r_ref, w_ref, d_ref):
    r_ref[...] = jnp.zeros_like(r_ref)

    def update(k):
        r0 = k * NB
        first = first_block(k, count)
        for j in range(k, count):
            r_ref[r0 : r0 + NB, j * NB : (j + 1) * NB] = g_ref[first + j - k] * scale
        if k > 0:
            r_ref[r0 : r0 + NB, r0:] -= lax.dot_general(
                r_ref[0:r0, r0 : r0 + NB], r_ref[0:r0, r0:], (((0,), (0,)), ((), ())), **DOT
            )
        d_ref[...] = r_ref[r0 : r0 + NB, r0 : r0 + NB]

    def panel(k):
        r0 = k * NB
        r_ref[r0 : r0 + NB, r0 : r0 + NB] = d_ref[...]
        if k + 1 < count:
            r_ref[r0 : r0 + NB, r0 + NB :] = lax.dot_general(
                w_ref[...], r_ref[r0 : r0 + NB, r0 + NB :], (((1,), (0,)), ((), ())), **DOT
            )

    def step(k, _):
        lax.switch(k, [functools.partial(update, i) for i in range(count)])
        rows, inv = factor_block([d_ref[8 * i : 8 * i + 8, :] for i in range(NB // 8)])
        for i in range(NB // 8):
            d_ref[8 * i : 8 * i + 8, :] = rows[i]
            w_ref[8 * i : 8 * i + 8, :] = inv[i]
        lax.switch(k, [functools.partial(panel, i) for i in range(count)])
        return 0

    lax.fori_loop(0, count, step, 0)


def upper_factor(blocks, count, scale):
    size = count * NB
    return pl.pallas_call(
        functools.partial(factor_body, count, scale),
        out_shape=jax.ShapeDtypeStruct((size, size), F32),
        in_specs=[VMEM],
        out_specs=VMEM,
        scratch_shapes=[pltpu.VMEM((NB, NB), F32)] * 2,
        compiler_params=pltpu.CompilerParams(vmem_limit_bytes=48 << 20),
    )(blocks)

def on_device(signals, channel_node, lag_offsets):
    axes = ("tm", "chan")
    parts = lax.axis_size("tm") * lax.axis_size("chan")
    groups = lax.axis_size("chan")
    count = lag_offsets.shape[0] * NODES // NB
    node_scale = 1.0 / math.sqrt(CH // NODES)
    onehot = (channel_node[:, None] == jnp.arange(NODES, dtype=jnp.int32)[None, :]).astype(
        jnp.bfloat16
    )
    partial_sum = jnp.dot(signals, onehot, preferred_element_type=jnp.float32)
    node_rows = lax.psum_scatter(partial_sum, "chan", scatter_dimension=0, tiled=True) * node_scale
    halo = lax.ppermute(node_rows[:MAXLAG], axes, [(i, i - 1) for i in range(1, parts)])
    extended = jnp.concatenate([node_rows, halo], axis=0)
    rows = node_rows.shape[0]
    blocks = local_gram(lag_offsets, extended, rows, groups)
    total = sum_all(blocks.reshape(-1, 8, NB)).reshape(blocks.shape)
    return upper_factor(total, count, 1.0 / (rows * parts))


def solution(mesh):
    in_specs = (P("tm", "chan"), P("chan"), P())
    out_specs = P()
    return jax.shard_map(
        on_device, mesh=mesh, in_specs=in_specs, out_specs=out_specs, check_vma=False
    )
```

```python
import functools
import math

import jax
import jax.numpy as jnp
from jax import lax
from jax.experimental import pallas as pl
from jax.experimental.pallas import tpu as pltpu
from jax.sharding import PartitionSpec as P

NODES = 128
CH = 2048
MAXLAG = 512
F32 = jnp.float32
MESH = pl.DeviceIdType.MESH
VMEM = pl.BlockSpec(memory_space=pltpu.VMEM)
NB = 128


def first_block(i, count):
    return i * count - i * (i - 1) // 2


def gram_body(rows, lag_count, groups, lags_ref, ext_ref, out_ref, rot_ref, hi_ref, lo_ref):
    width = NODES // groups
    per_tile = NB // width
    count = lag_count * NODES // NB
    chunk = 128
    for r in range(1, per_tile):
        rot_ref[r - 1] = pltpu.roll(ext_ref[...], width * r, 1)
    place = lax.broadcasted_iota(jnp.int32, (chunk, NB), 1) // width
    for tile in range(count):
        group, half = tile // (count // groups), tile % (count // groups)

        def build(step, _):
            value = None
            for m in range(per_tile):
                first = lags_ref[half * per_tile + m] + step * chunk
                r = (m - group) % per_tile
                if r == 0:
                    piece = ext_ref[pl.ds(first, chunk), :]
                else:
                    piece = rot_ref[r - 1, pl.ds(first, chunk), :]
                value = piece if value is None else jnp.where(place == m, piece, value)
            high = value.astype(jnp.bfloat16)
            low = (value - high.astype(F32)).astype(jnp.bfloat16)
            at = pl.ds(pl.multiple_of(step * chunk, chunk), chunk)
            hi_ref[at, tile * NB : (tile + 1) * NB] = high
            lo_ref[at, tile * NB : (tile + 1) * NB] = low
            return 0

        lax.fori_loop(0, rows // chunk, build, 0)
    dims = (((0,), (0,)), ((), ()))
    for i in range(count):
        mine = slice(i * NB, (i + 1) * NB)
        rest = slice(i * NB, count * NB)
        a, b = hi_ref[:, mine], lo_ref[:, mine]
        value = lax.dot_general(a, lo_ref[:, rest], dims, preferred_element_type=F32)
        value += lax.dot_general(b, hi_ref[:, rest], dims, preferred_element_type=F32)
        value += lax.dot_general(a, hi_ref[:, rest], dims, preferred_element_type=F32)
        for j in range(i, count):
            out_ref[first_block(i, count) + j - i] = value[:, (j - i) * NB : (j - i + 1) * NB]


def local_gram(lags, extended, rows, groups):
    lag_count = lags.shape[0]
    size = lag_count * NODES
    count = size // NB
    return pl.pallas_call(
        functools.partial(gram_body, rows, lag_count, groups),
        out_shape=jax.ShapeDtypeStruct((count * (count + 1) // 2, NB, NB), F32),
        in_specs=[pl.BlockSpec(memory_space=pltpu.SMEM), VMEM],
        out_specs=VMEM,
        scratch_shapes=[
            pltpu.VMEM((NB // (NODES // groups) - 1,) + extended.shape, F32),
            pltpu.VMEM((rows, size), jnp.bfloat16),
            pltpu.VMEM((rows, size), jnp.bfloat16),
        ],
        compiler_params=pltpu.CompilerParams(vmem_limit_bytes=48 << 20),
    )(lags, extended)


NX, NY, NZ = 4, 4, 8


def place():
    x = lax.axis_index("chan")
    t = lax.axis_index("tm")
    return x, t // (NZ * 2), lax.rem(t // 2, NZ), lax.rem(t, 2)


def device(x, y, z, c):
    return {"tm": (y * NZ + z) * 2 + c, "chan": x}


def remote(src, dst, send, recv, target):
    return pltpu.make_async_remote_copy(
        src_ref=src, dst_ref=dst, send_sem=send, recv_sem=recv,
        device_id=target, device_id_type=MESH,
    )


def sum_body(half, x_ref, out_ref, rc, h, ra, sa, rb, y18, rz, send, recv):
    x, y, z, c = place()
    quarter = half // 2 // 4
    small = quarter // 4
    piece = 2 * small // 6
    barrier = pltpu.get_barrier_semaphore()
    near = [device(x, y, z, 1 - c)]
    near += [device(lax.rem(x + d, NX), y, z, c) for d in range(1, NX)]
    near += [device(x, lax.rem(y + d, NY), z, c) for d in range(1, NY)]
    near += [device(x, y, lax.rem(z + d, NZ), c) for d in range(1, NZ)]
    for dev in near:
        pl.semaphore_signal(barrier, inc=1, device_id=dev, device_id_type=MESH)
    pl.semaphore_wait(barrier, len(near))
    sem = iter(range(64))

    def ring(color, d, first):
        along_x = (color == 0) == first
        if along_x:
            at = lax.rem(x + d, NX)
            return device(at, y, z, c), at
        at = lax.rem(y + d, NY)
        return device(x, at, z, c), at

    work = []
    for color in range(2):
        s = next(sem)
        lo = color * half // 2
        cp = remote(x_ref.at[pl.ds((1 - c) * half + lo, half // 2)], rc.at[pl.ds(lo, half // 2)],
                    send.at[s], recv.at[s], device(x, y, z, 1 - c))
        cp.start()
        work.append(cp)
    for color in range(2):
        work[color].wait_recv()
        lo = color * half // 2
        h[lo : lo + half // 2] = x_ref[pl.ds(c * half + lo, half // 2)] + rc[lo : lo + half // 2]
        for d in range(1, 4):
            s = next(sem)
            dev, at = ring(color, d, True)
            cp = remote(h.at[pl.ds(lo + at * quarter, quarter)], ra.at[color, d - 1],
                        send.at[s], recv.at[s], dev)
            cp.start()
            work.append(cp)
    for color in range(2):
        mine = work[2 + 3 * color : 5 + 3 * color]
        for cp in mine:
            cp.wait_recv()
        _, at = ring(color, 0, True)
        lo = color * half // 2
        sa[color] = ((h[pl.ds(lo + at * quarter, quarter)] + ra[color, 0])
                     + (ra[color, 1] + ra[color, 2]))
        for d in range(1, 4):
            s = next(sem)
            dev, at = ring(color, d, False)
            cp = remote(sa.at[color, pl.ds(at * small, small)], rb.at[color, d - 1],
                        send.at[s], recv.at[s], dev)
            cp.start()
            work.append(cp)
    for color in range(2):
        mine = work[8 + 3 * color : 11 + 3 * color]
        for cp in mine:
            cp.wait_recv()
        _, at = ring(color, 0, False)
        y18[color * small : (color + 1) * small] = (
            (sa[color, pl.ds(at * small, small)] + rb[color, 0]) + (rb[color, 1] + rb[color, 2]))
    for cp in work:
        cp.wait_send()
    zcopies = []
    for d in range(1, NZ):
        s = next(sem)
        to = lax.rem(z + d, NZ)
        own = jnp.minimum(to, 5)
        cp = remote(y18.at[pl.ds(own * piece, piece)], rz.at[d - 1], send.at[s], recv.at[s],
                    device(x, y, to, c))
        pl.when(to < 6)(cp.start)
        zcopies.append((cp, to))
    base = c * half

    def spot(p):
        color = p // 3
        chunk = jnp.where(color == 0, x * 4 + y, y * 4 + x)
        return base + color * (half // 2) + chunk * small + lax.rem(p, 3) * piece

    own = jnp.minimum(z, 5)

    @pl.when(z < 6)
    def _():
        total = y18[pl.ds(own * piece, piece)]
        for d in range(1, NZ):
            zcopies[d - 1][0].wait_recv()
            total = total + rz[d - 1]
        out_ref[pl.ds(spot(own), piece)] = total

    back = []
    for d in range(1, NZ):
        s = next(sem)
        to = lax.rem(z + d, NZ)
        at = pl.ds(spot(own), piece)
        cp = remote(out_ref.at[at], out_ref.at[at], send.at[s], recv.at[s], device(x, y, to, c))
        pl.when(z < 6)(cp.start)
        back.append(cp)
    for d in range(1, NZ):
        source = lax.rem(z - d + NZ, NZ)
        pl.when(source < 6)(back[d - 1].wait_recv)
    work = []
    for color in range(2):
        _, mine = ring(color, 0, True)
        _, sub = ring(color, 0, False)
        at = pl.ds(base + color * (half // 2) + mine * quarter + sub * small, small)
        for d in range(1, 4):
            s = next(sem)
            dev, _ = ring(color, d, False)
            cp = remote(out_ref.at[at], out_ref.at[at], send.at[s], recv.at[s], dev)
            cp.start()
            work.append(cp)
    for color in range(2):
        for cp in work[3 * color : 3 * color + 3]:
            cp.wait_recv()
        _, mine = ring(color, 0, True)
        at = pl.ds(base + color * (half // 2) + mine * quarter, quarter)
        for d in range(1, 4):
            s = next(sem)
            dev, _ = ring(color, d, True)
            cp = remote(out_ref.at[at], out_ref.at[at], send.at[s], recv.at[s], dev)
            cp.start()
            work.append(cp)
    for color in range(2):
        for cp in work[6 + 3 * color : 9 + 3 * color]:
            cp.wait_recv()
        s = next(sem)
        at = pl.ds(base + color * (half // 2), half // 2)
        cp = remote(out_ref.at[at], out_ref.at[at], send.at[s], recv.at[s], device(x, y, z, 1 - c))
        cp.start()
        work.append(cp)
    for cp in work[12:]:
        cp.wait_recv()
    for cp in work:
        cp.wait_send()
    for cp, to in zcopies:
        pl.when(to < 6)(cp.wait_send)
    for cp in back:
        pl.when(z < 6)(cp.wait_send)


def sum_all(value):
    units = value.shape[0]
    half = units // 2
    quarter = half // 8
    small = quarter // 4
    piece = 2 * small // 6
    tile = value.shape[1:]
    buf = lambda *lead: pltpu.VMEM(lead + tile, F32)
    return pl.pallas_call(
        functools.partial(sum_body, half),
        out_shape=jax.ShapeDtypeStruct(value.shape, F32),
        in_specs=[VMEM],
        out_specs=VMEM,
        scratch_shapes=[
            buf(half), buf(half), buf(2, 3, quarter), buf(2, quarter), buf(2, 3, small),
            buf(2 * small), buf(7, piece),
            pltpu.SemaphoreType.DMA((64,)), pltpu.SemaphoreType.DMA((64,)),
        ],
        compiler_params=pltpu.CompilerParams(
            collective_id=1, has_side_effects=True, vmem_limit_bytes=48 << 20),
    )(value)

def node_body(s_hbm, node_ref, ext_ref, sig, part, far, near, pair, fwd, load, send, recv):
    x, y, z, c = place()
    t = lax.axis_index("tm")
    rows = part.shape[0] // 4
    half, quarter = rows // 2, rows // 4

    def chunk_of(at):
        return jnp.where(c == 0, at, 3 - at)

    flip = (lambda v: v + 1 - 2 * lax.rem(v, 2), lambda v: 3 - v)
    others = (flip[0](x), flip[1](x))
    opposite = lax.rem(x + 2, 4)
    order = (opposite, others[0], others[1], x)
    loads = []
    for ph in range(2):
        for i, at in enumerate(order):
            rows_at = pl.ds(pl.multiple_of(chunk_of(at) * rows + ph * half, half), half)
            cp = pltpu.make_async_copy(s_hbm.at[rows_at], sig.at[rows_at], load.at[ph * 4 + i])
            cp.start()
            loads.append((cp, rows_at))
    b = chunk_of(x)
    has_to = jnp.logical_or(b > 0, t > 0)
    has_from = jnp.logical_or(b < 3, t < 2 * NY * NZ - 1)
    step = 1 - 2 * c
    to = {"tm": jnp.where(b > 0, t, jnp.maximum(t - 1, 0)), "chan": jnp.where(b > 0, x - step, x)}
    source = {"tm": jnp.where(b < 3, t, jnp.minimum(t + 1, 2 * NY * NZ - 1)),
              "chan": jnp.where(b < 3, x + step, x)}
    barrier = pltpu.get_barrier_semaphore()
    link = tuple(device(at, y, z, c) for at in others)
    for dev in link:
        pl.semaphore_signal(barrier, inc=1, device_id=dev, device_id_type=MESH)

    @pl.when(has_to)
    def _():
        pl.semaphore_signal(barrier, inc=1, device_id=to, device_id_type=MESH)

    @pl.when(has_from)
    def _():
        pl.semaphore_signal(barrier, inc=1, device_id=source, device_id_type=MESH)

    scale = 1.0 / math.sqrt(CH // NODES)
    chans = node_ref.shape[1]
    match = lax.broadcasted_iota(jnp.int32, (NODES, chans), 0) == node_ref[...]
    onehot = jnp.where(match, scale, 0.0).astype(jnp.bfloat16)

    def sums(ph, i):
        cp, rows_at = loads[ph * 4 + i]
        cp.wait()
        part[rows_at] = lax.dot_general(sig[rows_at], onehot, (((1,), (1,)), ((), ())),
                                        preferred_element_type=F32)

    def piece(at, ph, color):
        return pl.ds(pl.multiple_of(chunk_of(at) * rows + ph * half + color * quarter, quarter), quarter)

    def copy(src, dst, kind, ph, color, dev):
        s = (kind * 2 + ph) * 2 + color
        return remote(src, dst, send.at[s], recv.at[s], dev)

    def fars(ph):
        return [copy(part.at[piece(opposite, ph, k)], far.at[ph, k], 0, ph, k, link[k]) for k in range(2)]

    def nears(ph):
        return [copy(part.at[piece(others[k], ph, k)], near.at[ph, k], 1, ph, k, link[k]) for k in range(2)]

    def forwards(ph):
        return [copy(fwd.at[ph, k], pair.at[ph, k], 2, ph, k, link[1 - k]) for k in range(2)]

    sums(0, 0)
    count = 2 + has_to.astype(jnp.int32) + has_from.astype(jnp.int32)
    pl.semaphore_wait(barrier, count)
    work = [fars(0), nears(0), forwards(0), fars(1), nears(1), forwards(1)]

    def forward(ph):
        for k in range(2):
            work[3 * ph][k].wait_recv()
            fwd[ph, k] = part[piece(others[1 - k], ph, k)] + far[ph, k]
            work[3 * ph + 2][k].start()

    def finish(ph):
        for k in range(2):
            work[3 * ph + 1][k].wait_recv()
            work[3 * ph + 2][k].wait_recv()
            at = ph * half + k * quarter
            ext_ref[at : at + quarter] = part[piece(x, ph, k)] + near[ph, k] + pair[ph, k]

    for cp in work[0]:
        cp.start()
    sums(0, 1)
    work[1][0].start()
    sums(0, 2)
    work[1][1].start()
    for i in range(4):
        sums(1, i)
    sums(0, 3)
    forward(0)
    for cp in work[3] + work[4]:
        cp.start()
    finish(0)
    forward(1)
    halo = remote(ext_ref.at[0:half], ext_ref.at[rows : rows + half], send.at[12], recv.at[12], to)
    pl.when(has_to)(halo.start)

    @pl.when(jnp.logical_not(has_from))
    def _():
        ext_ref[rows : rows + half] = jnp.zeros((half, NODES), F32)

    finish(1)
    pl.when(has_from)(halo.wait_recv)
    for pair_of in work:
        for cp in pair_of:
            cp.wait_send()
    pl.when(has_to)(halo.wait_send)


def node_rows(signals, channel_node):
    length, chans = signals.shape
    rows = length // 4
    quarter = rows // 4
    buf = lambda: pltpu.VMEM((2, 2, quarter, NODES), F32)
    return pl.pallas_call(
        node_body,
        out_shape=jax.ShapeDtypeStruct((rows + MAXLAG, NODES), F32),
        in_specs=[pl.BlockSpec(memory_space=pl.ANY), VMEM],
        out_specs=VMEM,
        scratch_shapes=[
            pltpu.VMEM((length, chans), jnp.bfloat16), pltpu.VMEM((length, NODES), F32),
            buf(), buf(), buf(), buf(),
            pltpu.SemaphoreType.DMA((8,)), pltpu.SemaphoreType.DMA((13,)),
            pltpu.SemaphoreType.DMA((13,)),
        ],
        compiler_params=pltpu.CompilerParams(
            collective_id=2, has_side_effects=True, vmem_limit_bytes=48 << 20),
    )(signals, channel_node.reshape(1, chans))


def lanes(x, c):
    return jnp.broadcast_to(x[:, c : c + 1], x.shape)


def subs(x, r):
    return jnp.broadcast_to(x[r : r + 1, :], x.shape)


def factor_block(rows):
    count = NB // 8
    lane = lax.broadcasted_iota(jnp.int32, (8, NB), 1)
    sub = lax.broadcasted_iota(jnp.int32, (8, NB), 0)
    rows = list(rows)
    inv = [jnp.where(lane == sub + 8 * i, 1.0, 0.0).astype(F32) for i in range(count)]
    for p in range(count):
        r0 = 8 * p
        col = [[None] * count for _ in range(8)]
        for j in range(8):
            for b in range(p, count):
                col[j][b] = lanes(rows[b], r0 + j)
        e = [[None] * 8 for _ in range(8)]
        for i in range(8):
            for j in range(i, 8):
                e[i][j] = subs(col[i][p], j)
        rinv = [None] * 8
        for j in range(8):
            rinv[j] = 1.0 / e[j][j]
            for i in range(j + 1, 8):
                for k in range(i, 8):
                    e[i][k] = e[i][k] - (e[j][i] * e[j][k]) * rinv[j]
        diag = e[7][7]
        for j in range(7):
            diag = jnp.where(sub == j, e[j][j], diag)
        rs = lax.rsqrt(diag)
        for b in range(p, count):
            for j in range(8):
                v = col[j][b]
                for i in range(j):
                    v = v - col[i][b] * e[i][j]
                v = v * rinv[j]
                if b == p:
                    v = jnp.where(sub > j, v, 0.0)
                col[j][b] = v
        for j in range(8):
            ra, rw = subs(rows[p], j), subs(inv[p], j)
            for b in range(p, count):
                rows[b] = rows[b] - col[j][b] * ra
                inv[b] = inv[b] - col[j][b] * rw
        rows[p] = jnp.where(lane >= sub + r0, rows[p] * rs, 0.0)
        inv[p] = inv[p] * rs
    return rows, inv


DOT = dict(precision=lax.Precision.HIGHEST, preferred_element_type=F32)


def factor_body(count, scale, g_ref, r_ref, w_ref, d_ref):
    r_ref[...] = jnp.zeros_like(r_ref)

    def update(k):
        r0 = k * NB
        first = first_block(k, count)
        for j in range(k, count):
            r_ref[r0 : r0 + NB, j * NB : (j + 1) * NB] = g_ref[first + j - k] * scale
        if k > 0:
            r_ref[r0 : r0 + NB, r0:] -= lax.dot_general(
                r_ref[0:r0, r0 : r0 + NB], r_ref[0:r0, r0:], (((0,), (0,)), ((), ())), **DOT
            )
        d_ref[...] = r_ref[r0 : r0 + NB, r0 : r0 + NB]

    def panel(k):
        r0 = k * NB
        r_ref[r0 : r0 + NB, r0 : r0 + NB] = d_ref[...]
        if k + 1 < count:
            r_ref[r0 : r0 + NB, r0 + NB :] = lax.dot_general(
                w_ref[...], r_ref[r0 : r0 + NB, r0 + NB :], (((1,), (0,)), ((), ())), **DOT
            )

    def step(k, _):
        lax.switch(k, [functools.partial(update, i) for i in range(count)])
        rows, inv = factor_block([d_ref[8 * i : 8 * i + 8, :] for i in range(NB // 8)])
        for i in range(NB // 8):
            d_ref[8 * i : 8 * i + 8, :] = rows[i]
            w_ref[8 * i : 8 * i + 8, :] = inv[i]
        lax.switch(k, [functools.partial(panel, i) for i in range(count)])
        return 0

    lax.fori_loop(0, count, step, 0)


def upper_factor(blocks, count, scale):
    size = count * NB
    return pl.pallas_call(
        functools.partial(factor_body, count, scale),
        out_shape=jax.ShapeDtypeStruct((size, size), F32),
        in_specs=[VMEM],
        out_specs=VMEM,
        scratch_shapes=[pltpu.VMEM((NB, NB), F32)] * 2,
        compiler_params=pltpu.CompilerParams(vmem_limit_bytes=48 << 20),
    )(blocks)

def on_device(signals, channel_node, lag_offsets):
    parts = lax.axis_size("tm") * lax.axis_size("chan")
    groups = lax.axis_size("chan")
    count = lag_offsets.shape[0] * NODES // NB
    rows = signals.shape[0] // groups
    extended = node_rows(signals, channel_node)
    blocks = local_gram(lag_offsets, extended, rows, groups)
    total = sum_all(blocks.reshape(-1, 8, NB)).reshape(blocks.shape)
    return upper_factor(total, count, 1.0 / (rows * parts))


def solution(mesh):
    in_specs = (P("tm", "chan"), P("chan"), P())
    out_specs = P()
    return jax.shard_map(
        on_device, mesh=mesh, in_specs=in_specs, out_specs=out_specs, check_vma=False
    )
```

```python
import functools
import math

import jax
import jax.numpy as jnp
from jax import lax
from jax.experimental import pallas as pl
from jax.experimental.pallas import tpu as pltpu
from jax.sharding import PartitionSpec as P

NODES = 128
CH = 2048
MAXLAG = 512
F32 = jnp.float32
MESH = pl.DeviceIdType.MESH
VMEM = pl.BlockSpec(memory_space=pltpu.VMEM)
NB = 128


def first_block(i, count):
    return i * count - i * (i - 1) // 2


def gram_body(rows, lag_count, groups, lags_ref, ext_ref, out_ref, rot_ref, hi_ref, lo_ref):
    width = NODES // groups
    per_tile = NB // width
    count = lag_count * NODES // NB
    chunk = 128
    for r in range(1, per_tile):
        rot_ref[r - 1] = pltpu.roll(ext_ref[...], width * r, 1)
    place = lax.broadcasted_iota(jnp.int32, (chunk, NB), 1) // width
    for tile in range(count):
        group, half = tile // (count // groups), tile % (count // groups)

        def build(step, _):
            value = None
            for m in range(per_tile):
                first = lags_ref[half * per_tile + m] + step * chunk
                r = (m - group) % per_tile
                if r == 0:
                    piece = ext_ref[pl.ds(first, chunk), :]
                else:
                    piece = rot_ref[r - 1, pl.ds(first, chunk), :]
                value = piece if value is None else jnp.where(place == m, piece, value)
            high = value.astype(jnp.bfloat16)
            low = (value - high.astype(F32)).astype(jnp.bfloat16)
            at = pl.ds(pl.multiple_of(step * chunk, chunk), chunk)
            hi_ref[at, tile * NB : (tile + 1) * NB] = high
            lo_ref[at, tile * NB : (tile + 1) * NB] = low
            return 0

        lax.fori_loop(0, rows // chunk, build, 0)
    dims = (((0,), (0,)), ((), ()))
    for i in range(count):
        mine = slice(i * NB, (i + 1) * NB)
        rest = slice(i * NB, count * NB)
        a, b = hi_ref[:, mine], lo_ref[:, mine]
        value = lax.dot_general(a, lo_ref[:, rest], dims, preferred_element_type=F32)
        value += lax.dot_general(b, hi_ref[:, rest], dims, preferred_element_type=F32)
        value += lax.dot_general(a, hi_ref[:, rest], dims, preferred_element_type=F32)
        for j in range(i, count):
            out_ref[first_block(i, count) + j - i] = value[:, (j - i) * NB : (j - i + 1) * NB]


def local_gram(lags, extended, rows, groups):
    lag_count = lags.shape[0]
    size = lag_count * NODES
    count = size // NB
    return pl.pallas_call(
        functools.partial(gram_body, rows, lag_count, groups),
        out_shape=jax.ShapeDtypeStruct((count * (count + 1) // 2, NB, NB), F32),
        in_specs=[pl.BlockSpec(memory_space=pltpu.SMEM), VMEM],
        out_specs=VMEM,
        scratch_shapes=[
            pltpu.VMEM((NB // (NODES // groups) - 1,) + extended.shape, F32),
            pltpu.VMEM((rows, size), jnp.bfloat16),
            pltpu.VMEM((rows, size), jnp.bfloat16),
        ],
        compiler_params=pltpu.CompilerParams(vmem_limit_bytes=48 << 20),
    )(lags, extended)


NX, NY, NZ = 4, 4, 8


def place():
    x = lax.axis_index("chan")
    t = lax.axis_index("tm")
    return x, t // (NZ * 2), lax.rem(t // 2, NZ), lax.rem(t, 2)


def device(x, y, z, c):
    return {"tm": (y * NZ + z) * 2 + c, "chan": x}


def remote(src, dst, send, recv, target):
    return pltpu.make_async_remote_copy(
        src_ref=src, dst_ref=dst, send_sem=send, recv_sem=recv,
        device_id=target, device_id_type=MESH,
    )


def sum_body(half, x_ref, out_ref, rc, h, ra, sa, rb, y18, rz, send, recv):
    x, y, z, c = place()
    quarter = half // 2 // 4
    small = quarter // 4
    piece = 2 * small // 6
    barrier = pltpu.get_barrier_semaphore()
    near = [device(x, y, z, 1 - c)]
    near += [device(lax.rem(x + d, NX), y, z, c) for d in range(1, NX)]
    near += [device(x, lax.rem(y + d, NY), z, c) for d in range(1, NY)]
    near += [device(x, y, lax.rem(z + d, NZ), c) for d in range(1, NZ)]
    for dev in near:
        pl.semaphore_signal(barrier, inc=1, device_id=dev, device_id_type=MESH)
    pl.semaphore_wait(barrier, len(near))
    sem = iter(range(64))

    def ring(color, d, first):
        along_x = (color == 0) == first
        if along_x:
            at = lax.rem(x + d, NX)
            return device(at, y, z, c), at
        at = lax.rem(y + d, NY)
        return device(x, at, z, c), at

    work = []
    for color in range(2):
        s = next(sem)
        lo = color * half // 2
        cp = remote(x_ref.at[pl.ds((1 - c) * half + lo, half // 2)], rc.at[pl.ds(lo, half // 2)],
                    send.at[s], recv.at[s], device(x, y, z, 1 - c))
        cp.start()
        work.append(cp)
    for color in range(2):
        work[color].wait_recv()
        lo = color * half // 2
        h[lo : lo + half // 2] = x_ref[pl.ds(c * half + lo, half // 2)] + rc[lo : lo + half // 2]
        for d in range(1, 4):
            s = next(sem)
            dev, at = ring(color, d, True)
            cp = remote(h.at[pl.ds(lo + at * quarter, quarter)], ra.at[color, d - 1],
                        send.at[s], recv.at[s], dev)
            cp.start()
            work.append(cp)
    for color in range(2):
        mine = work[2 + 3 * color : 5 + 3 * color]
        for cp in mine:
            cp.wait_recv()
        _, at = ring(color, 0, True)
        lo = color * half // 2
        sa[color] = ((h[pl.ds(lo + at * quarter, quarter)] + ra[color, 0])
                     + (ra[color, 1] + ra[color, 2]))
        for d in range(1, 4):
            s = next(sem)
            dev, at = ring(color, d, False)
            cp = remote(sa.at[color, pl.ds(at * small, small)], rb.at[color, d - 1],
                        send.at[s], recv.at[s], dev)
            cp.start()
            work.append(cp)
    for color in range(2):
        mine = work[8 + 3 * color : 11 + 3 * color]
        for cp in mine:
            cp.wait_recv()
        _, at = ring(color, 0, False)
        y18[color * small : (color + 1) * small] = (
            (sa[color, pl.ds(at * small, small)] + rb[color, 0]) + (rb[color, 1] + rb[color, 2]))
    for cp in work:
        cp.wait_send()
    zcopies = []
    for d in range(1, NZ):
        s = next(sem)
        to = lax.rem(z + d, NZ)
        own = jnp.minimum(to, 5)
        cp = remote(y18.at[pl.ds(own * piece, piece)], rz.at[d - 1], send.at[s], recv.at[s],
                    device(x, y, to, c))
        pl.when(to < 6)(cp.start)
        zcopies.append((cp, to))
    base = c * half

    def spot(p):
        color = p // 3
        chunk = jnp.where(color == 0, x * 4 + y, y * 4 + x)
        return base + color * (half // 2) + chunk * small + lax.rem(p, 3) * piece

    own = jnp.minimum(z, 5)

    @pl.when(z < 6)
    def _():
        total = y18[pl.ds(own * piece, piece)]
        for d in range(1, NZ):
            zcopies[d - 1][0].wait_recv()
            total = total + rz[d - 1]
        out_ref[pl.ds(spot(own), piece)] = total

    back = []
    for d in range(1, NZ):
        s = next(sem)
        to = lax.rem(z + d, NZ)
        at = pl.ds(spot(own), piece)
        cp = remote(out_ref.at[at], out_ref.at[at], send.at[s], recv.at[s], device(x, y, to, c))
        pl.when(z < 6)(cp.start)
        back.append(cp)
    for d in range(1, NZ):
        source = lax.rem(z - d + NZ, NZ)
        pl.when(source < 6)(back[d - 1].wait_recv)
    work = []
    for color in range(2):
        _, mine = ring(color, 0, True)
        _, sub = ring(color, 0, False)
        at = pl.ds(base + color * (half // 2) + mine * quarter + sub * small, small)
        for d in range(1, 4):
            s = next(sem)
            dev, _ = ring(color, d, False)
            cp = remote(out_ref.at[at], out_ref.at[at], send.at[s], recv.at[s], dev)
            cp.start()
            work.append(cp)
    for color in range(2):
        for cp in work[3 * color : 3 * color + 3]:
            cp.wait_recv()
        _, mine = ring(color, 0, True)
        at = pl.ds(base + color * (half // 2) + mine * quarter, quarter)
        for d in range(1, 4):
            s = next(sem)
            dev, _ = ring(color, d, True)
            cp = remote(out_ref.at[at], out_ref.at[at], send.at[s], recv.at[s], dev)
            cp.start()
            work.append(cp)
    for color in range(2):
        for cp in work[6 + 3 * color : 9 + 3 * color]:
            cp.wait_recv()
        s = next(sem)
        at = pl.ds(base + color * (half // 2), half // 2)
        cp = remote(out_ref.at[at], out_ref.at[at], send.at[s], recv.at[s], device(x, y, z, 1 - c))
        cp.start()
        work.append(cp)
    for cp in work[12:]:
        cp.wait_recv()
    for cp in work:
        cp.wait_send()
    for cp, to in zcopies:
        pl.when(to < 6)(cp.wait_send)
    for cp in back:
        pl.when(z < 6)(cp.wait_send)


def sum_all(value):
    units = value.shape[0]
    half = units // 2
    quarter = half // 8
    small = quarter // 4
    piece = 2 * small // 6
    tile = value.shape[1:]
    buf = lambda *lead: pltpu.VMEM(lead + tile, F32)
    return pl.pallas_call(
        functools.partial(sum_body, half),
        out_shape=jax.ShapeDtypeStruct(value.shape, F32),
        in_specs=[VMEM],
        out_specs=VMEM,
        scratch_shapes=[
            buf(half), buf(half), buf(2, 3, quarter), buf(2, quarter), buf(2, 3, small),
            buf(2 * small), buf(7, piece),
            pltpu.SemaphoreType.DMA((64,)), pltpu.SemaphoreType.DMA((64,)),
        ],
        compiler_params=pltpu.CompilerParams(
            collective_id=1, has_side_effects=True, vmem_limit_bytes=48 << 20),
    )(value)

def node_body(s_hbm, node_ref, ext_ref, sig, part, far, near, pair, fwd, load, send, recv):
    x, y, z, c = place()
    t = lax.axis_index("tm")
    rows = part.shape[0] // 4
    half, quarter = rows // 2, rows // 4

    def chunk_of(at):
        return jnp.where(c == 0, at, 3 - at)

    flip = (lambda v: v + 1 - 2 * lax.rem(v, 2), lambda v: 3 - v)
    others = (flip[0](x), flip[1](x))
    opposite = lax.rem(x + 2, 4)
    order = (opposite, others[0], others[1], x)
    loads = []
    for ph in range(2):
        for i, at in enumerate(order):
            rows_at = pl.ds(pl.multiple_of(chunk_of(at) * rows + ph * half, half), half)
            cp = pltpu.make_async_copy(s_hbm.at[rows_at], sig.at[rows_at], load.at[ph * 4 + i])
            cp.start()
            loads.append((cp, rows_at))
    b = chunk_of(x)
    has_to = jnp.logical_or(b > 0, t > 0)
    has_from = jnp.logical_or(b < 3, t < 2 * NY * NZ - 1)
    step = 1 - 2 * c
    to = {"tm": jnp.where(b > 0, t, jnp.maximum(t - 1, 0)), "chan": jnp.where(b > 0, x - step, x)}
    source = {"tm": jnp.where(b < 3, t, jnp.minimum(t + 1, 2 * NY * NZ - 1)),
              "chan": jnp.where(b < 3, x + step, x)}
    barrier = pltpu.get_barrier_semaphore()
    link = tuple(device(at, y, z, c) for at in others)
    for dev in link:
        pl.semaphore_signal(barrier, inc=1, device_id=dev, device_id_type=MESH)

    @pl.when(has_to)
    def _():
        pl.semaphore_signal(barrier, inc=1, device_id=to, device_id_type=MESH)

    @pl.when(has_from)
    def _():
        pl.semaphore_signal(barrier, inc=1, device_id=source, device_id_type=MESH)

    scale = 1.0 / math.sqrt(CH // NODES)
    chans = node_ref.shape[1]
    match = lax.broadcasted_iota(jnp.int32, (NODES, chans), 0) == node_ref[...]
    onehot = jnp.where(match, scale, 0.0).astype(jnp.bfloat16)

    def sums(ph, i):
        cp, rows_at = loads[ph * 4 + i]
        cp.wait()
        part[rows_at] = lax.dot_general(sig[rows_at], onehot, (((1,), (1,)), ((), ())),
                                        preferred_element_type=F32)

    def piece(at, ph, color):
        return pl.ds(pl.multiple_of(chunk_of(at) * rows + ph * half + color * quarter, quarter), quarter)

    def copy(src, dst, kind, ph, color, dev):
        s = (kind * 2 + ph) * 2 + color
        return remote(src, dst, send.at[s], recv.at[s], dev)

    def fars(ph):
        return [copy(part.at[piece(opposite, ph, k)], far.at[ph, k], 0, ph, k, link[k]) for k in range(2)]

    def nears(ph):
        return [copy(part.at[piece(others[k], ph, k)], near.at[ph, k], 1, ph, k, link[k]) for k in range(2)]

    def forwards(ph):
        return [copy(fwd.at[ph, k], pair.at[ph, k], 2, ph, k, link[1 - k]) for k in range(2)]

    sums(0, 0)
    count = 2 + has_to.astype(jnp.int32) + has_from.astype(jnp.int32)
    pl.semaphore_wait(barrier, count)
    work = [fars(0), nears(0), forwards(0), fars(1), nears(1), forwards(1)]

    def forward(ph):
        for k in range(2):
            work[3 * ph][k].wait_recv()
            fwd[ph, k] = part[piece(others[1 - k], ph, k)] + far[ph, k]
            work[3 * ph + 2][k].start()

    def finish(ph):
        for k in range(2):
            work[3 * ph + 1][k].wait_recv()
            work[3 * ph + 2][k].wait_recv()
            at = ph * half + k * quarter
            ext_ref[at : at + quarter] = part[piece(x, ph, k)] + near[ph, k] + pair[ph, k]

    for cp in work[0]:
        cp.start()
    sums(0, 1)
    work[1][0].start()
    sums(0, 2)
    work[1][1].start()
    for i in range(4):
        sums(1, i)
    sums(0, 3)
    forward(0)
    for cp in work[3] + work[4]:
        cp.start()
    finish(0)
    forward(1)
    halo = remote(ext_ref.at[0:half], ext_ref.at[rows : rows + half], send.at[12], recv.at[12], to)
    pl.when(has_to)(halo.start)

    @pl.when(jnp.logical_not(has_from))
    def _():
        ext_ref[rows : rows + half] = jnp.zeros((half, NODES), F32)

    finish(1)
    pl.when(has_from)(halo.wait_recv)
    for pair_of in work:
        for cp in pair_of:
            cp.wait_send()
    pl.when(has_to)(halo.wait_send)


def node_rows(signals, channel_node):
    length, chans = signals.shape
    rows = length // 4
    quarter = rows // 4
    buf = lambda: pltpu.VMEM((2, 2, quarter, NODES), F32)
    return pl.pallas_call(
        node_body,
        out_shape=jax.ShapeDtypeStruct((rows + MAXLAG, NODES), F32),
        in_specs=[pl.BlockSpec(memory_space=pl.ANY), VMEM],
        out_specs=VMEM,
        scratch_shapes=[
            pltpu.VMEM((length, chans), jnp.bfloat16), pltpu.VMEM((length, NODES), F32),
            buf(), buf(), buf(), buf(),
            pltpu.SemaphoreType.DMA((8,)), pltpu.SemaphoreType.DMA((13,)),
            pltpu.SemaphoreType.DMA((13,)),
        ],
        compiler_params=pltpu.CompilerParams(
            collective_id=2, has_side_effects=True, vmem_limit_bytes=48 << 20),
    )(signals, channel_node.reshape(1, chans))


def lanes(x, c):
    return jnp.broadcast_to(x[:, c : c + 1], x.shape)


def subs(x, r):
    return jnp.broadcast_to(x[r : r + 1, :], x.shape)


def factor_block(rows):
    count = NB // 8
    lane = lax.broadcasted_iota(jnp.int32, (8, NB), 1)
    sub = lax.broadcasted_iota(jnp.int32, (8, NB), 0)
    rows = list(rows)
    upper, inv = [], []
    cur = [lanes(rows[0], j) for j in range(8)]
    for p in range(count):
        r0 = 8 * p
        raw = {b: [lanes(rows[b], r0 + j) for j in range(8)] for b in range(p + 1, count)}
        ahead = [lanes(rows[p + 1], r0 + 8 + j) for j in range(8)] if p + 1 < count else None
        here = jnp.logical_and(lane >= r0, lane < r0 + 8)
        top, low = rows[p], jnp.where(here, jnp.where(lane == sub + r0, 1.0, 0.0), rows[p])
        for b in range(p + 1, count):
            rows[b] = jnp.where(here, 0.0, rows[b])
        v, m, s, rinv = list(cur), [None] * 8, [[None] * 8 for _ in range(8)], [None] * 8
        diag = None
        for j in range(8):
            diag = v[j] if diag is None else jnp.where(sub >= j, v[j], diag)
            rinv[j] = 1.0 / subs(v[j], j)
            whole = v[j] * rinv[j]
            for k in range(j + 1, 8):
                s[j][k] = subs(v[j], k)
                if k == j + 1:
                    v[k] = v[k] - (v[j] * s[j][k]) * rinv[j]
                else:
                    v[k] = v[k] - whole * s[j][k]
            m[j] = jnp.where(sub > j, whole, 0.0)
        rs = lax.rsqrt(diag)
        ra = []
        for j in range(8):
            ra.append(subs(low, j))
            da = subs(top, j)
            low = low - m[j] * ra[j]
            top = top - m[j] * da
        for b in range(p + 1, count):
            u, mb = [], []
            for j in range(8):
                value = raw[b][j]
                for i in range(j):
                    value = value - mb[i] * s[i][j]
                u.append(value)
                mb.append(value * rinv[j])
            if b == p + 1:
                cur = []
                for i in range(8):
                    value = ahead[i]
                    for j in range(8):
                        value = value - mb[j] * subs(u[j], i)
                    cur.append(value)
            for j in range(8):
                rows[b] = rows[b] - mb[j] * ra[j]
        upper.append(jnp.where(lane >= sub + r0, top * rs, 0.0))
        inv.append(jnp.where(lane < r0 + 8, low * rs, 0.0))
    return upper, inv


DOT = dict(precision=lax.Precision.HIGHEST, preferred_element_type=F32)


def factor_body(count, scale, g_ref, r_ref, w_ref, d_ref):
    r_ref[...] = jnp.zeros_like(r_ref)

    def update(k):
        r0 = k * NB
        first = first_block(k, count)
        for j in range(k, count):
            r_ref[r0 : r0 + NB, j * NB : (j + 1) * NB] = g_ref[first + j - k] * scale
        if k > 0:
            r_ref[r0 : r0 + NB, r0:] -= lax.dot_general(
                r_ref[0:r0, r0 : r0 + NB], r_ref[0:r0, r0:], (((0,), (0,)), ((), ())), **DOT
            )
        d_ref[...] = r_ref[r0 : r0 + NB, r0 : r0 + NB]

    def panel(k):
        r0 = k * NB
        r_ref[r0 : r0 + NB, r0 : r0 + NB] = d_ref[...]
        if k + 1 < count:
            r_ref[r0 : r0 + NB, r0 + NB :] = lax.dot_general(
                w_ref[...], r_ref[r0 : r0 + NB, r0 + NB :], (((1,), (0,)), ((), ())), **DOT
            )

    def step(k, _):
        lax.switch(k, [functools.partial(update, i) for i in range(count)])
        rows, inv = factor_block([d_ref[8 * i : 8 * i + 8, :] for i in range(NB // 8)])
        for i in range(NB // 8):
            d_ref[8 * i : 8 * i + 8, :] = rows[i]
            w_ref[8 * i : 8 * i + 8, :] = inv[i]
        lax.switch(k, [functools.partial(panel, i) for i in range(count)])
        return 0

    lax.fori_loop(0, count, step, 0)


def upper_factor(blocks, count, scale):
    size = count * NB
    return pl.pallas_call(
        functools.partial(factor_body, count, scale),
        out_shape=jax.ShapeDtypeStruct((size, size), F32),
        in_specs=[VMEM],
        out_specs=VMEM,
        scratch_shapes=[pltpu.VMEM((NB, NB), F32)] * 2,
        compiler_params=pltpu.CompilerParams(vmem_limit_bytes=48 << 20),
    )(blocks)

def on_device(signals, channel_node, lag_offsets):
    parts = lax.axis_size("tm") * lax.axis_size("chan")
    groups = lax.axis_size("chan")
    count = lag_offsets.shape[0] * NODES // NB
    rows = signals.shape[0] // groups
    extended = node_rows(signals, channel_node)
    blocks = local_gram(lag_offsets, extended, rows, groups)
    total = sum_all(blocks.reshape(-1, 8, NB)).reshape(blocks.shape)
    return upper_factor(total, count, 1.0 / (rows * parts))


def solution(mesh):
    in_specs = (P("tm", "chan"), P("chan"), P())
    out_specs = P()
    return jax.shard_map(
        on_device, mesh=mesh, in_specs=in_specs, out_specs=out_specs, check_vma=False
    )
```

```python
import functools
import math

import jax
import jax.numpy as jnp
from jax import lax
from jax.experimental import pallas as pl
from jax.experimental.pallas import tpu as pltpu
from jax.sharding import PartitionSpec as P

NODES = 128
CH = 2048
MAXLAG = 512
F32 = jnp.float32
BF16 = jnp.bfloat16
MESH = pl.DeviceIdType.MESH
VMEM = pl.BlockSpec(memory_space=pltpu.VMEM)
NB = 128
NX, NY, NZ = 4, 4, 8
SEGMENTS = 3
OWNERS = 6


def first_block(i, count):
    return i * count - i * (i - 1) // 2


def device(x, y, z, c):
    return {"tm": (y * NZ + z) * 2 + c, "chan": x}


def remote(src, dst, send, recv, target):
    return pltpu.make_async_remote_copy(
        src_ref=src, dst_ref=dst, send_sem=send, recv_sem=recv,
        device_id=target, device_id_type=MESH,
    )


def gram_body(lag_count, lags_ref, s_hbm, node_ref, out_ref,
              sig, part, far, near, pair, fwd, own, land, rot, hi, lo,
              g, rc, h, ra, sa, rb, ys, rz, load, send, recv, ssend, srecv):
    x, t = lax.axis_index("chan"), lax.axis_index("tm")
    y, z, c = t // (NZ * 2), lax.rem(t // 2, NZ), lax.rem(t, 2)
    rows = own.shape[0]
    half, quarter = rows // 2, rows // 4

    def chunk_of(at):
        return jnp.where(c == 0, at, 3 - at)

    others = (x + 1 - 2 * lax.rem(x, 2), 3 - x)
    opposite = lax.rem(x + 2, 4)
    loads = []
    for ph in range(2):
        for i, at in enumerate((opposite, others[0], others[1], x)):
            rows_at = pl.ds(pl.multiple_of(chunk_of(at) * rows + ph * half, half), half)
            cp = pltpu.make_async_copy(s_hbm.at[rows_at], sig.at[rows_at], load.at[ph * 4 + i])
            cp.start()
            loads.append((cp, rows_at))
    b = chunk_of(x)
    has_to = jnp.logical_or(b > 0, t > 0)
    has_from = jnp.logical_or(b < 3, t < 2 * NY * NZ - 1)
    step = 1 - 2 * c
    to = {"tm": jnp.where(b > 0, t, jnp.maximum(t - 1, 0)), "chan": jnp.where(b > 0, x - step, x)}
    source = {"tm": jnp.where(b < 3, t, jnp.minimum(t + 1, 2 * NY * NZ - 1)),
              "chan": jnp.where(b < 3, x + step, x)}
    barrier = pltpu.get_barrier_semaphore()
    peers = [device(x, y, z, 1 - c)]
    peers += [device(lax.rem(x + d, NX), y, z, c) for d in range(1, NX)]
    peers += [device(x, lax.rem(y + d, NY), z, c) for d in range(1, NY)]
    peers += [device(x, y, lax.rem(z + d, NZ), c) for d in range(1, NZ)]
    for dev in peers:
        pl.semaphore_signal(barrier, inc=1, device_id=dev, device_id_type=MESH)

    @pl.when(has_to)
    def _():
        pl.semaphore_signal(barrier, inc=1, device_id=to, device_id_type=MESH)

    @pl.when(has_from)
    def _():
        pl.semaphore_signal(barrier, inc=1, device_id=source, device_id_type=MESH)

    scale = 1.0 / math.sqrt(CH // NODES)
    chans = node_ref.shape[1]
    match = lax.broadcasted_iota(jnp.int32, (NODES, chans), 0) == node_ref[...]
    onehot = jnp.where(match, scale, 0.0).astype(BF16)

    def sums(ph, i):
        cp, rows_at = loads[ph * 4 + i]
        cp.wait()
        part[rows_at] = lax.dot_general(sig[rows_at], onehot, (((1,), (1,)), ((), ())),
                                        preferred_element_type=F32)

    def piece(at, ph, color):
        first = chunk_of(at) * rows + ph * half + color * quarter
        return pl.ds(pl.multiple_of(first, quarter), quarter)

    link = tuple(device(at, y, z, c) for at in others)

    def copy(src, dst, kind, ph, color, dev):
        s = (kind * 2 + ph) * 2 + color
        return remote(src, dst, send.at[s], recv.at[s], dev)

    sums(0, 0)
    pl.semaphore_wait(barrier, len(peers) + has_to.astype(jnp.int32) + has_from.astype(jnp.int32))
    fars, nears, pairs = [], [], []
    for ph in range(2):
        fars.append([copy(part.at[piece(opposite, ph, k)], far.at[ph, k], 0, ph, k, link[k])
                     for k in range(2)])
        nears.append([copy(part.at[piece(others[k], ph, k)], near.at[ph, k], 1, ph, k, link[k])
                      for k in range(2)])
        pairs.append([copy(fwd.at[ph, k], pair.at[ph, k], 2, ph, k, link[1 - k])
                      for k in range(2)])

    def forward(ph):
        for k in range(2):
            fars[ph][k].wait_recv()
            fwd[ph, k] = part[piece(others[1 - k], ph, k)] + far[ph, k]
            pairs[ph][k].start()

    def finish(ph):
        for k in range(2):
            nears[ph][k].wait_recv()
            pairs[ph][k].wait_recv()
            at = ph * half + k * quarter
            own[at : at + quarter] = part[piece(x, ph, k)] + near[ph, k] + pair[ph, k]

    for cp in fars[0]:
        cp.start()
    sums(0, 1)
    nears[0][0].start()
    sums(0, 2)
    nears[0][1].start()
    for i in range(4):
        sums(1, i)
    sums(0, 3)
    forward(0)
    for cp in fars[1] + nears[1]:
        cp.start()
    finish(0)
    forward(1)
    halo = remote(own.at[0:half], land, send.at[12], recv.at[12], to)
    pl.when(has_to)(halo.start)
    finish(1)

    width = NODES // NX
    per_tile = NB // width
    count = lag_count * NODES // NB
    chunk = 128
    lane_group = lax.broadcasted_iota(jnp.int32, (chunk, NB), 1) // width

    def build(first_step, steps):
        for tile in range(count):
            group, top = tile // (count // NX), tile % (count // NX)

            def fill(i, _):
                value = None
                for m in range(per_tile):
                    first = lags_ref[top * per_tile + m] + i * chunk
                    got = rot[(m - group) % per_tile, pl.ds(first, chunk), :]
                    value = got if value is None else jnp.where(lane_group == m, got, value)
                high = value.astype(BF16)
                at = pl.ds(pl.multiple_of(i * chunk, chunk), chunk)
                hi[at, tile * NB : (tile + 1) * NB] = high
                lo[at, tile * NB : (tile + 1) * NB] = (value - high.astype(F32)).astype(BF16)
                return 0

            lax.fori_loop(first_step, first_step + steps, fill, 0)

    dims = (((0,), (0,)), ((), ()))

    def products(i, at, add):
        a, d = hi[at, i * NB : (i + 1) * NB], lo[at, i * NB : (i + 1) * NB]
        value = lax.dot_general(a, lo[at, i * NB :], dims, preferred_element_type=F32)
        value += lax.dot_general(d, hi[at, i * NB :], dims, preferred_element_type=F32)
        value += lax.dot_general(a, hi[at, i * NB :], dims, preferred_element_type=F32)
        for j in range(i, count):
            spot = 16 * (first_block(i, count) + j - i)
            block = value[:, (j - i) * NB : (j - i + 1) * NB].reshape(16, 8, NB)
            g[spot : spot + 16] = g[spot : spot + 16] + block if add else block

    for r in range(per_tile):
        rot[r, 0:rows] = own[...] if r == 0 else pltpu.roll(own[...], width * r, 1)
    steps = half // chunk
    build(0, steps)
    for i in range(count):
        products(i, slice(0, half), False)

    @pl.when(has_from)
    def _():
        halo.wait_recv()

    @pl.when(jnp.logical_not(has_from))
    def _():
        land[...] = jnp.zeros_like(land)

    for r in range(per_tile):
        rot[r, rows : rows + half] = land[...] if r == 0 else pltpu.roll(land[...], width * r, 1)
    build(steps, steps)

    units = g.shape[0] // SEGMENTS
    side = units // 2
    color_part = side // 2
    ring_part = color_part // 4
    small = ring_part // 4
    sems = iter(range(SEGMENTS * 42))
    ids = [[[next(sems) for _ in range(n)] for n in (2, 6, 6, 7, 7, 6, 6, 2)] for _ in range(SEGMENTS)]

    def ring(color, d, first):
        if (color == 0) == first:
            at = lax.rem(x + d, NX)
            return device(at, y, z, c), at
        at = lax.rem(y + d, NY)
        return device(x, at, z, c), at

    def send_to(src, dst, s, stage, n, dev):
        k = ids[s][stage][n]
        return remote(src, dst, ssend.at[k], srecv.at[k], dev)

    partner = device(x, y, z, 1 - c)
    plain = []
    stages = [[[] for _ in range(8)] for _ in range(SEGMENTS)]

    def go(s, stage, cp):
        cp.start()
        stages[s][stage].append(cp)
        plain.append(cp)

    def cores(s):
        for color in range(2):
            at = pl.ds(s * units + (1 - c) * side + color * color_part, color_part)
            go(s, 0, send_to(g.at[at], rc.at[s, color], s, 0, color, partner))

    def ring_first(s):
        for color in range(2):
            stages[s][0][color].wait_recv()
            at = pl.ds(s * units + c * side + color * color_part, color_part)
            h[s, color] = g[at] + rc[s, color]
            for d in range(1, 4):
                dev, spot = ring(color, d, True)
                go(s, 1, send_to(h.at[s, color, pl.ds(spot * ring_part, ring_part)],
                                 ra.at[s, color, d - 1], s, 1, 3 * color + d - 1, dev))

    def ring_second(s):
        for color in range(2):
            for cp in stages[s][1][3 * color : 3 * color + 3]:
                cp.wait_recv()
            _, spot = ring(color, 0, True)
            sa[s, color] = ((h[s, color, pl.ds(spot * ring_part, ring_part)] + ra[s, color, 0])
                            + (ra[s, color, 1] + ra[s, color, 2]))
            for d in range(1, 4):
                dev, spot = ring(color, d, False)
                go(s, 2, send_to(sa.at[s, color, pl.ds(spot * small, small)],
                                 rb.at[s, color, d - 1], s, 2, 3 * color + d - 1, dev))

    size = 2 * small // OWNERS
    mine = jnp.minimum(z, OWNERS - 1)

    def along_z(s):
        for color in range(2):
            for cp in stages[s][2][3 * color : 3 * color + 3]:
                cp.wait_recv()
            _, spot = ring(color, 0, False)
            ys[s, color * small : (color + 1) * small] = (
                (sa[s, color, pl.ds(spot * small, small)] + rb[s, color, 0])
                + (rb[s, color, 1] + rb[s, color, 2]))
        for d in range(1, NZ):
            dst = lax.rem(z + d, NZ)
            at = pl.ds(jnp.minimum(dst, OWNERS - 1) * size, size)
            cp = send_to(ys.at[s, at], rz.at[s, d - 1], s, 3, d - 1, device(x, y, dst, c))
            pl.when(dst < OWNERS)(cp.start)
            stages[s][3].append(cp)

    def spot_of(s, p):
        color = p // (OWNERS // 2)
        chunk_at = jnp.where(color == 0, x * 4 + y, y * 4 + x)
        return (s * units + c * side + color * color_part + chunk_at * small
                + lax.rem(p, OWNERS // 2) * size)

    def back_z(s):
        at = pl.ds(spot_of(s, mine), size)

        @pl.when(z < OWNERS)
        def _():
            total = ys[s, pl.ds(mine * size, size)]
            for d in range(1, NZ):
                stages[s][3][d - 1].wait_recv()
                total = total + rz[s, d - 1]
            out_ref[at] = total

        for d in range(1, NZ):
            cp = send_to(out_ref.at[at], out_ref.at[at], s, 4, d - 1,
                         device(x, y, lax.rem(z + d, NZ), c))
            pl.when(z < OWNERS)(cp.start)
            stages[s][4].append(cp)

    def back_second(s):
        for d in range(1, NZ):
            pl.when(lax.rem(z - d + NZ, NZ) < OWNERS)(stages[s][4][d - 1].wait_recv)
        for color in range(2):
            _, spot = ring(color, 0, True)
            _, sub = ring(color, 0, False)
            at = pl.ds(s * units + c * side + color * color_part + spot * ring_part + sub * small,
                       small)
            for d in range(1, 4):
                dev, _ = ring(color, d, False)
                go(s, 5, send_to(out_ref.at[at], out_ref.at[at], s, 5, 3 * color + d - 1, dev))

    def back_first(s):
        for color in range(2):
            for cp in stages[s][5][3 * color : 3 * color + 3]:
                cp.wait_recv()
            _, spot = ring(color, 0, True)
            at = pl.ds(s * units + c * side + color * color_part + spot * ring_part, ring_part)
            for d in range(1, 4):
                dev, _ = ring(color, d, True)
                go(s, 6, send_to(out_ref.at[at], out_ref.at[at], s, 6, 3 * color + d - 1, dev))

    def back_cores(s):
        for color in range(2):
            for cp in stages[s][6][3 * color : 3 * color + 3]:
                cp.wait_recv()
            at = pl.ds(s * units + c * side + color * color_part, color_part)
            go(s, 7, send_to(out_ref.at[at], out_ref.at[at], s, 7, color, partner))

    def last(s):
        for cp in stages[s][7]:
            cp.wait_recv()

    done = 0
    for s in range(SEGMENTS):
        while first_block(done, count) * 16 < (s + 1) * units:
            products(done, slice(half, rows), True)
            done += 1
        cores(s)
    chain = (ring_first, ring_second, along_z, back_z, back_second, back_first, back_cores, last)
    for slot in range(len(chain) + SEGMENTS - 1):
        for s in range(SEGMENTS):
            if 0 <= slot - s < len(chain):
                chain[slot - s](s)

    for ph in range(2):
        for cp in fars[ph] + nears[ph] + pairs[ph]:
            cp.wait_send()
    pl.when(has_to)(halo.wait_send)
    for cp in plain:
        cp.wait_send()
    for s in range(SEGMENTS):
        for d in range(1, NZ):
            pl.when(lax.rem(z + d, NZ) < OWNERS)(stages[s][3][d - 1].wait_send)
            pl.when(z < OWNERS)(stages[s][4][d - 1].wait_send)


def gram_blocks(signals, channel_node, lags):
    length, chans = signals.shape
    rows = length // NX
    size = lags.shape[0] * NODES
    count = size // NB
    blocks = count * (count + 1) // 2
    side = blocks * 16 // SEGMENTS // 2
    tiles = lambda *lead: pltpu.VMEM(lead + (8, NB), F32)
    quarters = pltpu.VMEM((2, 2, rows // 4, NODES), F32)
    S = SEGMENTS
    dma = pltpu.SemaphoreType.DMA
    total = pl.pallas_call(
        functools.partial(gram_body, lags.shape[0]),
        out_shape=jax.ShapeDtypeStruct((blocks * 16, 8, NB), F32),
        in_specs=[pl.BlockSpec(memory_space=pltpu.SMEM), pl.BlockSpec(memory_space=pl.ANY), VMEM],
        out_specs=VMEM,
        scratch_shapes=[
            pltpu.VMEM((length, chans), BF16), pltpu.VMEM((length, NODES), F32),
            quarters, quarters, quarters, quarters,
            pltpu.VMEM((rows, NODES), F32), pltpu.VMEM((MAXLAG, NODES), F32),
            pltpu.VMEM((NX, rows + MAXLAG, NODES), F32),
            pltpu.VMEM((rows, size), BF16), pltpu.VMEM((rows, size), BF16),
            tiles(blocks * 16), tiles(S, 2, side // 2), tiles(S, 2, side // 2),
            tiles(S, 2, 3, side // 8), tiles(S, 2, side // 8), tiles(S, 2, 3, side // 32),
            tiles(S, side // 16), tiles(S, NZ - 1, side // 16 // OWNERS),
            dma((8,)), dma((13,)), dma((13,)), dma((S * 42,)), dma((S * 42,)),
        ],
        compiler_params=pltpu.CompilerParams(
            collective_id=1, has_side_effects=True, vmem_limit_bytes=56 << 20),
    )(lags, signals, channel_node.reshape(1, chans))
    return total.reshape(blocks, NB, NB)


def lanes(x, c):
    return jnp.broadcast_to(x[:, c : c + 1], x.shape)


def subs(x, r):
    return jnp.broadcast_to(x[r : r + 1, :], x.shape)


def factor_block(rows):
    count = NB // 8
    lane = lax.broadcasted_iota(jnp.int32, (8, NB), 1)
    sub = lax.broadcasted_iota(jnp.int32, (8, NB), 0)
    rows = list(rows)
    upper, inv = [], []
    cur = [lanes(rows[0], j) for j in range(8)]
    for p in range(count):
        r0 = 8 * p
        raw = {b: [lanes(rows[b], r0 + j) for j in range(8)] for b in range(p + 1, count)}
        ahead = [lanes(rows[p + 1], r0 + 8 + j) for j in range(8)] if p + 1 < count else None
        here = jnp.logical_and(lane >= r0, lane < r0 + 8)
        top, low = rows[p], jnp.where(here, jnp.where(lane == sub + r0, 1.0, 0.0), rows[p])
        for b in range(p + 1, count):
            rows[b] = jnp.where(here, 0.0, rows[b])
        v, m, s, rinv = list(cur), [None] * 8, [[None] * 8 for _ in range(8)], [None] * 8
        diag = None
        for j in range(8):
            diag = v[j] if diag is None else jnp.where(sub >= j, v[j], diag)
            rinv[j] = 1.0 / subs(v[j], j)
            whole = v[j] * rinv[j]
            for k in range(j + 1, 8):
                s[j][k] = subs(v[j], k)
                if k == j + 1:
                    v[k] = v[k] - (v[j] * s[j][k]) * rinv[j]
                else:
                    v[k] = v[k] - whole * s[j][k]
            m[j] = jnp.where(sub > j, whole, 0.0)
        rs = lax.rsqrt(diag)
        ra = []
        for j in range(8):
            ra.append(subs(low, j))
            da = subs(top, j)
            low = low - m[j] * ra[j]
            top = top - m[j] * da
        for b in range(p + 1, count):
            u, mb = [], []
            for j in range(8):
                value = raw[b][j]
                for i in range(j):
                    value = value - mb[i] * s[i][j]
                u.append(value)
                mb.append(value * rinv[j])
            if b == p + 1:
                cur = []
                for i in range(8):
                    value = ahead[i]
                    for j in range(8):
                        value = value - mb[j] * subs(u[j], i)
                    cur.append(value)
            for j in range(8):
                rows[b] = rows[b] - mb[j] * ra[j]
        upper.append(jnp.where(lane >= sub + r0, top * rs, 0.0))
        inv.append(jnp.where(lane < r0 + 8, low * rs, 0.0))
    return upper, inv


DOT = dict(precision=lax.Precision.HIGHEST, preferred_element_type=F32)


def factor_body(count, scale, g_hbm, out_hbm, g_ref, r_ref, w_ref, d_ref, sem):
    def fetch(k):
        at = pl.ds(first_block(k, count), count - k)
        return pltpu.make_async_copy(g_hbm.at[at], g_ref.at[at], sem.at[count + k])

    for k in range(count):
        fetch(k).start()
    r_ref[...] = jnp.zeros_like(r_ref)

    def leave(k):
        at = pl.ds(k * NB, NB)
        return pltpu.make_async_copy(r_ref.at[at], out_hbm.at[at], sem.at[k])

    def update(k):
        r0 = k * NB
        first = first_block(k, count)
        fetch(k).wait()
        for j in range(k, count):
            r_ref[r0 : r0 + NB, j * NB : (j + 1) * NB] = g_ref[first + j - k] * scale
        if k > 0:
            r_ref[r0 : r0 + NB, r0:] -= lax.dot_general(
                r_ref[0:r0, r0 : r0 + NB], r_ref[0:r0, r0:], (((0,), (0,)), ((), ())), **DOT
            )
        d_ref[...] = r_ref[r0 : r0 + NB, r0 : r0 + NB]

    def panel(k):
        r0 = k * NB
        r_ref[r0 : r0 + NB, r0 : r0 + NB] = d_ref[...]
        if k + 1 < count:
            r_ref[r0 : r0 + NB, r0 + NB :] = lax.dot_general(
                w_ref[...], r_ref[r0 : r0 + NB, r0 + NB :], (((1,), (0,)), ((), ())), **DOT
            )
        leave(k).start()

    def step(k, _):
        lax.switch(k, [functools.partial(update, i) for i in range(count)])
        rows, inv = factor_block([d_ref[8 * i : 8 * i + 8, :] for i in range(NB // 8)])
        for i in range(NB // 8):
            d_ref[8 * i : 8 * i + 8, :] = rows[i]
            w_ref[8 * i : 8 * i + 8, :] = inv[i]
        lax.switch(k, [functools.partial(panel, i) for i in range(count)])
        return 0

    lax.fori_loop(0, count, step, 0)
    for k in range(count):
        leave(k).wait()


def upper_factor(blocks, count, scale):
    size = count * NB
    return pl.pallas_call(
        functools.partial(factor_body, count, scale),
        out_shape=jax.ShapeDtypeStruct((size, size), F32),
        in_specs=[pl.BlockSpec(memory_space=pltpu.HBM)],
        out_specs=pl.BlockSpec(memory_space=pltpu.HBM),
        scratch_shapes=[pltpu.VMEM(blocks.shape, F32), pltpu.VMEM((size, size), F32), pltpu.VMEM((NB, NB), F32),
                        pltpu.VMEM((NB, NB), F32), pltpu.SemaphoreType.DMA((2 * count,))],
        compiler_params=pltpu.CompilerParams(vmem_limit_bytes=48 << 20),
    )(blocks)


def on_device(signals, channel_node, lag_offsets):
    total_rows = signals.shape[0] * lax.axis_size("tm")
    count = lag_offsets.shape[0] * NODES // NB
    blocks = gram_blocks(signals, channel_node, lag_offsets)
    return upper_factor(blocks, count, 1.0 / total_rows)


def solution(mesh):
    in_specs = (P("tm", "chan"), P("chan"), P())
    out_specs = P()
    return jax.shard_map(
        on_device, mesh=mesh, in_specs=in_specs, out_specs=out_specs, check_vma=False
    )
```

```python
import functools
import math

import jax
import jax.numpy as jnp
from jax import lax
from jax.experimental import pallas as pl
from jax.experimental.pallas import tpu as pltpu
from jax.sharding import PartitionSpec as P

NODES = 128
CH = 2048
MAXLAG = 512
F32 = jnp.float32
BF16 = jnp.bfloat16
MESH = pl.DeviceIdType.MESH
VMEM = pl.BlockSpec(memory_space=pltpu.VMEM)
NB = 128
NX, NY, NZ = 4, 4, 8
SEGMENTS = 1
OWNERS = 6


def first_block(i, count):
    return i * count - i * (i - 1) // 2


def device(x, y, z, c):
    return {"tm": (y * NZ + z) * 2 + c, "chan": x}


def remote(src, dst, send, recv, target):
    return pltpu.make_async_remote_copy(
        src_ref=src, dst_ref=dst, send_sem=send, recv_sem=recv,
        device_id=target, device_id_type=MESH,
    )


def gram_body(lag_count, lags_ref, s_hbm, node_ref, out_ref,
              sig, part, far, near, pair, fwd, own, land, rot, hi, lo,
              g, rc, h, ra, sa, rb, ys, rz, load, send, recv, ssend, srecv):
    x, t = lax.axis_index("chan"), lax.axis_index("tm")
    y, z, c = t // (NZ * 2), lax.rem(t // 2, NZ), lax.rem(t, 2)
    rows = own.shape[0]
    half, quarter = rows // 2, rows // 4

    def chunk_of(at):
        return jnp.where(c == 0, at, 3 - at)

    others = (x + 1 - 2 * lax.rem(x, 2), 3 - x)
    opposite = lax.rem(x + 2, 4)
    loads = []
    for ph in range(2):
        for i, at in enumerate((opposite, others[0], others[1], x)):
            rows_at = pl.ds(pl.multiple_of(chunk_of(at) * rows + ph * half, half), half)
            cp = pltpu.make_async_copy(s_hbm.at[rows_at], sig.at[rows_at], load.at[ph * 4 + i])
            cp.start()
            loads.append((cp, rows_at))
    b = chunk_of(x)
    has_to = jnp.logical_or(b > 0, t > 0)
    has_from = jnp.logical_or(b < 3, t < 2 * NY * NZ - 1)
    step = 1 - 2 * c
    to = {"tm": jnp.where(b > 0, t, jnp.maximum(t - 1, 0)), "chan": jnp.where(b > 0, x - step, x)}
    source = {"tm": jnp.where(b < 3, t, jnp.minimum(t + 1, 2 * NY * NZ - 1)),
              "chan": jnp.where(b < 3, x + step, x)}
    barrier = pltpu.get_barrier_semaphore()
    peers = [device(x, y, z, 1 - c)]
    peers += [device(lax.rem(x + d, NX), y, z, c) for d in range(1, NX)]
    peers += [device(x, lax.rem(y + d, NY), z, c) for d in range(1, NY)]
    peers += [device(x, y, lax.rem(z + d, NZ), c) for d in range(1, NZ)]
    for dev in peers:
        pl.semaphore_signal(barrier, inc=1, device_id=dev, device_id_type=MESH)

    @pl.when(has_to)
    def _():
        pl.semaphore_signal(barrier, inc=1, device_id=to, device_id_type=MESH)

    @pl.when(has_from)
    def _():
        pl.semaphore_signal(barrier, inc=1, device_id=source, device_id_type=MESH)

    scale = 1.0 / math.sqrt(CH // NODES)
    chans = node_ref.shape[1]
    match = lax.broadcasted_iota(jnp.int32, (NODES, chans), 0) == node_ref[...]
    onehot = jnp.where(match, scale, 0.0).astype(BF16)

    def sums(ph, i):
        cp, rows_at = loads[ph * 4 + i]
        cp.wait()
        part[rows_at] = lax.dot_general(sig[rows_at], onehot, (((1,), (1,)), ((), ())),
                                        preferred_element_type=F32)

    def piece(at, ph, color):
        first = chunk_of(at) * rows + ph * half + color * quarter
        return pl.ds(pl.multiple_of(first, quarter), quarter)

    link = tuple(device(at, y, z, c) for at in others)

    def copy(src, dst, kind, ph, color, dev):
        s = (kind * 2 + ph) * 2 + color
        return remote(src, dst, send.at[s], recv.at[s], dev)

    sums(0, 0)
    pl.semaphore_wait(barrier, len(peers) + has_to.astype(jnp.int32) + has_from.astype(jnp.int32))
    fars, nears, pairs = [], [], []
    for ph in range(2):
        fars.append([copy(part.at[piece(opposite, ph, k)], far.at[ph, k], 0, ph, k, link[k])
                     for k in range(2)])
        nears.append([copy(part.at[piece(others[k], ph, k)], near.at[ph, k], 1, ph, k, link[k])
                      for k in range(2)])
        pairs.append([copy(fwd.at[ph, k], pair.at[ph, k], 2, ph, k, link[1 - k])
                      for k in range(2)])

    def forward(ph):
        for k in range(2):
            fars[ph][k].wait_recv()
            fwd[ph, k] = part[piece(others[1 - k], ph, k)] + far[ph, k]
            pairs[ph][k].start()

    def finish(ph):
        for k in range(2):
            nears[ph][k].wait_recv()
            pairs[ph][k].wait_recv()
            at = ph * half + k * quarter
            own[at : at + quarter] = part[piece(x, ph, k)] + near[ph, k] + pair[ph, k]

    for cp in fars[0]:
        cp.start()
    sums(0, 1)
    nears[0][0].start()
    sums(0, 2)
    nears[0][1].start()
    for i in range(4):
        sums(1, i)
    sums(0, 3)
    forward(0)
    for cp in fars[1] + nears[1]:
        cp.start()
    finish(0)
    forward(1)
    halo = remote(own.at[0:half], land, send.at[12], recv.at[12], to)
    pl.when(has_to)(halo.start)
    finish(1)

    width = NODES // NX
    per_tile = NB // width
    count = lag_count * NODES // NB
    chunk = 128
    lane_group = lax.broadcasted_iota(jnp.int32, (chunk, NB), 1) // width

    def build(first_step, steps):
        for tile in range(count):
            group, top = tile // (count // NX), tile % (count // NX)

            def fill(i, _):
                value = None
                for m in range(per_tile):
                    first = lags_ref[top * per_tile + m] + i * chunk
                    got = rot[(m - group) % per_tile, pl.ds(first, chunk), :]
                    value = got if value is None else jnp.where(lane_group == m, got, value)
                high = value.astype(BF16)
                at = pl.ds(pl.multiple_of(i * chunk, chunk), chunk)
                hi[at, tile * NB : (tile + 1) * NB] = high
                lo[at, tile * NB : (tile + 1) * NB] = (value - high.astype(F32)).astype(BF16)
                return 0

            lax.fori_loop(first_step, first_step + steps, fill, 0)

    dims = (((0,), (0,)), ((), ()))

    def products(i, at, add):
        a, d = hi[at, i * NB : (i + 1) * NB], lo[at, i * NB : (i + 1) * NB]
        value = lax.dot_general(a, lo[at, i * NB :], dims, preferred_element_type=F32)
        value += lax.dot_general(d, hi[at, i * NB :], dims, preferred_element_type=F32)
        value += lax.dot_general(a, hi[at, i * NB :], dims, preferred_element_type=F32)
        for j in range(i, count):
            spot = 16 * (first_block(i, count) + j - i)
            block = value[:, (j - i) * NB : (j - i + 1) * NB].reshape(16, 8, NB)
            g[spot : spot + 16] = g[spot : spot + 16] + block if add else block

    for r in range(per_tile):
        rot[r, 0:rows] = own[...] if r == 0 else pltpu.roll(own[...], width * r, 1)
    steps = half // chunk
    build(0, steps)
    for i in range(count):
        products(i, slice(0, half), False)

    @pl.when(has_from)
    def _():
        halo.wait_recv()

    @pl.when(jnp.logical_not(has_from))
    def _():
        land[...] = jnp.zeros_like(land)

    for r in range(per_tile):
        rot[r, rows : rows + half] = land[...] if r == 0 else pltpu.roll(land[...], width * r, 1)
    build(steps, steps)

    units = g.shape[0] // SEGMENTS
    side = units // 2
    color_part = side // 2
    ring_part = color_part // 4
    small = ring_part // 4
    sems = iter(range(SEGMENTS * 42))
    ids = [[[next(sems) for _ in range(n)] for n in (2, 6, 6, 7, 7, 6, 6, 2)] for _ in range(SEGMENTS)]

    def ring(color, d, first):
        if (color == 0) == first:
            at = lax.rem(x + d, NX)
            return device(at, y, z, c), at
        at = lax.rem(y + d, NY)
        return device(x, at, z, c), at

    def send_to(src, dst, s, stage, n, dev):
        k = ids[s][stage][n]
        return remote(src, dst, ssend.at[k], srecv.at[k], dev)

    partner = device(x, y, z, 1 - c)
    plain = []
    stages = [[[] for _ in range(8)] for _ in range(SEGMENTS)]

    def go(s, stage, cp):
        cp.start()
        stages[s][stage].append(cp)
        plain.append(cp)

    def cores(s):
        for color in range(2):
            at = pl.ds(s * units + (1 - c) * side + color * color_part, color_part)
            go(s, 0, send_to(g.at[at], rc.at[s, color], s, 0, color, partner))

    def ring_first(s):
        for color in range(2):
            stages[s][0][color].wait_recv()
            at = pl.ds(s * units + c * side + color * color_part, color_part)
            h[s, color] = g[at] + rc[s, color]
            for d in range(1, 4):
                dev, spot = ring(color, d, True)
                go(s, 1, send_to(h.at[s, color, pl.ds(spot * ring_part, ring_part)],
                                 ra.at[s, color, d - 1], s, 1, 3 * color + d - 1, dev))

    def ring_second(s):
        for color in range(2):
            for cp in stages[s][1][3 * color : 3 * color + 3]:
                cp.wait_recv()
            _, spot = ring(color, 0, True)
            sa[s, color] = ((h[s, color, pl.ds(spot * ring_part, ring_part)] + ra[s, color, 0])
                            + (ra[s, color, 1] + ra[s, color, 2]))
            for d in range(1, 4):
                dev, spot = ring(color, d, False)
                go(s, 2, send_to(sa.at[s, color, pl.ds(spot * small, small)],
                                 rb.at[s, color, d - 1], s, 2, 3 * color + d - 1, dev))

    size = 2 * small // OWNERS
    mine = jnp.minimum(z, OWNERS - 1)

    def along_z(s):
        for color in range(2):
            for cp in stages[s][2][3 * color : 3 * color + 3]:
                cp.wait_recv()
            _, spot = ring(color, 0, False)
            ys[s, color * small : (color + 1) * small] = (
                (sa[s, color, pl.ds(spot * small, small)] + rb[s, color, 0])
                + (rb[s, color, 1] + rb[s, color, 2]))
        for d in range(1, NZ):
            dst = lax.rem(z + d, NZ)
            at = pl.ds(jnp.minimum(dst, OWNERS - 1) * size, size)
            cp = send_to(ys.at[s, at], rz.at[s, d - 1], s, 3, d - 1, device(x, y, dst, c))
            pl.when(dst < OWNERS)(cp.start)
            stages[s][3].append(cp)

    def spot_of(s, p):
        color = p // (OWNERS // 2)
        chunk_at = jnp.where(color == 0, x * 4 + y, y * 4 + x)
        return (s * units + c * side + color * color_part + chunk_at * small
                + lax.rem(p, OWNERS // 2) * size)

    def back_z(s):
        at = pl.ds(spot_of(s, mine), size)

        @pl.when(z < OWNERS)
        def _():
            total = ys[s, pl.ds(mine * size, size)]
            for d in range(1, NZ):
                stages[s][3][d - 1].wait_recv()
                total = total + rz[s, d - 1]
            out_ref[at] = total

        for d in range(1, NZ):
            cp = send_to(out_ref.at[at], out_ref.at[at], s, 4, d - 1,
                         device(x, y, lax.rem(z + d, NZ), c))
            pl.when(z < OWNERS)(cp.start)
            stages[s][4].append(cp)

    def back_second(s):
        for d in range(1, NZ):
            pl.when(lax.rem(z - d + NZ, NZ) < OWNERS)(stages[s][4][d - 1].wait_recv)
        for color in range(2):
            _, spot = ring(color, 0, True)
            _, sub = ring(color, 0, False)
            at = pl.ds(s * units + c * side + color * color_part + spot * ring_part + sub * small,
                       small)
            for d in range(1, 4):
                dev, _ = ring(color, d, False)
                go(s, 5, send_to(out_ref.at[at], out_ref.at[at], s, 5, 3 * color + d - 1, dev))

    def back_first(s):
        for color in range(2):
            for cp in stages[s][5][3 * color : 3 * color + 3]:
                cp.wait_recv()
            _, spot = ring(color, 0, True)
            at = pl.ds(s * units + c * side + color * color_part + spot * ring_part, ring_part)
            for d in range(1, 4):
                dev, _ = ring(color, d, True)
                go(s, 6, send_to(out_ref.at[at], out_ref.at[at], s, 6, 3 * color + d - 1, dev))

    def back_cores(s):
        for color in range(2):
            for cp in stages[s][6][3 * color : 3 * color + 3]:
                cp.wait_recv()
            at = pl.ds(s * units + c * side + color * color_part, color_part)
            go(s, 7, send_to(out_ref.at[at], out_ref.at[at], s, 7, color, partner))

    def last(s):
        for cp in stages[s][7]:
            cp.wait_recv()

    done = 0
    for s in range(SEGMENTS):
        while first_block(done, count) * 16 < (s + 1) * units:
            products(done, slice(half, rows), True)
            done += 1
        cores(s)
    chain = (ring_first, ring_second, along_z, back_z, back_second, back_first, back_cores, last)
    for slot in range(len(chain) + SEGMENTS - 1):
        for s in range(SEGMENTS):
            if 0 <= slot - s < len(chain):
                chain[slot - s](s)

    for ph in range(2):
        for cp in fars[ph] + nears[ph] + pairs[ph]:
            cp.wait_send()
    pl.when(has_to)(halo.wait_send)
    for cp in plain:
        cp.wait_send()
    for s in range(SEGMENTS):
        for d in range(1, NZ):
            pl.when(lax.rem(z + d, NZ) < OWNERS)(stages[s][3][d - 1].wait_send)
            pl.when(z < OWNERS)(stages[s][4][d - 1].wait_send)


def gram_blocks(signals, channel_node, lags):
    length, chans = signals.shape
    rows = length // NX
    size = lags.shape[0] * NODES
    count = size // NB
    blocks = count * (count + 1) // 2
    side = blocks * 16 // SEGMENTS // 2
    tiles = lambda *lead: pltpu.VMEM(lead + (8, NB), F32)
    quarters = pltpu.VMEM((2, 2, rows // 4, NODES), F32)
    S = SEGMENTS
    dma = pltpu.SemaphoreType.DMA
    total = pl.pallas_call(
        functools.partial(gram_body, lags.shape[0]),
        out_shape=jax.ShapeDtypeStruct((blocks * 16, 8, NB), F32),
        in_specs=[pl.BlockSpec(memory_space=pltpu.SMEM), pl.BlockSpec(memory_space=pl.ANY), VMEM],
        out_specs=VMEM,
        scratch_shapes=[
            pltpu.VMEM((length, chans), BF16), pltpu.VMEM((length, NODES), F32),
            quarters, quarters, quarters, quarters,
            pltpu.VMEM((rows, NODES), F32), pltpu.VMEM((MAXLAG, NODES), F32),
            pltpu.VMEM((NX, rows + MAXLAG, NODES), F32),
            pltpu.VMEM((rows, size), BF16), pltpu.VMEM((rows, size), BF16),
            tiles(blocks * 16), tiles(S, 2, side // 2), tiles(S, 2, side // 2),
            tiles(S, 2, 3, side // 8), tiles(S, 2, side // 8), tiles(S, 2, 3, side // 32),
            tiles(S, side // 16), tiles(S, NZ - 1, side // 16 // OWNERS),
            dma((8,)), dma((13,)), dma((13,)), dma((S * 42,)), dma((S * 42,)),
        ],
        compiler_params=pltpu.CompilerParams(
            collective_id=1, has_side_effects=True, vmem_limit_bytes=56 << 20),
    )(lags, signals, channel_node.reshape(1, chans))
    return total.reshape(blocks, NB, NB)


def lanes(x, c):
    return jnp.broadcast_to(x[:, c : c + 1], x.shape)


def subs(x, r):
    return jnp.broadcast_to(x[r : r + 1, :], x.shape)


def factor_block(rows):
    count = NB // 8
    lane = lax.broadcasted_iota(jnp.int32, (8, NB), 1)
    sub = lax.broadcasted_iota(jnp.int32, (8, NB), 0)
    rows = list(rows)
    upper, inv = [], []
    cur = [lanes(rows[0], j) for j in range(8)]
    for p in range(count):
        r0 = 8 * p
        raw = {b: [lanes(rows[b], r0 + j) for j in range(8)] for b in range(p + 1, count)}
        ahead = [lanes(rows[p + 1], r0 + 8 + j) for j in range(8)] if p + 1 < count else None
        here = jnp.logical_and(lane >= r0, lane < r0 + 8)
        top, low = rows[p], jnp.where(here, jnp.where(lane == sub + r0, 1.0, 0.0), rows[p])
        for b in range(p + 1, count):
            rows[b] = jnp.where(here, 0.0, rows[b])
        v, m, s, rinv = list(cur), [None] * 8, [[None] * 8 for _ in range(8)], [None] * 8
        diag = None
        for j in range(8):
            diag = v[j] if diag is None else jnp.where(sub >= j, v[j], diag)
            rinv[j] = 1.0 / subs(v[j], j)
            whole = v[j] * rinv[j]
            for k in range(j + 1, 8):
                s[j][k] = subs(v[j], k)
                if k == j + 1:
                    v[k] = v[k] - (v[j] * s[j][k]) * rinv[j]
                else:
                    v[k] = v[k] - whole * s[j][k]
            m[j] = jnp.where(sub > j, whole, 0.0)
        rs = lax.rsqrt(diag)
        ra = []
        for j in range(8):
            ra.append(subs(low, j))
            da = subs(top, j)
            low = low - m[j] * ra[j]
            top = top - m[j] * da
        for b in range(p + 1, count):
            u, mb = [], []
            for j in range(8):
                value = raw[b][j]
                for i in range(j):
                    value = value - mb[i] * s[i][j]
                u.append(value)
                mb.append(value * rinv[j])
            if b == p + 1:
                cur = []
                for i in range(8):
                    value = ahead[i]
                    for j in range(8):
                        value = value - mb[j] * subs(u[j], i)
                    cur.append(value)
            for j in range(8):
                rows[b] = rows[b] - mb[j] * ra[j]
        upper.append(jnp.where(lane >= sub + r0, top * rs, 0.0))
        inv.append(jnp.where(lane < r0 + 8, low * rs, 0.0))
    return upper, inv


DOT = dict(precision=lax.Precision.HIGHEST, preferred_element_type=F32)


def factor_body(count, scale, g_hbm, out_hbm, g_ref, r_ref, w_ref, d_ref, sem):
    def fetch(k):
        at = pl.ds(first_block(k, count), count - k)
        return pltpu.make_async_copy(g_hbm.at[at], g_ref.at[at], sem.at[count + k])

    for k in range(count):
        fetch(k).start()
    r_ref[...] = jnp.zeros_like(r_ref)

    def leave(k):
        at = pl.ds(k * NB, NB)
        return pltpu.make_async_copy(r_ref.at[at], out_hbm.at[at], sem.at[k])

    def update(k):
        r0 = k * NB
        first = first_block(k, count)
        fetch(k).wait()
        for j in range(k, count):
            r_ref[r0 : r0 + NB, j * NB : (j + 1) * NB] = g_ref[first + j - k] * scale
        if k > 0:
            r_ref[r0 : r0 + NB, r0:] -= lax.dot_general(
                r_ref[0:r0, r0 : r0 + NB], r_ref[0:r0, r0:], (((0,), (0,)), ((), ())), **DOT
            )
        d_ref[...] = r_ref[r0 : r0 + NB, r0 : r0 + NB]

    def panel(k):
        r0 = k * NB
        r_ref[r0 : r0 + NB, r0 : r0 + NB] = d_ref[...]
        if k + 1 < count:
            r_ref[r0 : r0 + NB, r0 + NB :] = lax.dot_general(
                w_ref[...], r_ref[r0 : r0 + NB, r0 + NB :], (((1,), (0,)), ((), ())), **DOT
            )
        leave(k).start()

    def step(k, _):
        lax.switch(k, [functools.partial(update, i) for i in range(count)])
        rows, inv = factor_block([d_ref[8 * i : 8 * i + 8, :] for i in range(NB // 8)])
        for i in range(NB // 8):
            d_ref[8 * i : 8 * i + 8, :] = rows[i]
            w_ref[8 * i : 8 * i + 8, :] = inv[i]
        lax.switch(k, [functools.partial(panel, i) for i in range(count)])
        return 0

    lax.fori_loop(0, count, step, 0)
    for k in range(count):
        leave(k).wait()


def upper_factor(blocks, count, scale):
    size = count * NB
    return pl.pallas_call(
        functools.partial(factor_body, count, scale),
        out_shape=jax.ShapeDtypeStruct((size, size), F32),
        in_specs=[pl.BlockSpec(memory_space=pltpu.HBM)],
        out_specs=pl.BlockSpec(memory_space=pltpu.HBM),
        scratch_shapes=[pltpu.VMEM(blocks.shape, F32), pltpu.VMEM((size, size), F32), pltpu.VMEM((NB, NB), F32),
                        pltpu.VMEM((NB, NB), F32), pltpu.SemaphoreType.DMA((2 * count,))],
        compiler_params=pltpu.CompilerParams(vmem_limit_bytes=48 << 20),
    )(blocks)


def on_device(signals, channel_node, lag_offsets):
    total_rows = signals.shape[0] * lax.axis_size("tm")
    count = lag_offsets.shape[0] * NODES // NB
    blocks = gram_blocks(signals, channel_node, lag_offsets)
    return upper_factor(blocks, count, 1.0 / total_rows)


def solution(mesh):
    in_specs = (P("tm", "chan"), P("chan"), P())
    out_specs = P()
    return jax.shard_map(
        on_device, mesh=mesh, in_specs=in_specs, out_specs=out_specs, check_vma=False
    )
```

```python
import functools
import math

import jax
import jax.numpy as jnp
from jax import lax
from jax.experimental import pallas as pl
from jax.experimental.pallas import tpu as pltpu
from jax.sharding import PartitionSpec as P

NODES = 128
CH = 2048
MAXLAG = 512
F32 = jnp.float32
BF16 = jnp.bfloat16
MESH = pl.DeviceIdType.MESH
VMEM = pl.BlockSpec(memory_space=pltpu.VMEM)
NB = 128
NX, NY, NZ = 4, 4, 8
SEGMENTS = 1
OWNERS = 6


def first_block(i, count):
    return i * count - i * (i - 1) // 2


def device(x, y, z, c):
    return {"tm": (y * NZ + z) * 2 + c, "chan": x}


def remote(src, dst, send, recv, target):
    return pltpu.make_async_remote_copy(
        src_ref=src, dst_ref=dst, send_sem=send, recv_sem=recv,
        device_id=target, device_id_type=MESH,
    )


def gram_body(lag_count, lags_ref, s_hbm, node_ref, out_ref,
              sig, part, far, near, pair, fwd, own, land, rot, hi, lo,
              g, rc, h, ra, sa, rb, ys, rz, load, send, recv, ssend, srecv):
    x, t = lax.axis_index("chan"), lax.axis_index("tm")
    y, z, c = t // (NZ * 2), lax.rem(t // 2, NZ), lax.rem(t, 2)
    rows = own.shape[0]
    half, quarter = rows // 2, rows // 4

    def chunk_of(at):
        return jnp.where(c == 0, at, 3 - at)

    others = (x + 1 - 2 * lax.rem(x, 2), 3 - x)
    opposite = lax.rem(x + 2, 4)
    loads = []
    for ph in range(2):
        for i, at in enumerate((opposite, others[0], others[1], x)):
            rows_at = pl.ds(pl.multiple_of(chunk_of(at) * rows + ph * half, half), half)
            cp = pltpu.make_async_copy(s_hbm.at[rows_at], sig.at[rows_at], load.at[ph * 4 + i])
            cp.start()
            loads.append((cp, rows_at))
    b = chunk_of(x)
    has_to = jnp.logical_or(b > 0, t > 0)
    has_from = jnp.logical_or(b < 3, t < 2 * NY * NZ - 1)
    step = 1 - 2 * c
    to = {"tm": jnp.where(b > 0, t, jnp.maximum(t - 1, 0)), "chan": jnp.where(b > 0, x - step, x)}
    source = {"tm": jnp.where(b < 3, t, jnp.minimum(t + 1, 2 * NY * NZ - 1)),
              "chan": jnp.where(b < 3, x + step, x)}
    barrier = pltpu.get_barrier_semaphore()
    peers = [device(x, y, z, 1 - c)]
    peers += [device(lax.rem(x + d, NX), y, z, c) for d in range(1, NX)]
    peers += [device(x, lax.rem(y + d, NY), z, c) for d in range(1, NY)]
    peers += [device(x, y, lax.rem(z + d, NZ), c) for d in range(1, NZ)]
    for dev in peers:
        pl.semaphore_signal(barrier, inc=1, device_id=dev, device_id_type=MESH)

    @pl.when(has_to)
    def _():
        pl.semaphore_signal(barrier, inc=1, device_id=to, device_id_type=MESH)

    @pl.when(has_from)
    def _():
        pl.semaphore_signal(barrier, inc=1, device_id=source, device_id_type=MESH)

    scale = 1.0 / math.sqrt(CH // NODES)
    chans = node_ref.shape[1]
    match = lax.broadcasted_iota(jnp.int32, (NODES, chans), 0) == node_ref[...]
    onehot = jnp.where(match, scale, 0.0).astype(BF16)

    def sums(ph, i):
        cp, rows_at = loads[ph * 4 + i]
        cp.wait()
        part[rows_at] = lax.dot_general(sig[rows_at], onehot, (((1,), (1,)), ((), ())),
                                        preferred_element_type=F32)

    def piece(at, ph, color):
        first = chunk_of(at) * rows + ph * half + color * quarter
        return pl.ds(pl.multiple_of(first, quarter), quarter)

    link = tuple(device(at, y, z, c) for at in others)

    def copy(src, dst, kind, ph, color, dev):
        s = (kind * 2 + ph) * 2 + color
        return remote(src, dst, send.at[s], recv.at[s], dev)

    sums(0, 0)
    pl.semaphore_wait(barrier, len(peers) + has_to.astype(jnp.int32) + has_from.astype(jnp.int32))
    fars, nears, pairs = [], [], []
    for ph in range(2):
        fars.append([copy(part.at[piece(opposite, ph, k)], far.at[ph, k], 0, ph, k, link[k])
                     for k in range(2)])
        nears.append([copy(part.at[piece(others[k], ph, k)], near.at[ph, k], 1, ph, k, link[k])
                      for k in range(2)])
        pairs.append([copy(fwd.at[ph, k], pair.at[ph, k], 2, ph, k, link[1 - k])
                      for k in range(2)])

    def forward(ph):
        for k in range(2):
            fars[ph][k].wait_recv()
            fwd[ph, k] = part[piece(others[1 - k], ph, k)] + far[ph, k]
            pairs[ph][k].start()

    def finish(ph):
        for k in range(2):
            nears[ph][k].wait_recv()
            pairs[ph][k].wait_recv()
            at = ph * half + k * quarter
            own[at : at + quarter] = part[piece(x, ph, k)] + near[ph, k] + pair[ph, k]

    for cp in fars[0]:
        cp.start()
    sums(0, 1)
    nears[0][0].start()
    sums(0, 2)
    nears[0][1].start()
    for i in range(4):
        sums(1, i)
    sums(0, 3)
    forward(0)
    for cp in fars[1] + nears[1]:
        cp.start()
    finish(0)
    forward(1)
    halo = remote(own.at[0:half], land, send.at[12], recv.at[12], to)
    pl.when(has_to)(halo.start)
    finish(1)

    width = NODES // NX
    per_tile = NB // width
    count = lag_count * NODES // NB
    chunk = 128
    lane_group = lax.broadcasted_iota(jnp.int32, (chunk, NB), 1) // width

    def build(first_step, steps):
        for tile in range(count):
            group, top = tile // (count // NX), tile % (count // NX)

            def fill(i, _):
                value = None
                for m in range(per_tile):
                    first = lags_ref[top * per_tile + m] + i * chunk
                    got = rot[(m - group) % per_tile, pl.ds(first, chunk), :]
                    value = got if value is None else jnp.where(lane_group == m, got, value)
                high = value.astype(BF16)
                at = pl.ds(pl.multiple_of(i * chunk, chunk), chunk)
                hi[at, tile * NB : (tile + 1) * NB] = high
                lo[at, tile * NB : (tile + 1) * NB] = (value - high.astype(F32)).astype(BF16)
                return 0

            lax.fori_loop(first_step, first_step + steps, fill, 0)

    dims = (((0,), (0,)), ((), ()))

    def products(i, at, add):
        a, d = hi[at, i * NB : (i + 1) * NB], lo[at, i * NB : (i + 1) * NB]
        value = lax.dot_general(a, lo[at, i * NB :], dims, preferred_element_type=F32)
        value += lax.dot_general(d, hi[at, i * NB :], dims, preferred_element_type=F32)
        value += lax.dot_general(a, hi[at, i * NB :], dims, preferred_element_type=F32)
        square = lax.dot_general(d, d, dims, preferred_element_type=F32)
        for j in range(i, count):
            spot = 16 * (first_block(i, count) + j - i)
            block = value[:, (j - i) * NB : (j - i + 1) * NB]
            block = (block + square if j == i else block).reshape(16, 8, NB)
            g[spot : spot + 16] = g[spot : spot + 16] + block if add else block

    for r in range(per_tile):
        rot[r, 0:rows] = own[...] if r == 0 else pltpu.roll(own[...], width * r, 1)
    steps = half // chunk
    build(0, steps)
    for i in range(count):
        products(i, slice(0, half), False)

    @pl.when(has_from)
    def _():
        halo.wait_recv()

    @pl.when(jnp.logical_not(has_from))
    def _():
        land[...] = jnp.zeros_like(land)

    for r in range(per_tile):
        rot[r, rows : rows + half] = land[...] if r == 0 else pltpu.roll(land[...], width * r, 1)
    build(steps, steps)

    units = g.shape[0] // SEGMENTS
    side = units // 2
    color_part = side // 2
    ring_part = color_part // 4
    small = ring_part // 4
    sems = iter(range(SEGMENTS * 42))
    ids = [[[next(sems) for _ in range(n)] for n in (2, 6, 6, 7, 7, 6, 6, 2)] for _ in range(SEGMENTS)]

    def ring(color, d, first):
        if (color == 0) == first:
            at = lax.rem(x + d, NX)
            return device(at, y, z, c), at
        at = lax.rem(y + d, NY)
        return device(x, at, z, c), at

    def send_to(src, dst, s, stage, n, dev):
        k = ids[s][stage][n]
        return remote(src, dst, ssend.at[k], srecv.at[k], dev)

    partner = device(x, y, z, 1 - c)
    plain = []
    stages = [[[] for _ in range(8)] for _ in range(SEGMENTS)]

    def go(s, stage, cp):
        cp.start()
        stages[s][stage].append(cp)
        plain.append(cp)

    def cores(s):
        for color in range(2):
            at = pl.ds(s * units + (1 - c) * side + color * color_part, color_part)
            go(s, 0, send_to(g.at[at], rc.at[s, color], s, 0, color, partner))

    def ring_first(s):
        for color in range(2):
            stages[s][0][color].wait_recv()
            at = pl.ds(s * units + c * side + color * color_part, color_part)
            h[s, color] = g[at] + rc[s, color]
            for d in range(1, 4):
                dev, spot = ring(color, d, True)
                go(s, 1, send_to(h.at[s, color, pl.ds(spot * ring_part, ring_part)],
                                 ra.at[s, color, d - 1], s, 1, 3 * color + d - 1, dev))

    def ring_second(s):
        for color in range(2):
            for cp in stages[s][1][3 * color : 3 * color + 3]:
                cp.wait_recv()
            _, spot = ring(color, 0, True)
            sa[s, color] = ((h[s, color, pl.ds(spot * ring_part, ring_part)] + ra[s, color, 0])
                            + (ra[s, color, 1] + ra[s, color, 2]))
            for d in range(1, 4):
                dev, spot = ring(color, d, False)
                go(s, 2, send_to(sa.at[s, color, pl.ds(spot * small, small)],
                                 rb.at[s, color, d - 1], s, 2, 3 * color + d - 1, dev))

    size = 2 * small // OWNERS
    mine = jnp.minimum(z, OWNERS - 1)

    def along_z(s):
        for color in range(2):
            for cp in stages[s][2][3 * color : 3 * color + 3]:
                cp.wait_recv()
            _, spot = ring(color, 0, False)
            ys[s, color * small : (color + 1) * small] = (
                (sa[s, color, pl.ds(spot * small, small)] + rb[s, color, 0])
                + (rb[s, color, 1] + rb[s, color, 2]))
        for d in range(1, NZ):
            dst = lax.rem(z + d, NZ)
            at = pl.ds(jnp.minimum(dst, OWNERS - 1) * size, size)
            cp = send_to(ys.at[s, at], rz.at[s, d - 1], s, 3, d - 1, device(x, y, dst, c))
            pl.when(dst < OWNERS)(cp.start)
            stages[s][3].append(cp)

    def spot_of(s, p):
        color = p // (OWNERS // 2)
        chunk_at = jnp.where(color == 0, x * 4 + y, y * 4 + x)
        return (s * units + c * side + color * color_part + chunk_at * small
                + lax.rem(p, OWNERS // 2) * size)

    def back_z(s):
        at = pl.ds(spot_of(s, mine), size)

        @pl.when(z < OWNERS)
        def _():
            total = ys[s, pl.ds(mine * size, size)]
            for d in range(1, NZ):
                stages[s][3][d - 1].wait_recv()
                total = total + rz[s, d - 1]
            out_ref[at] = total

        for d in range(1, NZ):
            cp = send_to(out_ref.at[at], out_ref.at[at], s, 4, d - 1,
                         device(x, y, lax.rem(z + d, NZ), c))
            pl.when(z < OWNERS)(cp.start)
            stages[s][4].append(cp)

    def back_second(s):
        for d in range(1, NZ):
            pl.when(lax.rem(z - d + NZ, NZ) < OWNERS)(stages[s][4][d - 1].wait_recv)
        for color in range(2):
            _, spot = ring(color, 0, True)
            _, sub = ring(color, 0, False)
            at = pl.ds(s * units + c * side + color * color_part + spot * ring_part + sub * small,
                       small)
            for d in range(1, 4):
                dev, _ = ring(color, d, False)
                go(s, 5, send_to(out_ref.at[at], out_ref.at[at], s, 5, 3 * color + d - 1, dev))

    def back_first(s):
        for color in range(2):
            for cp in stages[s][5][3 * color : 3 * color + 3]:
                cp.wait_recv()
            _, spot = ring(color, 0, True)
            at = pl.ds(s * units + c * side + color * color_part + spot * ring_part, ring_part)
            for d in range(1, 4):
                dev, _ = ring(color, d, True)
                go(s, 6, send_to(out_ref.at[at], out_ref.at[at], s, 6, 3 * color + d - 1, dev))

    def back_cores(s):
        for color in range(2):
            for cp in stages[s][6][3 * color : 3 * color + 3]:
                cp.wait_recv()
            at = pl.ds(s * units + c * side + color * color_part, color_part)
            go(s, 7, send_to(out_ref.at[at], out_ref.at[at], s, 7, color, partner))

    def last(s):
        for cp in stages[s][7]:
            cp.wait_recv()

    done = 0
    for s in range(SEGMENTS):
        while first_block(done, count) * 16 < (s + 1) * units:
            products(done, slice(half, rows), True)
            done += 1
        cores(s)
    chain = (ring_first, ring_second, along_z, back_z, back_second, back_first, back_cores, last)
    for slot in range(len(chain) + SEGMENTS - 1):
        for s in range(SEGMENTS):
            if 0 <= slot - s < len(chain):
                chain[slot - s](s)

    for ph in range(2):
        for cp in fars[ph] + nears[ph] + pairs[ph]:
            cp.wait_send()
    pl.when(has_to)(halo.wait_send)
    for cp in plain:
        cp.wait_send()
    for s in range(SEGMENTS):
        for d in range(1, NZ):
            pl.when(lax.rem(z + d, NZ) < OWNERS)(stages[s][3][d - 1].wait_send)
            pl.when(z < OWNERS)(stages[s][4][d - 1].wait_send)


def gram_blocks(signals, channel_node, lags):
    length, chans = signals.shape
    rows = length // NX
    size = lags.shape[0] * NODES
    count = size // NB
    blocks = count * (count + 1) // 2
    side = blocks * 16 // SEGMENTS // 2
    tiles = lambda *lead: pltpu.VMEM(lead + (8, NB), F32)
    quarters = pltpu.VMEM((2, 2, rows // 4, NODES), F32)
    S = SEGMENTS
    dma = pltpu.SemaphoreType.DMA
    total = pl.pallas_call(
        functools.partial(gram_body, lags.shape[0]),
        out_shape=jax.ShapeDtypeStruct((blocks * 16, 8, NB), F32),
        in_specs=[pl.BlockSpec(memory_space=pltpu.SMEM), pl.BlockSpec(memory_space=pl.ANY), VMEM],
        out_specs=VMEM,
        scratch_shapes=[
            pltpu.VMEM((length, chans), BF16), pltpu.VMEM((length, NODES), F32),
            quarters, quarters, quarters, quarters,
            pltpu.VMEM((rows, NODES), F32), pltpu.VMEM((MAXLAG, NODES), F32),
            pltpu.VMEM((NX, rows + MAXLAG, NODES), F32),
            pltpu.VMEM((rows, size), BF16), pltpu.VMEM((rows, size), BF16),
            tiles(blocks * 16), tiles(S, 2, side // 2), tiles(S, 2, side // 2),
            tiles(S, 2, 3, side // 8), tiles(S, 2, side // 8), tiles(S, 2, 3, side // 32),
            tiles(S, side // 16), tiles(S, NZ - 1, side // 16 // OWNERS),
            dma((8,)), dma((13,)), dma((13,)), dma((S * 42,)), dma((S * 42,)),
        ],
        compiler_params=pltpu.CompilerParams(
            collective_id=1, has_side_effects=True, vmem_limit_bytes=56 << 20),
    )(lags, signals, channel_node.reshape(1, chans))
    return total.reshape(blocks, NB, NB)


DOT = dict(precision=lax.Precision.HIGHEST, preferred_element_type=F32)


def lanes(x, c):
    return jnp.broadcast_to(x[:, c : c + 1], x.shape)


def subs(x, r):
    return jnp.broadcast_to(x[r : r + 1, :], x.shape)


def factor_block(rows):
    count = NB // 8
    lane = lax.broadcasted_iota(jnp.int32, (8, NB), 1)
    sub = lax.broadcasted_iota(jnp.int32, (8, NB), 0)
    rows = list(rows)
    upper, inv, merged = [], [], []
    cur = [lanes(rows[0], j) for j in range(8)]
    for p in range(count):
        r0 = 8 * p
        end = count // 2 if p < count // 2 else count
        if p == count // 2:
            above = jnp.concatenate(merged, axis=0)
            product = lax.dot_general(above, above, (((0,), (0,)), ((), ())), **DOT)
            for b in range(p, count):
                rows[b] = jnp.where(lane >= r0, rows[b], 0.0) - product[8 * b : 8 * b + 8]
            cur = [lanes(rows[p], r0 + j) for j in range(8)]
        raw = {b: [lanes(rows[b], r0 + j) for j in range(8)] for b in range(p + 1, end)}
        ahead = [lanes(rows[p + 1], r0 + 8 + j) for j in range(8)] if p + 1 < end else None
        here = jnp.logical_and(lane >= r0, lane < r0 + 8)
        top, low = rows[p], jnp.where(here, jnp.where(lane == sub + r0, 1.0, 0.0), rows[p])
        for b in range(p + 1, end):
            rows[b] = jnp.where(here, 0.0, rows[b])
        v, m, s, rinv = list(cur), [None] * 8, [[None] * 8 for _ in range(8)], [None] * 8
        diag = None
        for j in range(8):
            diag = v[j] if diag is None else jnp.where(sub >= j, v[j], diag)
            rinv[j] = 1.0 / subs(v[j], j)
            whole = v[j] * rinv[j]
            for k in range(j + 1, 8):
                s[j][k] = subs(v[j], k)
                if k == j + 1:
                    v[k] = v[k] - (v[j] * s[j][k]) * rinv[j]
                else:
                    v[k] = v[k] - whole * s[j][k]
            m[j] = jnp.where(sub > j, whole, 0.0)
        rs = lax.rsqrt(diag)
        ra = []
        for j in range(8):
            ra.append(subs(low, j))
            da = subs(top, j)
            low = low - m[j] * ra[j]
            top = top - m[j] * da
        for b in range(p + 1, end):
            u, mb = [], []
            for j in range(8):
                value = raw[b][j]
                for i in range(j):
                    value = value - mb[i] * s[i][j]
                u.append(value)
                mb.append(value * rinv[j])
            if b == p + 1:
                cur = []
                for i in range(8):
                    value = ahead[i]
                    for j in range(8):
                        value = value - mb[j] * subs(u[j], i)
                    cur.append(value)
            for j in range(8):
                rows[b] = rows[b] - mb[j] * ra[j]
        upper.append(jnp.where(lane >= sub + r0, top * rs, 0.0))
        inv.append(jnp.where(lane < r0 + 8, low * rs, 0.0))
        merged.append(jnp.where(lane < NB // 2, inv[-1], upper[-1]))
    return upper, inv


def factor_body(count, scale, g_hbm, out_hbm, g_ref, r_ref, w_ref, d_ref, sem):
    def fetch(k):
        at = pl.ds(first_block(k, count), count - k)
        return pltpu.make_async_copy(g_hbm.at[at], g_ref.at[at], sem.at[count + k])

    for k in range(count):
        fetch(k).start()
    r_ref[...] = jnp.zeros_like(r_ref)

    def leave(k):
        at = pl.ds(k * NB, NB)
        return pltpu.make_async_copy(r_ref.at[at], out_hbm.at[at], sem.at[k])

    def update(k):
        r0 = k * NB
        first = first_block(k, count)
        fetch(k).wait()
        for j in range(k, count):
            r_ref[r0 : r0 + NB, j * NB : (j + 1) * NB] = g_ref[first + j - k] * scale
        if k > 0:
            r_ref[r0 : r0 + NB, r0:] -= lax.dot_general(
                r_ref[0:r0, r0 : r0 + NB], r_ref[0:r0, r0:], (((0,), (0,)), ((), ())), **DOT
            )
        d_ref[...] = r_ref[r0 : r0 + NB, r0 : r0 + NB]

    def panel(k):
        r0 = k * NB
        r_ref[r0 : r0 + NB, r0 : r0 + NB] = d_ref[...]
        if k + 1 < count:
            r_ref[r0 : r0 + NB, r0 + NB :] = lax.dot_general(
                w_ref[...], r_ref[r0 : r0 + NB, r0 + NB :], (((1,), (0,)), ((), ())), **DOT
            )
        leave(k).start()

    def step(k, _):
        lax.switch(k, [functools.partial(update, i) for i in range(count)])
        rows, inv = factor_block([d_ref[8 * i : 8 * i + 8, :] for i in range(NB // 8)])
        for i in range(NB // 8):
            d_ref[8 * i : 8 * i + 8, :] = rows[i]
            w_ref[8 * i : 8 * i + 8, :] = inv[i]
        lax.switch(k, [functools.partial(panel, i) for i in range(count)])
        return 0

    lax.fori_loop(0, count, step, 0)
    for k in range(count):
        leave(k).wait()


def upper_factor(blocks, count, scale):
    size = count * NB
    return pl.pallas_call(
        functools.partial(factor_body, count, scale),
        out_shape=jax.ShapeDtypeStruct((size, size), F32),
        in_specs=[pl.BlockSpec(memory_space=pltpu.HBM)],
        out_specs=pl.BlockSpec(memory_space=pltpu.HBM),
        scratch_shapes=[pltpu.VMEM(blocks.shape, F32), pltpu.VMEM((size, size), F32), pltpu.VMEM((NB, NB), F32),
                        pltpu.VMEM((NB, NB), F32), pltpu.SemaphoreType.DMA((2 * count,))],
        compiler_params=pltpu.CompilerParams(vmem_limit_bytes=63_000_000),
    )(blocks)


def on_device(signals, channel_node, lag_offsets):
    total_rows = signals.shape[0] * lax.axis_size("tm")
    count = lag_offsets.shape[0] * NODES // NB
    blocks = gram_blocks(signals, channel_node, lag_offsets)
    return upper_factor(blocks, count, 1.0 / total_rows)


def solution(mesh):
    in_specs = (P("tm", "chan"), P("chan"), P())
    out_specs = P()
    return jax.shard_map(
        on_device, mesh=mesh, in_specs=in_specs, out_specs=out_specs, check_vma=False
    )
```

```python
import functools
import math

import jax
import jax.numpy as jnp
from jax import lax
from jax.experimental import pallas as pl
from jax.experimental.pallas import tpu as pltpu
from jax.sharding import PartitionSpec as P

NODES = 128
CH = 2048
MAXLAG = 512
F32 = jnp.float32
BF16 = jnp.bfloat16
MESH = pl.DeviceIdType.MESH
VMEM = pl.BlockSpec(memory_space=pltpu.VMEM)
NB = 128
NX, NY, NZ = 4, 4, 8
SEGMENTS = 1
OWNERS = 6


def first_block(i, count):
    return i * count - i * (i - 1) // 2


def device(x, y, z, c):
    return {"tm": (y * NZ + z) * 2 + c, "chan": x}


def remote(src, dst, send, recv, target):
    return pltpu.make_async_remote_copy(
        src_ref=src, dst_ref=dst, send_sem=send, recv_sem=recv,
        device_id=target, device_id_type=MESH,
    )


def gram_body(lag_count, lags_ref, s_hbm, node_ref, out_ref,
              sig, part, far, near, pair, fwd, own, land, rot, hi, lo,
              g, rc, h, ra, sa, rb, ys, rz, load, send, recv, ssend, srecv):
    x, t = lax.axis_index("chan"), lax.axis_index("tm")
    y, z, c = t // (NZ * 2), lax.rem(t // 2, NZ), lax.rem(t, 2)
    rows = own.shape[0]
    half, quarter = rows // 2, rows // 4

    def chunk_of(at):
        return jnp.where(c == 0, at, 3 - at)

    others = (x + 1 - 2 * lax.rem(x, 2), 3 - x)
    opposite = lax.rem(x + 2, 4)
    loads = []
    for ph in range(2):
        for i, at in enumerate((opposite, others[0], others[1], x)):
            rows_at = pl.ds(pl.multiple_of(chunk_of(at) * rows + ph * half, half), half)
            cp = pltpu.make_async_copy(s_hbm.at[rows_at], sig.at[rows_at], load.at[ph * 4 + i])
            cp.start()
            loads.append((cp, rows_at))
    b = chunk_of(x)
    has_to = jnp.logical_or(b > 0, t > 0)
    has_from = jnp.logical_or(b < 3, t < 2 * NY * NZ - 1)
    step = 1 - 2 * c
    to = {"tm": jnp.where(b > 0, t, jnp.maximum(t - 1, 0)), "chan": jnp.where(b > 0, x - step, x)}
    source = {"tm": jnp.where(b < 3, t, jnp.minimum(t + 1, 2 * NY * NZ - 1)),
              "chan": jnp.where(b < 3, x + step, x)}
    barrier = pltpu.get_barrier_semaphore()
    peers = [device(x, y, z, 1 - c)]
    peers += [device(lax.rem(x + d, NX), y, z, c) for d in range(1, NX)]
    peers += [device(x, lax.rem(y + d, NY), z, c) for d in range(1, NY)]
    peers += [device(x, y, lax.rem(z + d, NZ), c) for d in range(1, NZ)]
    for dev in peers:
        pl.semaphore_signal(barrier, inc=1, device_id=dev, device_id_type=MESH)

    @pl.when(has_to)
    def _():
        pl.semaphore_signal(barrier, inc=1, device_id=to, device_id_type=MESH)

    @pl.when(has_from)
    def _():
        pl.semaphore_signal(barrier, inc=1, device_id=source, device_id_type=MESH)

    scale = 1.0 / math.sqrt(CH // NODES)
    chans = node_ref.shape[1]
    match = lax.broadcasted_iota(jnp.int32, (NODES, chans), 0) == node_ref[...]
    onehot = jnp.where(match, scale, 0.0).astype(BF16)

    def sums(ph, i):
        cp, rows_at = loads[ph * 4 + i]
        cp.wait()
        part[rows_at] = lax.dot_general(sig[rows_at], onehot, (((1,), (1,)), ((), ())),
                                        preferred_element_type=F32)

    def piece(at, ph, color):
        first = chunk_of(at) * rows + ph * half + color * quarter
        return pl.ds(pl.multiple_of(first, quarter), quarter)

    link = tuple(device(at, y, z, c) for at in others)

    def copy(src, dst, kind, ph, color, dev):
        s = (kind * 2 + ph) * 2 + color
        return remote(src, dst, send.at[s], recv.at[s], dev)

    sums(0, 0)
    pl.semaphore_wait(barrier, len(peers) + has_to.astype(jnp.int32) + has_from.astype(jnp.int32))
    fars, nears, pairs = [], [], []
    for ph in range(2):
        fars.append([copy(part.at[piece(opposite, ph, k)], far.at[ph, k], 0, ph, k, link[k])
                     for k in range(2)])
        nears.append([copy(part.at[piece(others[k], ph, k)], near.at[ph, k], 1, ph, k, link[k])
                      for k in range(2)])
        pairs.append([copy(fwd.at[ph, k], pair.at[ph, k], 2, ph, k, link[1 - k])
                      for k in range(2)])

    def forward(ph):
        for k in range(2):
            fars[ph][k].wait_recv()
            fwd[ph, k] = part[piece(others[1 - k], ph, k)] + far[ph, k]
            pairs[ph][k].start()

    def finish(ph):
        for k in range(2):
            nears[ph][k].wait_recv()
            pairs[ph][k].wait_recv()
            at = ph * half + k * quarter
            own[at : at + quarter] = part[piece(x, ph, k)] + near[ph, k] + pair[ph, k]

    for cp in fars[0]:
        cp.start()
    sums(0, 1)
    nears[0][0].start()
    sums(0, 2)
    nears[0][1].start()
    for i in range(4):
        sums(1, i)
    sums(0, 3)
    forward(0)
    for cp in fars[1] + nears[1]:
        cp.start()
    finish(0)
    forward(1)
    halo = remote(own.at[0:half], land, send.at[12], recv.at[12], to)
    pl.when(has_to)(halo.start)
    finish(1)

    width = NODES // NX
    per_tile = NB // width
    count = lag_count * NODES // NB
    chunk = 128
    lane_group = lax.broadcasted_iota(jnp.int32, (chunk, NB), 1) // width

    def build(first_step, steps):
        for tile in range(count):
            group, top = tile // (count // NX), tile % (count // NX)

            def fill(i, _):
                value = None
                for m in range(per_tile):
                    first = lags_ref[top * per_tile + m] + i * chunk
                    got = rot[(m - group) % per_tile, pl.ds(first, chunk), :]
                    value = got if value is None else jnp.where(lane_group == m, got, value)
                high = value.astype(BF16)
                at = pl.ds(pl.multiple_of(i * chunk, chunk), chunk)
                hi[at, tile * NB : (tile + 1) * NB] = high
                lo[at, tile * NB : (tile + 1) * NB] = (value - high.astype(F32)).astype(BF16)
                return 0

            lax.fori_loop(first_step, first_step + steps, fill, 0)

    dims = (((0,), (0,)), ((), ()))

    def products(i, at, add):
        a, d = hi[at, i * NB : (i + 1) * NB], lo[at, i * NB : (i + 1) * NB]
        value = lax.dot_general(a, lo[at, i * NB :], dims, preferred_element_type=F32)
        value += lax.dot_general(d, hi[at, i * NB :], dims, preferred_element_type=F32)
        value += lax.dot_general(a, hi[at, i * NB :], dims, preferred_element_type=F32)
        square = lax.dot_general(d, d, dims, preferred_element_type=F32)
        for j in range(i, count):
            spot = 16 * (first_block(i, count) + j - i)
            block = value[:, (j - i) * NB : (j - i + 1) * NB]
            block = (block + square if j == i else block).reshape(16, 8, NB)
            g[spot : spot + 16] = g[spot : spot + 16] + block if add else block

    for r in range(per_tile):
        rot[r, 0:rows] = own[...] if r == 0 else pltpu.roll(own[...], width * r, 1)
    steps = half // chunk
    build(0, steps)
    for i in range(count):
        products(i, slice(0, half), False)

    @pl.when(has_from)
    def _():
        halo.wait_recv()

    @pl.when(jnp.logical_not(has_from))
    def _():
        land[...] = jnp.zeros_like(land)

    for r in range(per_tile):
        rot[r, rows : rows + half] = land[...] if r == 0 else pltpu.roll(land[...], width * r, 1)
    build(steps, steps)

    units = g.shape[0] // SEGMENTS
    side = units // 2
    color_part = side // 2
    ring_part = color_part // 4
    small = ring_part // 4
    sems = iter(range(SEGMENTS * 54))
    ids = [[[next(sems) for _ in range(n)] for n in (8, 6, 6, 7, 7, 6, 6, 8)] for _ in range(SEGMENTS)]

    def ring(color, d, first):
        if (color == 0) == first:
            at = lax.rem(x + d, NX)
            return device(at, y, z, c), at
        at = lax.rem(y + d, NY)
        return device(x, at, z, c), at

    def send_to(src, dst, s, stage, n, dev):
        k = ids[s][stage][n]
        return remote(src, dst, ssend.at[k], srecv.at[k], dev)

    partner = device(x, y, z, 1 - c)
    plain = []
    stages = [[[] for _ in range(8)] for _ in range(SEGMENTS)]

    def go(s, stage, cp):
        cp.start()
        stages[s][stage].append(cp)
        plain.append(cp)

    far_first = (2, 1, 3)

    def cores(s):
        for n, d in enumerate(far_first + (0,)):
            for color in range(2):
                part_at = pl.ds(ring(color, d, True)[1] * ring_part, ring_part)
                first = s * units + (1 - c) * side + color * color_part
                at = pl.ds(first + ring(color, d, True)[1] * ring_part, ring_part)
                go(s, 0, send_to(g.at[at], rc.at[s, color, part_at], s, 0, 2 * n + color, partner))

    def ring_first(s):
        for n, d in enumerate(far_first + (0,)):
            for color in range(2):
                stages[s][0][2 * n + color].wait_recv()
                dev, spot = ring(color, d, True)
                part_at = pl.ds(spot * ring_part, ring_part)
                at = pl.ds(s * units + c * side + color * color_part + spot * ring_part, ring_part)
                h[s, color, part_at] = g[at] + rc[s, color, part_at]
                if d > 0:
                    go(s, 1, send_to(h.at[s, color, part_at], ra.at[s, color, d - 1],
                                     s, 1, 3 * color + d - 1, dev))

    def ring_second(s):
        for color in range(2):
            for cp in stages[s][1][color::2]:
                cp.wait_recv()
            _, spot = ring(color, 0, True)
            sa[s, color] = ((h[s, color, pl.ds(spot * ring_part, ring_part)] + ra[s, color, 0])
                            + (ra[s, color, 1] + ra[s, color, 2]))
            for d in far_first:
                dev, spot = ring(color, d, False)
                go(s, 2, send_to(sa.at[s, color, pl.ds(spot * small, small)],
                                 rb.at[s, color, d - 1], s, 2, 3 * color + d - 1, dev))

    size = 2 * small // OWNERS
    z_order = (4, 3, 5, 2, 6, 1, 7)
    to_z, from_z = [{} for _ in range(SEGMENTS)], [{} for _ in range(SEGMENTS)]
    mine = jnp.minimum(z, OWNERS - 1)

    def along_z(s):
        for color in range(2):
            for cp in stages[s][2][3 * color : 3 * color + 3]:
                cp.wait_recv()
            _, spot = ring(color, 0, False)
            ys[s, color * small : (color + 1) * small] = (
                (sa[s, color, pl.ds(spot * small, small)] + rb[s, color, 0])
                + (rb[s, color, 1] + rb[s, color, 2]))
        for d in z_order:
            dst = lax.rem(z + d, NZ)
            at = pl.ds(jnp.minimum(dst, OWNERS - 1) * size, size)
            cp = send_to(ys.at[s, at], rz.at[s, d - 1], s, 3, d - 1, device(x, y, dst, c))
            pl.when(dst < OWNERS)(cp.start)
            to_z[s][d] = cp

    def spot_of(s, p):
        color = p // (OWNERS // 2)
        chunk_at = jnp.where(color == 0, x * 4 + y, y * 4 + x)
        return (s * units + c * side + color * color_part + chunk_at * small
                + lax.rem(p, OWNERS // 2) * size)

    def back_z(s):
        at = pl.ds(spot_of(s, mine), size)

        @pl.when(z < OWNERS)
        def _():
            total = ys[s, pl.ds(mine * size, size)]
            for d in reversed(z_order):
                to_z[s][d].wait_recv()
                total = total + rz[s, d - 1]
            out_ref[at] = total

        for d in z_order:
            cp = send_to(out_ref.at[at], out_ref.at[at], s, 4, d - 1,
                         device(x, y, lax.rem(z + d, NZ), c))
            pl.when(z < OWNERS)(cp.start)
            from_z[s][d] = cp

    def back_second(s):
        for d in range(1, NZ):
            pl.when(lax.rem(z - d + NZ, NZ) < OWNERS)(from_z[s][d].wait_recv)
        for color in range(2):
            _, spot = ring(color, 0, True)
            _, sub = ring(color, 0, False)
            at = pl.ds(s * units + c * side + color * color_part + spot * ring_part + sub * small,
                       small)
            for d in far_first:
                dev, _ = ring(color, d, False)
                go(s, 5, send_to(out_ref.at[at], out_ref.at[at], s, 5, 3 * color + d - 1, dev))

    def back_first(s):
        for color in range(2):
            for cp in stages[s][5][3 * color : 3 * color + 3]:
                cp.wait_recv()
            _, spot = ring(color, 0, True)
            at = pl.ds(s * units + c * side + color * color_part + spot * ring_part, ring_part)
            for d in far_first:
                dev, _ = ring(color, d, True)
                go(s, 6, send_to(out_ref.at[at], out_ref.at[at], s, 6, 3 * color + d - 1, dev))

    def hand_over(s, color, d):
        _, spot = ring(color, (4 - d) % 4, True)
        at = pl.ds(s * units + c * side + color * color_part + spot * ring_part, ring_part)
        go(s, 7, send_to(out_ref.at[at], out_ref.at[at], s, 7, 4 * color + d, partner))

    def back_cores(s):
        for color in range(2):
            hand_over(s, color, 0)
        for d in (1, 3, 2):
            for color in range(2):
                stages[s][6][3 * color + far_first.index(d)].wait_recv()
                hand_over(s, color, d)

    def last(s):
        for cp in stages[s][7]:
            cp.wait_recv()

    cut = next(r for r in range(count) if 2 * first_block(r + 1, count) > first_block(count, count))
    late = slice(half, rows)

    def some(core, first, stop):
        @pl.when(c == core)
        def _():
            for i in range(first, stop):
                products(i, late, True)

    some(0, cut, count)
    some(1, 0, cut + 1)
    cores(0)
    some(0, 0, cut)
    some(1, cut + 1, count)
    chain = (ring_first, ring_second, along_z, back_z, back_second, back_first, back_cores, last)
    for slot in range(len(chain) + SEGMENTS - 1):
        for s in range(SEGMENTS):
            if 0 <= slot - s < len(chain):
                chain[slot - s](s)

    for ph in range(2):
        for cp in fars[ph] + nears[ph] + pairs[ph]:
            cp.wait_send()
    pl.when(has_to)(halo.wait_send)
    for cp in plain:
        cp.wait_send()
    for s in range(SEGMENTS):
        for d in range(1, NZ):
            pl.when(lax.rem(z + d, NZ) < OWNERS)(to_z[s][d].wait_send)
            pl.when(z < OWNERS)(from_z[s][d].wait_send)


def gram_blocks(signals, channel_node, lags):
    length, chans = signals.shape
    rows = length // NX
    size = lags.shape[0] * NODES
    count = size // NB
    blocks = count * (count + 1) // 2
    side = blocks * 16 // SEGMENTS // 2
    tiles = lambda *lead: pltpu.VMEM(lead + (8, NB), F32)
    quarters = pltpu.VMEM((2, 2, rows // 4, NODES), F32)
    S = SEGMENTS
    dma = pltpu.SemaphoreType.DMA
    total = pl.pallas_call(
        functools.partial(gram_body, lags.shape[0]),
        out_shape=jax.ShapeDtypeStruct((blocks * 16, 8, NB), F32),
        in_specs=[pl.BlockSpec(memory_space=pltpu.SMEM), pl.BlockSpec(memory_space=pl.ANY), VMEM],
        out_specs=VMEM,
        scratch_shapes=[
            pltpu.VMEM((length, chans), BF16), pltpu.VMEM((length, NODES), F32),
            quarters, quarters, quarters, quarters,
            pltpu.VMEM((rows, NODES), F32), pltpu.VMEM((MAXLAG, NODES), F32),
            pltpu.VMEM((NX, rows + MAXLAG, NODES), F32),
            pltpu.VMEM((rows, size), BF16), pltpu.VMEM((rows, size), BF16),
            tiles(blocks * 16), tiles(S, 2, side // 2), tiles(S, 2, side // 2),
            tiles(S, 2, 3, side // 8), tiles(S, 2, side // 8), tiles(S, 2, 3, side // 32),
            tiles(S, side // 16), tiles(S, NZ - 1, side // 16 // OWNERS),
            dma((8,)), dma((13,)), dma((13,)), dma((S * 54,)), dma((S * 54,)),
        ],
        compiler_params=pltpu.CompilerParams(
            collective_id=1, has_side_effects=True, vmem_limit_bytes=56 << 20),
    )(lags, signals, channel_node.reshape(1, chans))
    return total.reshape(blocks, NB, NB)


DOT = dict(precision=lax.Precision.HIGHEST, preferred_element_type=F32)


def lanes(x, c):
    return jnp.broadcast_to(x[:, c : c + 1], x.shape)


def subs(x, r):
    return jnp.broadcast_to(x[r : r + 1, :], x.shape)


def factor_block(rows):
    count = NB // 8
    lane = lax.broadcasted_iota(jnp.int32, (8, NB), 1)
    sub = lax.broadcasted_iota(jnp.int32, (8, NB), 0)
    rows = list(rows)
    upper, inv, merged = [], [], []
    cur = [lanes(rows[0], j) for j in range(8)]
    for p in range(count):
        r0 = 8 * p
        end = count // 2 if p < count // 2 else count
        if p == count // 2:
            above = jnp.concatenate(merged, axis=0)
            product = lax.dot_general(above, above, (((0,), (0,)), ((), ())), **DOT)
            for b in range(p, count):
                rows[b] = jnp.where(lane >= r0, rows[b], 0.0) - product[8 * b : 8 * b + 8]
            cur = [lanes(rows[p], r0 + j) for j in range(8)]
        raw = {b: [lanes(rows[b], r0 + j) for j in range(8)] for b in range(p + 1, end)}
        ahead = [lanes(rows[p + 1], r0 + 8 + j) for j in range(8)] if p + 1 < end else None
        here = jnp.logical_and(lane >= r0, lane < r0 + 8)
        top, low = rows[p], jnp.where(here, jnp.where(lane == sub + r0, 1.0, 0.0), rows[p])
        for b in range(p + 1, end):
            rows[b] = jnp.where(here, 0.0, rows[b])
        v, m, s, rinv = list(cur), [None] * 8, [[None] * 8 for _ in range(8)], [None] * 8
        diag = None
        for j in range(8):
            diag = v[j] if diag is None else jnp.where(sub >= j, v[j], diag)
            rinv[j] = 1.0 / subs(v[j], j)
            whole = v[j] * rinv[j]
            for k in range(j + 1, 8):
                s[j][k] = subs(v[j], k)
                if k == j + 1:
                    v[k] = v[k] - (v[j] * s[j][k]) * rinv[j]
                else:
                    v[k] = v[k] - whole * s[j][k]
            m[j] = jnp.where(sub > j, whole, 0.0)
        rs = lax.rsqrt(diag)
        ra = []
        for j in range(8):
            ra.append(subs(low, j))
            da = subs(top, j)
            low = low - m[j] * ra[j]
            top = top - m[j] * da
        for b in range(p + 1, end):
            u, mb = [], []
            for j in range(8):
                value = raw[b][j]
                for i in range(j):
                    value = value - mb[i] * s[i][j]
                u.append(value)
                mb.append(value * rinv[j])
            if b == p + 1:
                cur = []
                for i in range(8):
                    value = ahead[i]
                    for j in range(8):
                        value = value - mb[j] * subs(u[j], i)
                    cur.append(value)
            for j in range(8):
                rows[b] = rows[b] - mb[j] * ra[j]
        upper.append(jnp.where(lane >= sub + r0, top * rs, 0.0))
        inv.append(jnp.where(lane < r0 + 8, low * rs, 0.0))
        merged.append(jnp.where(lane < NB // 2, inv[-1], upper[-1]))
    return upper, inv


def factor_body(count, scale, g_hbm, out_hbm, g_ref, r_ref, w_ref, d_ref, sem):
    def fetch(k):
        at = pl.ds(first_block(k, count), count - k)
        return pltpu.make_async_copy(g_hbm.at[at], g_ref.at[at], sem.at[count + k])

    for k in range(count):
        fetch(k).start()
    r_ref[...] = jnp.zeros_like(r_ref)

    def leave(k):
        at = pl.ds(k * NB, NB)
        return pltpu.make_async_copy(r_ref.at[at], out_hbm.at[at], sem.at[k])

    def update(k):
        r0 = k * NB
        first = first_block(k, count)
        fetch(k).wait()
        for j in range(k, count):
            r_ref[r0 : r0 + NB, j * NB : (j + 1) * NB] = g_ref[first + j - k] * scale
        if k > 0:
            r_ref[r0 : r0 + NB, r0:] -= lax.dot_general(
                r_ref[0:r0, r0 : r0 + NB], r_ref[0:r0, r0:], (((0,), (0,)), ((), ())), **DOT
            )
        d_ref[...] = r_ref[r0 : r0 + NB, r0 : r0 + NB]

    def panel(k):
        r0 = k * NB
        r_ref[r0 : r0 + NB, r0 : r0 + NB] = d_ref[...]
        if k + 1 < count:
            r_ref[r0 : r0 + NB, r0 + NB :] = lax.dot_general(
                w_ref[...], r_ref[r0 : r0 + NB, r0 + NB :], (((1,), (0,)), ((), ())), **DOT
            )
        leave(k).start()

    def step(k, _):
        lax.switch(k, [functools.partial(update, i) for i in range(count)])
        rows, inv = factor_block([d_ref[8 * i : 8 * i + 8, :] for i in range(NB // 8)])
        for i in range(NB // 8):
            d_ref[8 * i : 8 * i + 8, :] = rows[i]
            w_ref[8 * i : 8 * i + 8, :] = inv[i]
        lax.switch(k, [functools.partial(panel, i) for i in range(count)])
        return 0

    lax.fori_loop(0, count, step, 0)
    for k in range(count):
        leave(k).wait()


def upper_factor(blocks, count, scale):
    size = count * NB
    return pl.pallas_call(
        functools.partial(factor_body, count, scale),
        out_shape=jax.ShapeDtypeStruct((size, size), F32),
        in_specs=[pl.BlockSpec(memory_space=pltpu.HBM)],
        out_specs=pl.BlockSpec(memory_space=pltpu.HBM),
        scratch_shapes=[pltpu.VMEM(blocks.shape, F32), pltpu.VMEM((size, size), F32), pltpu.VMEM((NB, NB), F32),
                        pltpu.VMEM((NB, NB), F32), pltpu.SemaphoreType.DMA((2 * count,))],
        compiler_params=pltpu.CompilerParams(vmem_limit_bytes=63_000_000),
    )(blocks)


def on_device(signals, channel_node, lag_offsets):
    total_rows = signals.shape[0] * lax.axis_size("tm")
    count = lag_offsets.shape[0] * NODES // NB
    blocks = gram_blocks(signals, channel_node, lag_offsets)
    return upper_factor(blocks, count, 1.0 / total_rows)


def solution(mesh):
    in_specs = (P("tm", "chan"), P("chan"), P())
    out_specs = P()
    return jax.shard_map(
        on_device, mesh=mesh, in_specs=in_specs, out_specs=out_specs, check_vma=False
    )
```

```python
import functools
import math

import jax
import jax.numpy as jnp
from jax import lax
from jax.experimental import pallas as pl
from jax.experimental.pallas import tpu as pltpu
from jax.sharding import PartitionSpec as P

NODES = 128
CH = 2048
MAXLAG = 512
F32 = jnp.float32
BF16 = jnp.bfloat16
MESH = pl.DeviceIdType.MESH
VMEM = pl.BlockSpec(memory_space=pltpu.VMEM)
NB = 128
NX, NY, NZ = 4, 4, 8
SEGMENTS = 1
OWNERS = 6


def first_block(i, count):
    return i * count - i * (i - 1) // 2


def device(x, y, z, c):
    return {"tm": (y * NZ + z) * 2 + c, "chan": x}


def remote(src, dst, send, recv, target):
    return pltpu.make_async_remote_copy(
        src_ref=src, dst_ref=dst, send_sem=send, recv_sem=recv,
        device_id=target, device_id_type=MESH,
    )


def gram_body(lag_count, lags_ref, s_hbm, node_ref, out_ref,
              sig, part, far, near, pair, fwd, own, land, rot, hi, lo,
              g, rc, h, ra, sa, rb, ys, rz, load, send, recv, ssend, srecv):
    x, t = lax.axis_index("chan"), lax.axis_index("tm")
    y, z, c = t // (NZ * 2), lax.rem(t // 2, NZ), lax.rem(t, 2)
    rows = own.shape[0]
    half, quarter = rows // 2, rows // 4

    def chunk_of(at):
        return jnp.where(c == 0, at, 3 - at)

    others = (x + 1 - 2 * lax.rem(x, 2), 3 - x)
    opposite = lax.rem(x + 2, 4)
    loads = []
    for ph in range(2):
        for i, at in enumerate((opposite, others[0], others[1], x)):
            rows_at = pl.ds(pl.multiple_of(chunk_of(at) * rows + ph * half, half), half)
            cp = pltpu.make_async_copy(s_hbm.at[rows_at], sig.at[rows_at], load.at[ph * 4 + i])
            cp.start()
            loads.append((cp, rows_at))
    b = chunk_of(x)
    has_to = jnp.logical_or(b > 0, t > 0)
    has_from = jnp.logical_or(b < 3, t < 2 * NY * NZ - 1)
    step = 1 - 2 * c
    to = {"tm": jnp.where(b > 0, t, jnp.maximum(t - 1, 0)), "chan": jnp.where(b > 0, x - step, x)}
    source = {"tm": jnp.where(b < 3, t, jnp.minimum(t + 1, 2 * NY * NZ - 1)),
              "chan": jnp.where(b < 3, x + step, x)}
    barrier = pltpu.get_barrier_semaphore()
    peers = [device(x, y, z, 1 - c)]
    peers += [device(lax.rem(x + d, NX), y, z, c) for d in range(1, NX)]
    peers += [device(x, lax.rem(y + d, NY), z, c) for d in range(1, NY)]
    peers += [device(x, y, lax.rem(z + d, NZ), c) for d in range(1, NZ)]
    for dev in peers:
        pl.semaphore_signal(barrier, inc=1, device_id=dev, device_id_type=MESH)

    @pl.when(has_to)
    def _():
        pl.semaphore_signal(barrier, inc=1, device_id=to, device_id_type=MESH)

    @pl.when(has_from)
    def _():
        pl.semaphore_signal(barrier, inc=1, device_id=source, device_id_type=MESH)

    scale = 1.0 / math.sqrt(CH // NODES)
    chans = node_ref.shape[1]
    match = lax.broadcasted_iota(jnp.int32, (NODES, chans), 0) == node_ref[...]
    onehot = jnp.where(match, scale, 0.0).astype(BF16)

    def sums(ph, i):
        cp, rows_at = loads[ph * 4 + i]
        cp.wait()
        part[rows_at] = lax.dot_general(sig[rows_at], onehot, (((1,), (1,)), ((), ())),
                                        preferred_element_type=F32)

    def piece(at, ph, color):
        first = chunk_of(at) * rows + ph * half + color * quarter
        return pl.ds(pl.multiple_of(first, quarter), quarter)

    link = tuple(device(at, y, z, c) for at in others)

    def copy(src, dst, kind, ph, color, dev):
        s = (kind * 2 + ph) * 2 + color
        return remote(src, dst, send.at[s], recv.at[s], dev)

    sums(0, 0)
    pl.semaphore_wait(barrier, len(peers) + has_to.astype(jnp.int32) + has_from.astype(jnp.int32))
    fars, nears, pairs = [], [], []
    for ph in range(2):
        fars.append([copy(part.at[piece(opposite, ph, k)], far.at[ph, k], 0, ph, k, link[k])
                     for k in range(2)])
        nears.append([copy(part.at[piece(others[k], ph, k)], near.at[ph, k], 1, ph, k, link[k])
                      for k in range(2)])
        pairs.append([copy(fwd.at[ph, k], pair.at[ph, k], 2, ph, k, link[1 - k])
                      for k in range(2)])

    def forward(ph):
        for k in range(2):
            fars[ph][k].wait_recv()
            fwd[ph, k] = part[piece(others[1 - k], ph, k)] + far[ph, k]
            pairs[ph][k].start()

    def finish(ph):
        for k in range(2):
            nears[ph][k].wait_recv()
            pairs[ph][k].wait_recv()
            at = ph * half + k * quarter
            own[at : at + quarter] = part[piece(x, ph, k)] + near[ph, k] + pair[ph, k]

    for cp in fars[0]:
        cp.start()
    sums(0, 1)
    nears[0][0].start()
    sums(0, 2)
    nears[0][1].start()
    for i in range(4):
        sums(1, i)
    sums(0, 3)
    forward(0)
    for cp in fars[1] + nears[1]:
        cp.start()
    finish(0)
    forward(1)
    halo = remote(own.at[0:half], land, send.at[12], recv.at[12], to)
    pl.when(has_to)(halo.start)
    finish(1)

    width = NODES // NX
    per_tile = NB // width
    count = lag_count * NODES // NB
    chunk = 128
    lane_group = lax.broadcasted_iota(jnp.int32, (chunk, NB), 1) // width

    def build(first_step, steps):
        for tile in range(count):
            group, top = tile // (count // NX), tile % (count // NX)

            def fill(i, _):
                value = None
                for m in range(per_tile):
                    first = lags_ref[top * per_tile + m] + i * chunk
                    got = rot[(m - group) % per_tile, pl.ds(first, chunk), :]
                    value = got if value is None else jnp.where(lane_group == m, got, value)
                high = value.astype(BF16)
                at = pl.ds(pl.multiple_of(i * chunk, chunk), chunk)
                hi[at, tile * NB : (tile + 1) * NB] = high
                lo[at, tile * NB : (tile + 1) * NB] = (value - high.astype(F32)).astype(BF16)
                return 0

            lax.fori_loop(first_step, first_step + steps, fill, 0)

    dims = (((0,), (0,)), ((), ()))

    def products(i, at, add):
        a, d = hi[at, i * NB : (i + 1) * NB], lo[at, i * NB : (i + 1) * NB]
        value = lax.dot_general(a, lo[at, i * NB :], dims, preferred_element_type=F32)
        value += lax.dot_general(d, hi[at, i * NB :], dims, preferred_element_type=F32)
        value += lax.dot_general(a, hi[at, i * NB :], dims, preferred_element_type=F32)
        square = lax.dot_general(d, d, dims, preferred_element_type=F32)
        for j in range(i, count):
            spot = 16 * (first_block(i, count) + j - i)
            block = value[:, (j - i) * NB : (j - i + 1) * NB]
            block = (block + square if j == i else block).reshape(16, 8, NB)
            g[spot : spot + 16] = g[spot : spot + 16] + block if add else block

    for r in range(per_tile):
        rot[r, 0:rows] = own[...] if r == 0 else pltpu.roll(own[...], width * r, 1)
    steps = half // chunk
    build(0, steps)
    for i in range(count):
        products(i, slice(0, half), False)

    @pl.when(has_from)
    def _():
        halo.wait_recv()

    @pl.when(jnp.logical_not(has_from))
    def _():
        land[...] = jnp.zeros_like(land)

    for r in range(per_tile):
        rot[r, rows : rows + half] = land[...] if r == 0 else pltpu.roll(land[...], width * r, 1)
    build(steps, steps)

    units = g.shape[0] // SEGMENTS
    side = units // 2
    color_part = side // 2
    ring_part = color_part // 4
    small = ring_part // 4
    sems = iter(range(SEGMENTS * 54))
    ids = [[[next(sems) for _ in range(n)] for n in (8, 6, 6, 7, 7, 6, 6, 8)] for _ in range(SEGMENTS)]

    def ring(color, d, first):
        if (color == 0) == first:
            at = lax.rem(x + d, NX)
            return device(at, y, z, c), at
        at = lax.rem(y + d, NY)
        return device(x, at, z, c), at

    def send_to(src, dst, s, stage, n, dev):
        k = ids[s][stage][n]
        return remote(src, dst, ssend.at[k], srecv.at[k], dev)

    partner = device(x, y, z, 1 - c)
    plain = []
    stages = [[[] for _ in range(8)] for _ in range(SEGMENTS)]

    def go(s, stage, cp):
        cp.start()
        stages[s][stage].append(cp)
        plain.append(cp)

    far_first = (2, 1, 3)

    def cores(s):
        for n, d in enumerate(far_first + (0,)):
            for color in range(2):
                part_at = pl.ds(ring(color, d, True)[1] * ring_part, ring_part)
                first = s * units + (1 - c) * side + color * color_part
                at = pl.ds(first + ring(color, d, True)[1] * ring_part, ring_part)
                go(s, 0, send_to(g.at[at], rc.at[s, color, part_at], s, 0, 2 * n + color, partner))

    def ring_first(s):
        for n, d in enumerate(far_first + (0,)):
            for color in range(2):
                stages[s][0][2 * n + color].wait_recv()
                dev, spot = ring(color, d, True)
                part_at = pl.ds(spot * ring_part, ring_part)
                at = pl.ds(s * units + c * side + color * color_part + spot * ring_part, ring_part)
                h[s, color, part_at] = g[at] + rc[s, color, part_at]
                if d > 0:
                    go(s, 1, send_to(h.at[s, color, part_at], ra.at[s, color, d - 1],
                                     s, 1, 3 * color + d - 1, dev))

    def ring_second(s):
        for color in range(2):
            for cp in stages[s][1][color::2]:
                cp.wait_recv()
            _, spot = ring(color, 0, True)
            sa[s, color] = ((h[s, color, pl.ds(spot * ring_part, ring_part)] + ra[s, color, 0])
                            + (ra[s, color, 1] + ra[s, color, 2]))
            for d in far_first:
                dev, spot = ring(color, d, False)
                go(s, 2, send_to(sa.at[s, color, pl.ds(spot * small, small)],
                                 rb.at[s, color, d - 1], s, 2, 3 * color + d - 1, dev))

    size = 2 * small // OWNERS
    z_order = (4, 3, 5, 2, 6, 1, 7)
    to_z, from_z = [{} for _ in range(SEGMENTS)], [{} for _ in range(SEGMENTS)]
    mine = jnp.minimum(z, OWNERS - 1)

    def along_z(s):
        for color in range(2):
            for cp in stages[s][2][3 * color : 3 * color + 3]:
                cp.wait_recv()
            _, spot = ring(color, 0, False)
            ys[s, color * small : (color + 1) * small] = (
                (sa[s, color, pl.ds(spot * small, small)] + rb[s, color, 0])
                + (rb[s, color, 1] + rb[s, color, 2]))
        for d in z_order:
            dst = lax.rem(z + d, NZ)
            at = pl.ds(jnp.minimum(dst, OWNERS - 1) * size, size)
            cp = send_to(ys.at[s, at], rz.at[s, d - 1], s, 3, d - 1, device(x, y, dst, c))
            pl.when(dst < OWNERS)(cp.start)
            to_z[s][d] = cp

    def spot_of(s, p):
        color = p // (OWNERS // 2)
        chunk_at = jnp.where(color == 0, x * 4 + y, y * 4 + x)
        return (s * units + c * side + color * color_part + chunk_at * small
                + lax.rem(p, OWNERS // 2) * size)

    def back_z(s):
        at = pl.ds(spot_of(s, mine), size)

        @pl.when(z < OWNERS)
        def _():
            total = ys[s, pl.ds(mine * size, size)]
            for d in reversed(z_order):
                to_z[s][d].wait_recv()
                total = total + rz[s, d - 1]
            out_ref[at] = total

        for d in z_order:
            cp = send_to(out_ref.at[at], out_ref.at[at], s, 4, d - 1,
                         device(x, y, lax.rem(z + d, NZ), c))
            pl.when(z < OWNERS)(cp.start)
            from_z[s][d] = cp

    def back_second(s):
        for d in range(1, NZ):
            pl.when(lax.rem(z - d + NZ, NZ) < OWNERS)(from_z[s][d].wait_recv)
        for color in range(2):
            _, spot = ring(color, 0, True)
            _, sub = ring(color, 0, False)
            at = pl.ds(s * units + c * side + color * color_part + spot * ring_part + sub * small,
                       small)
            for d in far_first:
                dev, _ = ring(color, d, False)
                go(s, 5, send_to(out_ref.at[at], out_ref.at[at], s, 5, 3 * color + d - 1, dev))

    def back_first(s):
        for color in range(2):
            for cp in stages[s][5][3 * color : 3 * color + 3]:
                cp.wait_recv()
            _, spot = ring(color, 0, True)
            at = pl.ds(s * units + c * side + color * color_part + spot * ring_part, ring_part)
            for d in far_first:
                dev, _ = ring(color, d, True)
                go(s, 6, send_to(out_ref.at[at], out_ref.at[at], s, 6, 3 * color + d - 1, dev))

    def hand_over(s, color, d):
        _, spot = ring(color, (4 - d) % 4, True)
        at = pl.ds(s * units + c * side + color * color_part + spot * ring_part, ring_part)
        go(s, 7, send_to(out_ref.at[at], out_ref.at[at], s, 7, 4 * color + d, partner))

    def back_cores(s):
        for color in range(2):
            hand_over(s, color, 0)
        for d in (1, 3, 2):
            for color in range(2):
                stages[s][6][3 * color + far_first.index(d)].wait_recv()
                hand_over(s, color, d)

    def last(s):
        for cp in stages[s][7]:
            cp.wait_recv()

    cut = next(r for r in range(count) if 2 * first_block(r + 1, count) > first_block(count, count))
    late = slice(half, rows)

    def some(core, first, stop):
        @pl.when(c == core)
        def _():
            for i in range(first, stop):
                products(i, late, True)

    some(0, cut, count)
    some(1, 0, cut + 1)
    cores(0)
    some(0, 0, cut)
    some(1, cut + 1, count)
    chain = (ring_first, ring_second, along_z, back_z, back_second, back_first, back_cores, last)
    for slot in range(len(chain) + SEGMENTS - 1):
        for s in range(SEGMENTS):
            if 0 <= slot - s < len(chain):
                chain[slot - s](s)

    for ph in range(2):
        for cp in fars[ph] + nears[ph] + pairs[ph]:
            cp.wait_send()
    pl.when(has_to)(halo.wait_send)
    for cp in plain:
        cp.wait_send()
    for s in range(SEGMENTS):
        for d in range(1, NZ):
            pl.when(lax.rem(z + d, NZ) < OWNERS)(to_z[s][d].wait_send)
            pl.when(z < OWNERS)(from_z[s][d].wait_send)


def gram_blocks(signals, channel_node, lags):
    length, chans = signals.shape
    rows = length // NX
    size = lags.shape[0] * NODES
    count = size // NB
    blocks = count * (count + 1) // 2
    side = blocks * 16 // SEGMENTS // 2
    tiles = lambda *lead: pltpu.VMEM(lead + (8, NB), F32)
    quarters = pltpu.VMEM((2, 2, rows // 4, NODES), F32)
    S = SEGMENTS
    dma = pltpu.SemaphoreType.DMA
    total = pl.pallas_call(
        functools.partial(gram_body, lags.shape[0]),
        out_shape=jax.ShapeDtypeStruct((blocks * 16, 8, NB), F32),
        in_specs=[pl.BlockSpec(memory_space=pltpu.SMEM), pl.BlockSpec(memory_space=pl.ANY), VMEM],
        out_specs=VMEM,
        scratch_shapes=[
            pltpu.VMEM((length, chans), BF16), pltpu.VMEM((length, NODES), F32),
            quarters, quarters, quarters, quarters,
            pltpu.VMEM((rows, NODES), F32), pltpu.VMEM((MAXLAG, NODES), F32),
            pltpu.VMEM((NX, rows + MAXLAG, NODES), F32),
            pltpu.VMEM((rows, size), BF16), pltpu.VMEM((rows, size), BF16),
            tiles(blocks * 16), tiles(S, 2, side // 2), tiles(S, 2, side // 2),
            tiles(S, 2, 3, side // 8), tiles(S, 2, side // 8), tiles(S, 2, 3, side // 32),
            tiles(S, side // 16), tiles(S, NZ - 1, side // 16 // OWNERS),
            dma((8,)), dma((13,)), dma((13,)), dma((S * 54,)), dma((S * 54,)),
        ],
        compiler_params=pltpu.CompilerParams(
            collective_id=1, has_side_effects=True, vmem_limit_bytes=56 << 20),
    )(lags, signals, channel_node.reshape(1, chans))
    return total.reshape(blocks, NB, NB)


DOT = dict(precision=lax.Precision.HIGHEST, preferred_element_type=F32)


def lanes(x, c):
    return jnp.broadcast_to(x[:, c : c + 1], x.shape)


def subs(x, r):
    return jnp.broadcast_to(x[r : r + 1, :], x.shape)


def factor_block(rows):
    count = NB // 8
    lane = lax.broadcasted_iota(jnp.int32, (8, NB), 1)
    sub = lax.broadcasted_iota(jnp.int32, (8, NB), 0)
    rows = list(rows)
    upper, inv, merged = [], [], []
    cur = [lanes(rows[0], j) for j in range(8)]
    for p in range(count):
        r0 = 8 * p
        end = count // 2 if p < count // 2 else count
        if p == count // 2:
            above = jnp.concatenate(merged, axis=0)
            product = lax.dot_general(above, above, (((0,), (0,)), ((), ())), **DOT)
            for b in range(p, count):
                rows[b] = jnp.where(lane >= r0, rows[b], 0.0) - product[8 * b : 8 * b + 8]
            cur = [lanes(rows[p], r0 + j) for j in range(8)]
        raw = {b: [lanes(rows[b], r0 + j) for j in range(8)] for b in range(p + 1, end)}
        ahead = [lanes(rows[p + 1], r0 + 8 + j) for j in range(8)] if p + 1 < end else None
        here = jnp.logical_and(lane >= r0, lane < r0 + 8)
        top, low = rows[p], jnp.where(here, jnp.where(lane == sub + r0, 1.0, 0.0), rows[p])
        for b in range(p + 1, end):
            rows[b] = jnp.where(here, 0.0, rows[b])
        v, m, s, rinv = list(cur), [None] * 8, [[None] * 8 for _ in range(8)], [None] * 8
        diag = None
        for j in range(8):
            diag = v[j] if diag is None else jnp.where(sub >= j, v[j], diag)
            rinv[j] = 1.0 / subs(v[j], j)
            whole = v[j] * rinv[j]
            for k in range(j + 1, 8):
                s[j][k] = subs(v[j], k)
                if k == j + 1:
                    v[k] = v[k] - (v[j] * s[j][k]) * rinv[j]
                else:
                    v[k] = v[k] - whole * s[j][k]
            m[j] = jnp.where(sub > j, whole, 0.0)
        rs = lax.rsqrt(diag)
        ra = []
        for j in range(8):
            ra.append(subs(low, j))
            da = subs(top, j)
            low = low - m[j] * ra[j]
            top = top - m[j] * da
        for b in range(p + 1, end):
            u, mb = [], []
            for j in range(8):
                value = raw[b][j]
                for i in range(j):
                    value = value - mb[i] * s[i][j]
                u.append(value)
                mb.append(value * rinv[j])
            if b == p + 1:
                cur = []
                for i in range(8):
                    value = ahead[i]
                    for j in range(8):
                        value = value - mb[j] * subs(u[j], i)
                    cur.append(value)
            for j in range(8):
                rows[b] = rows[b] - mb[j] * ra[j]
        upper.append(jnp.where(lane >= sub + r0, top * rs, 0.0))
        inv.append(jnp.where(lane < r0 + 8, low * rs, 0.0))
        merged.append(jnp.where(lane < NB // 2, inv[-1], upper[-1]))
    return upper, inv


def factor_body(count, scale, g_hbm, out_hbm, g_ref, r_ref, w_ref, d_ref, sem):
    def fetch(k):
        at = pl.ds(first_block(k, count), count - k)
        return pltpu.make_async_copy(g_hbm.at[at], g_ref.at[at], sem.at[count + k])

    for k in range(count):
        fetch(k).start()
    r_ref[...] = jnp.zeros_like(r_ref)

    def leave(k):
        at = pl.ds(k * NB, NB)
        return pltpu.make_async_copy(r_ref.at[at], out_hbm.at[at], sem.at[k])

    def take(k, less):
        fetch(k).wait()
        for j in range(k, count):
            value = g_ref[first_block(k, count) + j - k] * scale
            if less is not None:
                value = value - less[:, (j - k) * NB : (j - k + 1) * NB]
            r_ref[k * NB : (k + 1) * NB, j * NB : (j + 1) * NB] = value

    def update(k):
        r0, r1 = k * NB, (k + 1) * NB
        if k % 2 == 0:
            less = [None, None]
            if k > 0:
                both = lax.dot_general(r_ref[0:r0, r0 : r1 + NB], r_ref[0:r0, r0:],
                                       (((0,), (0,)), ((), ())), **DOT)
                less = [both[:NB], both[NB:, NB:]]
            take(k, less[0])
            take(k + 1, less[1])
        else:
            r_ref[r0:r1, r0:] -= lax.dot_general(
                r_ref[r0 - NB : r0, r0:r1], r_ref[r0 - NB : r0, r0:],
                (((0,), (0,)), ((), ())), **DOT)
        d_ref[...] = r_ref[r0:r1, r0:r1]

    def panel(k):
        r0 = k * NB
        r_ref[r0 : r0 + NB, r0 : r0 + NB] = d_ref[...]
        if k + 1 < count:
            r_ref[r0 : r0 + NB, r0 + NB :] = lax.dot_general(
                w_ref[...], r_ref[r0 : r0 + NB, r0 + NB :], (((1,), (0,)), ((), ())), **DOT
            )
        leave(k).start()

    def step(k, _):
        lax.switch(k, [functools.partial(update, i) for i in range(count)])
        rows, inv = factor_block([d_ref[8 * i : 8 * i + 8, :] for i in range(NB // 8)])
        for i in range(NB // 8):
            d_ref[8 * i : 8 * i + 8, :] = rows[i]
            w_ref[8 * i : 8 * i + 8, :] = inv[i]
        lax.switch(k, [functools.partial(panel, i) for i in range(count)])
        return 0

    lax.fori_loop(0, count, step, 0)
    for k in range(count):
        leave(k).wait()


def upper_factor(blocks, count, scale):
    size = count * NB
    return pl.pallas_call(
        functools.partial(factor_body, count, scale),
        out_shape=jax.ShapeDtypeStruct((size, size), F32),
        in_specs=[pl.BlockSpec(memory_space=pltpu.HBM)],
        out_specs=pl.BlockSpec(memory_space=pltpu.HBM),
        scratch_shapes=[pltpu.VMEM(blocks.shape, F32), pltpu.VMEM((size, size), F32), pltpu.VMEM((NB, NB), F32),
                        pltpu.VMEM((NB, NB), F32), pltpu.SemaphoreType.DMA((2 * count,))],
        compiler_params=pltpu.CompilerParams(vmem_limit_bytes=63_000_000),
    )(blocks)


def on_device(signals, channel_node, lag_offsets):
    total_rows = signals.shape[0] * lax.axis_size("tm")
    count = lag_offsets.shape[0] * NODES // NB
    blocks = gram_blocks(signals, channel_node, lag_offsets)
    return upper_factor(blocks, count, 1.0 / total_rows)


def solution(mesh):
    in_specs = (P("tm", "chan"), P("chan"), P())
    out_specs = P()
    return jax.shard_map(
        on_device, mesh=mesh, in_specs=in_specs, out_specs=out_specs, check_vma=False
    )
```

```python
import functools
import math

import jax
import jax.numpy as jnp
from jax import lax
from jax.experimental import pallas as pl
from jax.experimental.pallas import tpu as pltpu
from jax.sharding import PartitionSpec as P

NODES = 128
CH = 2048
MAXLAG = 512
F32 = jnp.float32
BF16 = jnp.bfloat16
MESH = pl.DeviceIdType.MESH
VMEM = pl.BlockSpec(memory_space=pltpu.VMEM)
NB = 128
NX, NY, NZ = 4, 4, 8
SEGMENTS = 1
OWNERS = 6


def first_block(i, count):
    return i * count - i * (i - 1) // 2


def device(x, y, z, c):
    return {"tm": (y * NZ + z) * 2 + c, "chan": x}


def remote(src, dst, send, recv, target):
    return pltpu.make_async_remote_copy(
        src_ref=src, dst_ref=dst, send_sem=send, recv_sem=recv,
        device_id=target, device_id_type=MESH,
    )


def gram_body(lag_count, lags_ref, s_hbm, node_ref, out_hbm,
              sig, part, far, near, pair, fwd, own, land, rot, hi, lo,
              g, rc, h, ra, sa, rb, ys, rz, out_ref, load, send, recv, ssend, srecv, leaves):
    x, t = lax.axis_index("chan"), lax.axis_index("tm")
    y, z, c = t // (NZ * 2), lax.rem(t // 2, NZ), lax.rem(t, 2)
    rows = own.shape[0]
    half, quarter = rows // 2, rows // 4

    def chunk_of(at):
        return jnp.where(c == 0, at, 3 - at)

    others = (x + 1 - 2 * lax.rem(x, 2), 3 - x)
    opposite = lax.rem(x + 2, 4)
    loads = []
    for ph in range(2):
        for i, at in enumerate((opposite, others[0], others[1], x)):
            rows_at = pl.ds(pl.multiple_of(chunk_of(at) * rows + ph * half, half), half)
            cp = pltpu.make_async_copy(s_hbm.at[rows_at], sig.at[rows_at], load.at[ph * 4 + i])
            cp.start()
            loads.append((cp, rows_at))
    b = chunk_of(x)
    has_to = jnp.logical_or(b > 0, t > 0)
    has_from = jnp.logical_or(b < 3, t < 2 * NY * NZ - 1)
    step = 1 - 2 * c
    to = {"tm": jnp.where(b > 0, t, jnp.maximum(t - 1, 0)), "chan": jnp.where(b > 0, x - step, x)}
    source = {"tm": jnp.where(b < 3, t, jnp.minimum(t + 1, 2 * NY * NZ - 1)),
              "chan": jnp.where(b < 3, x + step, x)}
    barrier = pltpu.get_barrier_semaphore()
    peers = [device(x, y, z, 1 - c)]
    peers += [device(lax.rem(x + d, NX), y, z, c) for d in range(1, NX)]
    peers += [device(x, lax.rem(y + d, NY), z, c) for d in range(1, NY)]
    peers += [device(x, y, lax.rem(z + d, NZ), c) for d in range(1, NZ)]
    for dev in peers:
        pl.semaphore_signal(barrier, inc=1, device_id=dev, device_id_type=MESH)

    @pl.when(has_to)
    def _():
        pl.semaphore_signal(barrier, inc=1, device_id=to, device_id_type=MESH)

    @pl.when(has_from)
    def _():
        pl.semaphore_signal(barrier, inc=1, device_id=source, device_id_type=MESH)

    scale = 1.0 / math.sqrt(CH // NODES)
    chans = node_ref.shape[1]
    match = lax.broadcasted_iota(jnp.int32, (NODES, chans), 0) == node_ref[...]
    onehot = jnp.where(match, scale, 0.0).astype(BF16)

    def sums(ph, i):
        cp, rows_at = loads[ph * 4 + i]
        cp.wait()
        part[rows_at] = lax.dot_general(sig[rows_at], onehot, (((1,), (1,)), ((), ())),
                                        preferred_element_type=F32)

    def piece(at, ph, color):
        first = chunk_of(at) * rows + ph * half + color * quarter
        return pl.ds(pl.multiple_of(first, quarter), quarter)

    link = tuple(device(at, y, z, c) for at in others)

    def copy(src, dst, kind, ph, color, dev):
        s = (kind * 2 + ph) * 2 + color
        return remote(src, dst, send.at[s], recv.at[s], dev)

    sums(0, 0)
    pl.semaphore_wait(barrier, len(peers) + has_to.astype(jnp.int32) + has_from.astype(jnp.int32))
    fars, nears, pairs = [], [], []
    for ph in range(2):
        fars.append([copy(part.at[piece(opposite, ph, k)], far.at[ph, k], 0, ph, k, link[k])
                     for k in range(2)])
        nears.append([copy(part.at[piece(others[k], ph, k)], near.at[ph, k], 1, ph, k, link[k])
                      for k in range(2)])
        pairs.append([copy(fwd.at[ph, k], pair.at[ph, k], 2, ph, k, link[1 - k])
                      for k in range(2)])

    def forward(ph):
        for k in range(2):
            fars[ph][k].wait_recv()
            fwd[ph, k] = part[piece(others[1 - k], ph, k)] + far[ph, k]
            pairs[ph][k].start()

    def finish(ph):
        for k in range(2):
            nears[ph][k].wait_recv()
            pairs[ph][k].wait_recv()
            at = ph * half + k * quarter
            own[at : at + quarter] = part[piece(x, ph, k)] + near[ph, k] + pair[ph, k]

    for cp in fars[0]:
        cp.start()
    sums(0, 1)
    nears[0][0].start()
    sums(0, 2)
    nears[0][1].start()
    for i in range(4):
        sums(1, i)
    sums(0, 3)
    forward(0)
    for cp in fars[1] + nears[1]:
        cp.start()
    finish(0)
    forward(1)
    halo = remote(own.at[0:half], land, send.at[12], recv.at[12], to)
    pl.when(has_to)(halo.start)
    finish(1)

    width = NODES // NX
    per_tile = NB // width
    count = lag_count * NODES // NB
    chunk = 128
    lane_group = lax.broadcasted_iota(jnp.int32, (chunk, NB), 1) // width

    def build(first_step, steps):
        for tile in range(count):
            group, top = tile // (count // NX), tile % (count // NX)

            def fill(i, _):
                value = None
                for m in range(per_tile):
                    first = lags_ref[top * per_tile + m] + i * chunk
                    got = rot[(m - group) % per_tile, pl.ds(first, chunk), :]
                    value = got if value is None else jnp.where(lane_group == m, got, value)
                high = value.astype(BF16)
                at = pl.ds(pl.multiple_of(i * chunk, chunk), chunk)
                hi[at, tile * NB : (tile + 1) * NB] = high
                lo[at, tile * NB : (tile + 1) * NB] = (value - high.astype(F32)).astype(BF16)
                return 0

            lax.fori_loop(first_step, first_step + steps, fill, 0)

    dims = (((0,), (0,)), ((), ()))

    def products(i, at, add):
        a, d = hi[at, i * NB : (i + 1) * NB], lo[at, i * NB : (i + 1) * NB]
        value = lax.dot_general(a, lo[at, i * NB :], dims, preferred_element_type=F32)
        value += lax.dot_general(d, hi[at, i * NB :], dims, preferred_element_type=F32)
        value += lax.dot_general(a, hi[at, i * NB :], dims, preferred_element_type=F32)
        square = lax.dot_general(d, d, dims, preferred_element_type=F32)
        for j in range(i, count):
            spot = 16 * (first_block(i, count) + j - i)
            block = value[:, (j - i) * NB : (j - i + 1) * NB]
            block = (block + square if j == i else block).reshape(16, 8, NB)
            g[spot : spot + 16] = g[spot : spot + 16] + block if add else block

    for r in range(per_tile):
        rot[r, 0:rows] = own[...] if r == 0 else pltpu.roll(own[...], width * r, 1)
    steps = half // chunk
    build(0, steps)
    for i in range(count):
        products(i, slice(0, half), False)

    @pl.when(has_from)
    def _():
        halo.wait_recv()

    @pl.when(jnp.logical_not(has_from))
    def _():
        land[...] = jnp.zeros_like(land)

    for r in range(per_tile):
        rot[r, rows : rows + half] = land[...] if r == 0 else pltpu.roll(land[...], width * r, 1)
    build(steps, steps)

    units = g.shape[0] // SEGMENTS
    side = units // 2
    color_part = side // 2
    ring_part = color_part // 4
    small = ring_part // 4
    sems = iter(range(SEGMENTS * 54))
    ids = [[[next(sems) for _ in range(n)] for n in (8, 6, 6, 7, 7, 6, 6, 8)] for _ in range(SEGMENTS)]

    def ring(color, d, first):
        if (color == 0) == first:
            at = lax.rem(x + d, NX)
            return device(at, y, z, c), at
        at = lax.rem(y + d, NY)
        return device(x, at, z, c), at

    def send_to(src, dst, s, stage, n, dev):
        k = ids[s][stage][n]
        return remote(src, dst, ssend.at[k], srecv.at[k], dev)

    partner = device(x, y, z, 1 - c)
    plain = []
    stages = [[[] for _ in range(8)] for _ in range(SEGMENTS)]

    def go(s, stage, cp):
        cp.start()
        stages[s][stage].append(cp)
        plain.append(cp)

    far_first = (2, 1, 3)

    def cores(s):
        for n, d in enumerate(far_first + (0,)):
            for color in range(2):
                part_at = pl.ds(ring(color, d, True)[1] * ring_part, ring_part)
                first = s * units + (1 - c) * side + color * color_part
                at = pl.ds(first + ring(color, d, True)[1] * ring_part, ring_part)
                go(s, 0, send_to(g.at[at], rc.at[s, color, part_at], s, 0, 2 * n + color, partner))

    def ring_first(s):
        for n, d in enumerate(far_first + (0,)):
            for color in range(2):
                stages[s][0][2 * n + color].wait_recv()
                dev, spot = ring(color, d, True)
                part_at = pl.ds(spot * ring_part, ring_part)
                at = pl.ds(s * units + c * side + color * color_part + spot * ring_part, ring_part)
                h[s, color, part_at] = g[at] + rc[s, color, part_at]
                if d > 0:
                    go(s, 1, send_to(h.at[s, color, part_at], ra.at[s, color, d - 1],
                                     s, 1, 3 * color + d - 1, dev))

    def ring_second(s):
        for color in range(2):
            for cp in stages[s][1][color::2]:
                cp.wait_recv()
            _, spot = ring(color, 0, True)
            sa[s, color] = ((h[s, color, pl.ds(spot * ring_part, ring_part)] + ra[s, color, 0])
                            + (ra[s, color, 1] + ra[s, color, 2]))
            for d in far_first:
                dev, spot = ring(color, d, False)
                go(s, 2, send_to(sa.at[s, color, pl.ds(spot * small, small)],
                                 rb.at[s, color, d - 1], s, 2, 3 * color + d - 1, dev))

    size = 2 * small // OWNERS
    z_order = (4, 3, 5, 2, 6, 1, 7)
    to_z, from_z = [{} for _ in range(SEGMENTS)], [{} for _ in range(SEGMENTS)]
    mine = jnp.minimum(z, OWNERS - 1)

    def along_z(s):
        for color in range(2):
            for cp in stages[s][2][3 * color : 3 * color + 3]:
                cp.wait_recv()
            _, spot = ring(color, 0, False)
            ys[s, color * small : (color + 1) * small] = (
                (sa[s, color, pl.ds(spot * small, small)] + rb[s, color, 0])
                + (rb[s, color, 1] + rb[s, color, 2]))
        for d in z_order:
            dst = lax.rem(z + d, NZ)
            at = pl.ds(jnp.minimum(dst, OWNERS - 1) * size, size)
            cp = send_to(ys.at[s, at], rz.at[s, d - 1], s, 3, d - 1, device(x, y, dst, c))
            pl.when(dst < OWNERS)(cp.start)
            to_z[s][d] = cp

    def spot_of(s, p):
        color = p // (OWNERS // 2)
        chunk_at = jnp.where(color == 0, x * 4 + y, y * 4 + x)
        return (s * units + c * side + color * color_part + chunk_at * small
                + lax.rem(p, OWNERS // 2) * size)

    def back_z(s):
        at = pl.ds(spot_of(s, mine), size)

        @pl.when(z < OWNERS)
        def _():
            total = ys[s, pl.ds(mine * size, size)]
            for d in reversed(z_order):
                to_z[s][d].wait_recv()
                total = total + rz[s, d - 1]
            out_ref[at] = total

        for d in z_order:
            cp = send_to(out_ref.at[at], out_ref.at[at], s, 4, d - 1,
                         device(x, y, lax.rem(z + d, NZ), c))
            pl.when(z < OWNERS)(cp.start)
            from_z[s][d] = cp

    def back_second(s):
        for d in range(1, NZ):
            pl.when(lax.rem(z - d + NZ, NZ) < OWNERS)(from_z[s][d].wait_recv)
        for color in range(2):
            _, spot = ring(color, 0, True)
            _, sub = ring(color, 0, False)
            at = pl.ds(s * units + c * side + color * color_part + spot * ring_part + sub * small,
                       small)
            for d in far_first:
                dev, _ = ring(color, d, False)
                go(s, 5, send_to(out_ref.at[at], out_ref.at[at], s, 5, 3 * color + d - 1, dev))

    def back_first(s):
        for color in range(2):
            for cp in stages[s][5][3 * color : 3 * color + 3]:
                cp.wait_recv()
            _, spot = ring(color, 0, True)
            at = pl.ds(s * units + c * side + color * color_part + spot * ring_part, ring_part)
            for d in far_first:
                dev, _ = ring(color, d, True)
                go(s, 6, send_to(out_ref.at[at], out_ref.at[at], s, 6, 3 * color + d - 1, dev))

    def part_at(s, core, color, d):
        _, spot = ring(color, (4 - d) % 4, True)
        return pl.ds(s * units + core * side + color * color_part + spot * ring_part, ring_part)

    left = []

    def leave(at):
        cp = pltpu.make_async_copy(out_ref.at[at], out_hbm.at[at], leaves.at[len(left)])
        cp.start()
        left.append(cp)

    def hand_over(s, color, d):
        at = part_at(s, c, color, d)
        go(s, 7, send_to(out_ref.at[at], out_ref.at[at], s, 7, 4 * color + d, partner))
        leave(at)

    def back_cores(s):
        for color in range(2):
            hand_over(s, color, 0)
        for d in (1, 3, 2):
            for color in range(2):
                stages[s][6][3 * color + far_first.index(d)].wait_recv()
                hand_over(s, color, d)

    def last(s):
        for n, d in enumerate((0, 1, 3, 2)):
            for color in range(2):
                stages[s][7][2 * n + color].wait_recv()
                leave(part_at(s, 1 - c, color, d))
        for cp in left:
            cp.wait()

    cut = next(r for r in range(count) if 2 * first_block(r + 1, count) > first_block(count, count))
    late = slice(half, rows)

    def some(core, first, stop):
        @pl.when(c == core)
        def _():
            for i in range(first, stop):
                products(i, late, True)

    some(0, cut, count)
    some(1, 0, cut + 1)
    cores(0)
    some(0, 0, cut)
    some(1, cut + 1, count)
    chain = (ring_first, ring_second, along_z, back_z, back_second, back_first, back_cores, last)
    for slot in range(len(chain) + SEGMENTS - 1):
        for s in range(SEGMENTS):
            if 0 <= slot - s < len(chain):
                chain[slot - s](s)

    for ph in range(2):
        for cp in fars[ph] + nears[ph] + pairs[ph]:
            cp.wait_send()
    pl.when(has_to)(halo.wait_send)
    for cp in plain:
        cp.wait_send()
    for s in range(SEGMENTS):
        for d in range(1, NZ):
            pl.when(lax.rem(z + d, NZ) < OWNERS)(to_z[s][d].wait_send)
            pl.when(z < OWNERS)(from_z[s][d].wait_send)


def gram_blocks(signals, channel_node, lags):
    length, chans = signals.shape
    rows = length // NX
    size = lags.shape[0] * NODES
    count = size // NB
    blocks = count * (count + 1) // 2
    side = blocks * 16 // SEGMENTS // 2
    tiles = lambda *lead: pltpu.VMEM(lead + (8, NB), F32)
    quarters = pltpu.VMEM((2, 2, rows // 4, NODES), F32)
    S = SEGMENTS
    dma = pltpu.SemaphoreType.DMA
    total = pl.pallas_call(
        functools.partial(gram_body, lags.shape[0]),
        out_shape=jax.ShapeDtypeStruct((blocks * 16, 8, NB), F32),
        in_specs=[pl.BlockSpec(memory_space=pltpu.SMEM), pl.BlockSpec(memory_space=pl.ANY), VMEM],
        out_specs=pl.BlockSpec(memory_space=pltpu.HBM),
        scratch_shapes=[
            pltpu.VMEM((length, chans), BF16), pltpu.VMEM((length, NODES), F32),
            quarters, quarters, quarters, quarters,
            pltpu.VMEM((rows, NODES), F32), pltpu.VMEM((MAXLAG, NODES), F32),
            pltpu.VMEM((NX, rows + MAXLAG, NODES), F32),
            pltpu.VMEM((rows, size), BF16), pltpu.VMEM((rows, size), BF16),
            tiles(blocks * 16), tiles(S, 2, side // 2), tiles(S, 2, side // 2),
            tiles(S, 2, 3, side // 8), tiles(S, 2, side // 8), tiles(S, 2, 3, side // 32),
            tiles(S, side // 16), tiles(S, NZ - 1, side // 16 // OWNERS),
            tiles(blocks * 16),
            dma((8,)), dma((13,)), dma((13,)), dma((S * 54,)), dma((S * 54,)), dma((16,)),
        ],
        compiler_params=pltpu.CompilerParams(
            collective_id=1, has_side_effects=True, vmem_limit_bytes=56 << 20),
    )(lags, signals, channel_node.reshape(1, chans))
    return total.reshape(blocks, NB, NB)


DOT = dict(precision=lax.Precision.HIGHEST, preferred_element_type=F32)


def lanes(x, c):
    return jnp.broadcast_to(x[:, c : c + 1], x.shape)


def subs(x, r):
    return jnp.broadcast_to(x[r : r + 1, :], x.shape)


def factor_block(rows):
    count = NB // 8
    lane = lax.broadcasted_iota(jnp.int32, (8, NB), 1)
    sub = lax.broadcasted_iota(jnp.int32, (8, NB), 0)
    rows = list(rows)
    upper, inv, merged = [], [], []
    cur = [lanes(rows[0], j) for j in range(8)]
    for p in range(count):
        r0 = 8 * p
        end = count // 2 if p < count // 2 else count
        if p == count // 2:
            above = jnp.concatenate(merged, axis=0)
            product = lax.dot_general(above, above, (((0,), (0,)), ((), ())), **DOT)
            for b in range(p, count):
                rows[b] = jnp.where(lane >= r0, rows[b], 0.0) - product[8 * b : 8 * b + 8]
            cur = [lanes(rows[p], r0 + j) for j in range(8)]
        raw = {b: [lanes(rows[b], r0 + j) for j in range(8)] for b in range(p + 1, end)}
        ahead = [lanes(rows[p + 1], r0 + 8 + j) for j in range(8)] if p + 1 < end else None
        here = jnp.logical_and(lane >= r0, lane < r0 + 8)
        top, low = rows[p], jnp.where(here, jnp.where(lane == sub + r0, 1.0, 0.0), rows[p])
        for b in range(p + 1, end):
            rows[b] = jnp.where(here, 0.0, rows[b])
        v, m, s, rinv = list(cur), [None] * 8, [[None] * 8 for _ in range(8)], [None] * 8
        diag = None
        for j in range(8):
            diag = v[j] if diag is None else jnp.where(sub >= j, v[j], diag)
            rinv[j] = 1.0 / subs(v[j], j)
            whole = v[j] * rinv[j]
            for k in range(j + 1, 8):
                s[j][k] = subs(v[j], k)
                if k == j + 1:
                    v[k] = v[k] - (v[j] * s[j][k]) * rinv[j]
                else:
                    v[k] = v[k] - whole * s[j][k]
            m[j] = jnp.where(sub > j, whole, 0.0)
        rs = lax.rsqrt(diag)
        ra = []
        for j in range(8):
            ra.append(subs(low, j))
            da = subs(top, j)
            low = low - m[j] * ra[j]
            top = top - m[j] * da
        for b in range(p + 1, end):
            u, mb = [], []
            for j in range(8):
                value = raw[b][j]
                for i in range(j):
                    value = value - mb[i] * s[i][j]
                u.append(value)
                mb.append(value * rinv[j])
            if b == p + 1:
                cur = []
                for i in range(8):
                    value = ahead[i]
                    for j in range(8):
                        value = value - mb[j] * subs(u[j], i)
                    cur.append(value)
            for j in range(8):
                rows[b] = rows[b] - mb[j] * ra[j]
        upper.append(jnp.where(lane >= sub + r0, top * rs, 0.0))
        inv.append(jnp.where(lane < r0 + 8, low * rs, 0.0))
        merged.append(jnp.where(lane < NB // 2, inv[-1], upper[-1]))
    return upper, inv


def factor_body(count, scale, g_hbm, out_hbm, g_ref, r_ref, w_ref, d_ref, sem):
    def fetch(k):
        at = pl.ds(first_block(k, count), count - k)
        return pltpu.make_async_copy(g_hbm.at[at], g_ref.at[at], sem.at[count + k])

    for k in range(count):
        fetch(k).start()
    r_ref[...] = jnp.zeros_like(r_ref)

    def leave(k):
        at = pl.ds(k * NB, NB)
        return pltpu.make_async_copy(r_ref.at[at], out_hbm.at[at], sem.at[k])

    def take(k, less):
        fetch(k).wait()
        for j in range(k, count):
            value = g_ref[first_block(k, count) + j - k] * scale
            if less is not None:
                value = value - less[:, (j - k) * NB : (j - k + 1) * NB]
            r_ref[k * NB : (k + 1) * NB, j * NB : (j + 1) * NB] = value

    def update(k):
        r0, r1 = k * NB, (k + 1) * NB
        if k % 2 == 0:
            less = [None, None]
            if k > 0:
                both = lax.dot_general(r_ref[0:r0, r0 : r1 + NB], r_ref[0:r0, r0:],
                                       (((0,), (0,)), ((), ())), **DOT)
                less = [both[:NB], both[NB:, NB:]]
            take(k, less[0])
            take(k + 1, less[1])
        else:
            r_ref[r0:r1, r0:] -= lax.dot_general(
                r_ref[r0 - NB : r0, r0:r1], r_ref[r0 - NB : r0, r0:],
                (((0,), (0,)), ((), ())), **DOT)
        d_ref[...] = r_ref[r0:r1, r0:r1]

    def panel(k):
        r0 = k * NB
        r_ref[r0 : r0 + NB, r0 : r0 + NB] = d_ref[...]
        if k + 1 < count:
            r_ref[r0 : r0 + NB, r0 + NB :] = lax.dot_general(
                w_ref[...], r_ref[r0 : r0 + NB, r0 + NB :], (((1,), (0,)), ((), ())), **DOT
            )
        leave(k).start()

    def step(k, _):
        lax.switch(k, [functools.partial(update, i) for i in range(count)])
        rows, inv = factor_block([d_ref[8 * i : 8 * i + 8, :] for i in range(NB // 8)])
        for i in range(NB // 8):
            d_ref[8 * i : 8 * i + 8, :] = rows[i]
            w_ref[8 * i : 8 * i + 8, :] = inv[i]
        lax.switch(k, [functools.partial(panel, i) for i in range(count)])
        return 0

    lax.fori_loop(0, count, step, 0)
    for k in range(count):
        leave(k).wait()


def upper_factor(blocks, count, scale):
    size = count * NB
    return pl.pallas_call(
        functools.partial(factor_body, count, scale),
        out_shape=jax.ShapeDtypeStruct((size, size), F32),
        in_specs=[pl.BlockSpec(memory_space=pltpu.HBM)],
        out_specs=pl.BlockSpec(memory_space=pltpu.HBM),
        scratch_shapes=[pltpu.VMEM(blocks.shape, F32), pltpu.VMEM((size, size), F32), pltpu.VMEM((NB, NB), F32),
                        pltpu.VMEM((NB, NB), F32), pltpu.SemaphoreType.DMA((2 * count,))],
        compiler_params=pltpu.CompilerParams(vmem_limit_bytes=63_000_000),
    )(blocks)


def on_device(signals, channel_node, lag_offsets):
    total_rows = signals.shape[0] * lax.axis_size("tm")
    count = lag_offsets.shape[0] * NODES // NB
    blocks = gram_blocks(signals, channel_node, lag_offsets)
    return upper_factor(blocks, count, 1.0 / total_rows)


def solution(mesh):
    in_specs = (P("tm", "chan"), P("chan"), P())
    out_specs = P()
    return jax.shard_map(
        on_device, mesh=mesh, in_specs=in_specs, out_specs=out_specs, check_vma=False
    )
```

```python
import functools
import math

import jax
import jax.numpy as jnp
from jax import lax
from jax.experimental import pallas as pl
from jax.experimental.pallas import tpu as pltpu
from jax.sharding import PartitionSpec as P

NODES = 128
CH = 2048
MAXLAG = 512
F32 = jnp.float32
BF16 = jnp.bfloat16
MESH = pl.DeviceIdType.MESH
VMEM = pl.BlockSpec(memory_space=pltpu.VMEM)
NB = 128
NX, NY, NZ = 4, 4, 8
SEGMENTS = 1
OWNERS = 6


def first_block(i, count):
    return i * count - i * (i - 1) // 2


def device(x, y, z, c):
    return {"tm": (y * NZ + z) * 2 + c, "chan": x}


def remote(src, dst, send, recv, target):
    return pltpu.make_async_remote_copy(
        src_ref=src, dst_ref=dst, send_sem=send, recv_sem=recv,
        device_id=target, device_id_type=MESH,
    )


def gram_body(lag_count, lags_ref, s_hbm, node_ref, out_hbm,
              sig, part, far, near, pair, fwd, own, land, rot, hi, lo,
              g, rc, h, ra, sa, rb, ys, rz, out_ref, load, send, recv, ssend, srecv, leaves):
    x, t = lax.axis_index("chan"), lax.axis_index("tm")
    y, z, c = t // (NZ * 2), lax.rem(t // 2, NZ), lax.rem(t, 2)
    rows = own.shape[0]
    half, quarter = rows // 2, rows // 4

    def chunk_of(at):
        return jnp.where(c == 0, at, 3 - at)

    others = (x + 1 - 2 * lax.rem(x, 2), 3 - x)
    opposite = lax.rem(x + 2, 4)
    loads = []
    for ph in range(2):
        for i, at in enumerate((opposite, others[0], others[1], x)):
            rows_at = pl.ds(pl.multiple_of(chunk_of(at) * rows + ph * half, half), half)
            cp = pltpu.make_async_copy(s_hbm.at[rows_at], sig.at[rows_at], load.at[ph * 4 + i])
            cp.start()
            loads.append((cp, rows_at))
    b = chunk_of(x)
    has_to = jnp.logical_or(b > 0, t > 0)
    has_from = jnp.logical_or(b < 3, t < 2 * NY * NZ - 1)
    step = 1 - 2 * c
    to = {"tm": jnp.where(b > 0, t, jnp.maximum(t - 1, 0)), "chan": jnp.where(b > 0, x - step, x)}
    source = {"tm": jnp.where(b < 3, t, jnp.minimum(t + 1, 2 * NY * NZ - 1)),
              "chan": jnp.where(b < 3, x + step, x)}
    barrier = pltpu.get_barrier_semaphore()
    peers = [device(x, y, z, 1 - c)]
    peers += [device(lax.rem(x + d, NX), y, z, c) for d in range(1, NX)]
    peers += [device(x, lax.rem(y + d, NY), z, c) for d in range(1, NY)]
    peers += [device(x, y, lax.rem(z + d, NZ), c) for d in range(1, NZ)]
    for dev in peers:
        pl.semaphore_signal(barrier, inc=1, device_id=dev, device_id_type=MESH)

    @pl.when(has_to)
    def _():
        pl.semaphore_signal(barrier, inc=1, device_id=to, device_id_type=MESH)

    @pl.when(has_from)
    def _():
        pl.semaphore_signal(barrier, inc=1, device_id=source, device_id_type=MESH)

    scale = 1.0 / math.sqrt(CH // NODES)
    chans = node_ref.shape[1]
    match = lax.broadcasted_iota(jnp.int32, (NODES, chans), 0) == node_ref[...]
    onehot = jnp.where(match, scale, 0.0).astype(BF16)

    def sums(ph, i):
        cp, rows_at = loads[ph * 4 + i]
        cp.wait()
        part[rows_at] = lax.dot_general(sig[rows_at], onehot, (((1,), (1,)), ((), ())),
                                        preferred_element_type=F32)

    def piece(at, ph, color):
        first = chunk_of(at) * rows + ph * half + color * quarter
        return pl.ds(pl.multiple_of(first, quarter), quarter)

    link = tuple(device(at, y, z, c) for at in others)

    def copy(src, dst, kind, ph, color, dev):
        s = (kind * 2 + ph) * 2 + color
        return remote(src, dst, send.at[s], recv.at[s], dev)

    sums(0, 0)
    pl.semaphore_wait(barrier, len(peers) + has_to.astype(jnp.int32) + has_from.astype(jnp.int32))
    fars, nears, pairs = [], [], []
    for ph in range(2):
        fars.append([copy(part.at[piece(opposite, ph, k)], far.at[ph, k], 0, ph, k, link[k])
                     for k in range(2)])
        nears.append([copy(part.at[piece(others[k], ph, k)], near.at[ph, k], 1, ph, k, link[k])
                      for k in range(2)])
        pairs.append([copy(fwd.at[ph, k], pair.at[ph, k], 2, ph, k, link[1 - k])
                      for k in range(2)])

    def forward(ph):
        for k in range(2):
            fars[ph][k].wait_recv()
            fwd[ph, k] = part[piece(others[1 - k], ph, k)] + far[ph, k]
            pairs[ph][k].start()

    def finish(ph):
        for k in range(2):
            nears[ph][k].wait_recv()
            pairs[ph][k].wait_recv()
            at = ph * half + k * quarter
            own[at : at + quarter] = part[piece(x, ph, k)] + near[ph, k] + pair[ph, k]

    for cp in fars[0]:
        cp.start()
    sums(0, 1)
    nears[0][0].start()
    sums(0, 2)
    nears[0][1].start()
    for i in range(4):
        sums(1, i)
    sums(0, 3)
    forward(0)
    for cp in fars[1] + nears[1]:
        cp.start()
    finish(0)
    forward(1)
    halo = remote(own.at[0:half], land, send.at[12], recv.at[12], to)
    pl.when(has_to)(halo.start)
    finish(1)

    width = NODES // NX
    per_tile = NB // width
    count = lag_count * NODES // NB
    chunk = 128
    lane_group = lax.broadcasted_iota(jnp.int32, (chunk, NB), 1) // width

    def build(first_step, steps):
        for tile in range(count):
            group, top = tile // (count // NX), tile % (count // NX)

            def fill(i, _):
                value = None
                for m in range(per_tile):
                    first = lags_ref[top * per_tile + m] + i * chunk
                    got = rot[(m - group) % per_tile, pl.ds(first, chunk), :]
                    value = got if value is None else jnp.where(lane_group == m, got, value)
                high = value.astype(BF16)
                at = pl.ds(pl.multiple_of(i * chunk, chunk), chunk)
                hi[at, tile * NB : (tile + 1) * NB] = high
                lo[at, tile * NB : (tile + 1) * NB] = (value - high.astype(F32)).astype(BF16)
                return 0

            lax.fori_loop(first_step, first_step + steps, fill, 0)

    dims = (((0,), (0,)), ((), ()))

    def products(i, at, add):
        a, d = hi[at, i * NB : (i + 1) * NB], lo[at, i * NB : (i + 1) * NB]
        value = lax.dot_general(a, lo[at, i * NB :], dims, preferred_element_type=F32)
        value += lax.dot_general(d, hi[at, i * NB :], dims, preferred_element_type=F32)
        value += lax.dot_general(a, hi[at, i * NB :], dims, preferred_element_type=F32)
        square = lax.dot_general(d, d, dims, preferred_element_type=F32)
        for j in range(i, count):
            spot = 16 * (first_block(i, count) + j - i)
            block = value[:, (j - i) * NB : (j - i + 1) * NB]
            block = (block + square if j == i else block).reshape(16, 8, NB)
            g[spot : spot + 16] = g[spot : spot + 16] + block if add else block

    for r in range(per_tile):
        rot[r, 0:rows] = own[...] if r == 0 else pltpu.roll(own[...], width * r, 1)
    steps = half // chunk
    build(0, steps)
    for i in range(count):
        products(i, slice(0, half), False)

    @pl.when(has_from)
    def _():
        halo.wait_recv()

    @pl.when(jnp.logical_not(has_from))
    def _():
        land[...] = jnp.zeros_like(land)

    for r in range(per_tile):
        rot[r, rows : rows + half] = land[...] if r == 0 else pltpu.roll(land[...], width * r, 1)
    build(steps, steps)

    units = g.shape[0] // SEGMENTS
    side = units // 2
    color_part = side // 2
    ring_part = color_part // 4
    small = ring_part // 4
    sems = iter(range(SEGMENTS * 54))
    ids = [[[next(sems) for _ in range(n)] for n in (8, 6, 6, 7, 7, 6, 6, 8)] for _ in range(SEGMENTS)]

    def ring(color, d, first):
        if (color == 0) == first:
            at = lax.rem(x + d, NX)
            return device(at, y, z, c), at
        at = lax.rem(y + d, NY)
        return device(x, at, z, c), at

    def send_to(src, dst, s, stage, n, dev):
        k = ids[s][stage][n]
        return remote(src, dst, ssend.at[k], srecv.at[k], dev)

    partner = device(x, y, z, 1 - c)
    plain = []
    stages = [[[] for _ in range(8)] for _ in range(SEGMENTS)]

    def go(s, stage, cp):
        cp.start()
        stages[s][stage].append(cp)
        plain.append(cp)

    far_first = (2, 1, 3)

    def cores(s):
        for n, d in enumerate(far_first + (0,)):
            for color in range(2):
                part_at = pl.ds(ring(color, d, True)[1] * ring_part, ring_part)
                first = s * units + (1 - c) * side + color * color_part
                at = pl.ds(first + ring(color, d, True)[1] * ring_part, ring_part)
                go(s, 0, send_to(g.at[at], rc.at[s, color, part_at], s, 0, 2 * n + color, partner))

    def ring_first(s):
        for n, d in enumerate(far_first + (0,)):
            for color in range(2):
                stages[s][0][2 * n + color].wait_recv()
                dev, spot = ring(color, d, True)
                part_at = pl.ds(spot * ring_part, ring_part)
                at = pl.ds(s * units + c * side + color * color_part + spot * ring_part, ring_part)
                h[s, color, part_at] = g[at] + rc[s, color, part_at]
                if d > 0:
                    go(s, 1, send_to(h.at[s, color, part_at], ra.at[s, color, d - 1],
                                     s, 1, 3 * color + d - 1, dev))

    def ring_second(s):
        for color in range(2):
            for cp in stages[s][1][color::2]:
                cp.wait_recv()
            _, spot = ring(color, 0, True)
            sa[s, color] = ((h[s, color, pl.ds(spot * ring_part, ring_part)] + ra[s, color, 0])
                            + (ra[s, color, 1] + ra[s, color, 2]))
            for d in far_first:
                dev, spot = ring(color, d, False)
                go(s, 2, send_to(sa.at[s, color, pl.ds(spot * small, small)],
                                 rb.at[s, color, d - 1], s, 2, 3 * color + d - 1, dev))

    size = 2 * small // OWNERS
    z_order = (4, 3, 5, 2, 6, 1, 7)
    to_z, from_z = [{} for _ in range(SEGMENTS)], [{} for _ in range(SEGMENTS)]
    mine = jnp.minimum(z, OWNERS - 1)

    def along_z(s):
        for color in range(2):
            for cp in stages[s][2][3 * color : 3 * color + 3]:
                cp.wait_recv()
            _, spot = ring(color, 0, False)
            ys[s, color * small : (color + 1) * small] = (
                (sa[s, color, pl.ds(spot * small, small)] + rb[s, color, 0])
                + (rb[s, color, 1] + rb[s, color, 2]))
        for d in z_order:
            dst = lax.rem(z + d, NZ)
            at = pl.ds(jnp.minimum(dst, OWNERS - 1) * size, size)
            cp = send_to(ys.at[s, at], rz.at[s, d - 1], s, 3, d - 1, device(x, y, dst, c))
            pl.when(dst < OWNERS)(cp.start)
            to_z[s][d] = cp

    def spot_of(s, p):
        color = p // (OWNERS // 2)
        chunk_at = jnp.where(color == 0, x * 4 + y, y * 4 + x)
        return (s * units + c * side + color * color_part + chunk_at * small
                + lax.rem(p, OWNERS // 2) * size)

    def back_z(s):
        at = pl.ds(spot_of(s, mine), size)

        @pl.when(z < OWNERS)
        def _():
            total = ys[s, pl.ds(mine * size, size)]
            for d in reversed(z_order):
                to_z[s][d].wait_recv()
                total = total + rz[s, d - 1]
            out_ref[at] = total

        for d in z_order:
            cp = send_to(out_ref.at[at], out_ref.at[at], s, 4, d - 1,
                         device(x, y, lax.rem(z + d, NZ), c))
            pl.when(z < OWNERS)(cp.start)
            from_z[s][d] = cp

    def back_second(s):
        for d in range(1, NZ):
            pl.when(lax.rem(z - d + NZ, NZ) < OWNERS)(from_z[s][d].wait_recv)
        for color in range(2):
            _, spot = ring(color, 0, True)
            _, sub = ring(color, 0, False)
            at = pl.ds(s * units + c * side + color * color_part + spot * ring_part + sub * small,
                       small)
            for d in far_first:
                dev, _ = ring(color, d, False)
                go(s, 5, send_to(out_ref.at[at], out_ref.at[at], s, 5, 3 * color + d - 1, dev))

    def back_first(s):
        for color in range(2):
            for cp in stages[s][5][3 * color : 3 * color + 3]:
                cp.wait_recv()
            _, spot = ring(color, 0, True)
            at = pl.ds(s * units + c * side + color * color_part + spot * ring_part, ring_part)
            for d in far_first:
                dev, _ = ring(color, d, True)
                go(s, 6, send_to(out_ref.at[at], out_ref.at[at], s, 6, 3 * color + d - 1, dev))

    def part_at(s, core, color, d):
        _, spot = ring(color, (4 - d) % 4, True)
        return pl.ds(s * units + core * side + color * color_part + spot * ring_part, ring_part)

    left = []

    def leave(at):
        cp = pltpu.make_async_copy(out_ref.at[at], out_hbm.at[at], leaves.at[len(left)])
        cp.start()
        left.append(cp)

    def hand_over(s, color, d):
        at = part_at(s, c, color, d)
        go(s, 7, send_to(out_ref.at[at], out_ref.at[at], s, 7, 4 * color + d, partner))
        leave(at)

    def back_cores(s):
        for color in range(2):
            hand_over(s, color, 0)
        for d in (1, 3, 2):
            for color in range(2):
                stages[s][6][3 * color + far_first.index(d)].wait_recv()
                hand_over(s, color, d)

    def last(s):
        for n, d in enumerate((0, 1, 3, 2)):
            for color in range(2):
                stages[s][7][2 * n + color].wait_recv()
                leave(part_at(s, 1 - c, color, d))
        for cp in left:
            cp.wait()

    cut = next(r for r in range(count) if 2 * first_block(r + 1, count) > first_block(count, count))
    late = slice(half, rows)

    def some(core, first, stop):
        @pl.when(c == core)
        def _():
            for i in range(first, stop):
                products(i, late, True)

    some(0, cut, count)
    some(1, 0, cut + 1)
    cores(0)
    some(0, 0, cut)
    some(1, cut + 1, count)
    chain = (ring_first, ring_second, along_z, back_z, back_second, back_first, back_cores, last)
    for slot in range(len(chain) + SEGMENTS - 1):
        for s in range(SEGMENTS):
            if 0 <= slot - s < len(chain):
                chain[slot - s](s)

    for ph in range(2):
        for cp in fars[ph] + nears[ph] + pairs[ph]:
            cp.wait_send()
    pl.when(has_to)(halo.wait_send)
    for cp in plain:
        cp.wait_send()
    for s in range(SEGMENTS):
        for d in range(1, NZ):
            pl.when(lax.rem(z + d, NZ) < OWNERS)(to_z[s][d].wait_send)
            pl.when(z < OWNERS)(from_z[s][d].wait_send)


def gram_blocks(signals, channel_node, lags):
    length, chans = signals.shape
    rows = length // NX
    size = lags.shape[0] * NODES
    count = size // NB
    blocks = count * (count + 1) // 2
    side = blocks * 16 // SEGMENTS // 2
    tiles = lambda *lead: pltpu.VMEM(lead + (8, NB), F32)
    quarters = pltpu.VMEM((2, 2, rows // 4, NODES), F32)
    S = SEGMENTS
    dma = pltpu.SemaphoreType.DMA
    total = pl.pallas_call(
        functools.partial(gram_body, lags.shape[0]),
        out_shape=jax.ShapeDtypeStruct((blocks * 16, 8, NB), F32),
        in_specs=[pl.BlockSpec(memory_space=pltpu.SMEM), pl.BlockSpec(memory_space=pl.ANY), VMEM],
        out_specs=pl.BlockSpec(memory_space=pltpu.HBM),
        scratch_shapes=[
            pltpu.VMEM((length, chans), BF16), pltpu.VMEM((length, NODES), F32),
            quarters, quarters, quarters, quarters,
            pltpu.VMEM((rows, NODES), F32), pltpu.VMEM((MAXLAG, NODES), F32),
            pltpu.VMEM((NX, rows + MAXLAG, NODES), F32),
            pltpu.VMEM((rows, size), BF16), pltpu.VMEM((rows, size), BF16),
            tiles(blocks * 16), tiles(S, 2, side // 2), tiles(S, 2, side // 2),
            tiles(S, 2, 3, side // 8), tiles(S, 2, side // 8), tiles(S, 2, 3, side // 32),
            tiles(S, side // 16), tiles(S, NZ - 1, side // 16 // OWNERS),
            tiles(blocks * 16),
            dma((8,)), dma((13,)), dma((13,)), dma((S * 54,)), dma((S * 54,)), dma((16,)),
        ],
        compiler_params=pltpu.CompilerParams(
            collective_id=1, has_side_effects=True, vmem_limit_bytes=56 << 20),
    )(lags, signals, channel_node.reshape(1, chans))
    return total.reshape(blocks, NB, NB)


DOT = dict(precision=lax.Precision.HIGHEST, preferred_element_type=F32)


def lanes(x, c):
    return jnp.broadcast_to(x[:, c : c + 1], x.shape)


def subs(x, r):
    return jnp.broadcast_to(x[r : r + 1, :], x.shape)


def factor_block(rows):
    count = NB // 8
    lane = lax.broadcasted_iota(jnp.int32, (8, NB), 1)
    sub = lax.broadcasted_iota(jnp.int32, (8, NB), 0)
    rows = list(rows)
    upper, inv, merged = [], [], []
    cur = [lanes(rows[0], j) for j in range(8)]
    for p in range(count):
        r0 = 8 * p
        end = count // 2 if p < count // 2 else count
        if p == count // 2:
            above = jnp.concatenate(merged, axis=0)
            product = lax.dot_general(above, above, (((0,), (0,)), ((), ())), **DOT)
            for b in range(p, count):
                rows[b] = jnp.where(lane >= r0, rows[b], 0.0) - product[8 * b : 8 * b + 8]
            cur = [lanes(rows[p], r0 + j) for j in range(8)]
        raw = {b: [lanes(rows[b], r0 + j) for j in range(8)] for b in range(p + 1, end)}
        ahead = [lanes(rows[p + 1], r0 + 8 + j) for j in range(8)] if p + 1 < end else None
        here = jnp.logical_and(lane >= r0, lane < r0 + 8)
        top, low = rows[p], jnp.where(here, jnp.where(lane == sub + r0, 1.0, 0.0), rows[p])
        for b in range(p + 1, end):
            rows[b] = jnp.where(here, 0.0, rows[b])
        v, m, s, rinv = list(cur), [None] * 8, [[None] * 8 for _ in range(8)], [None] * 8
        diag = None
        for j in range(8):
            diag = v[j] if diag is None else jnp.where(sub >= j, v[j], diag)
            rinv[j] = 1.0 / subs(v[j], j)
            whole = v[j] * rinv[j]
            for k in range(j + 1, 8):
                s[j][k] = subs(v[j], k)
                if k == j + 1:
                    v[k] = v[k] - (v[j] * s[j][k]) * rinv[j]
                else:
                    v[k] = v[k] - whole * s[j][k]
            m[j] = jnp.where(sub > j, whole, 0.0)
        rs = lax.rsqrt(diag)
        ra = []
        for j in range(8):
            ra.append(subs(low, j))
            da = subs(top, j)
            low = low - m[j] * ra[j]
            top = top - m[j] * da
        for b in range(p + 1, end):
            u, mb = [], []
            for j in range(8):
                value = raw[b][j]
                for i in range(j):
                    value = value - mb[i] * s[i][j]
                u.append(value)
                mb.append(value * rinv[j])
            if b == p + 1:
                cur = []
                for i in range(8):
                    value = ahead[i]
                    for j in range(8):
                        value = value - mb[j] * subs(u[j], i)
                    cur.append(value)
            for j in range(8):
                rows[b] = rows[b] - mb[j] * ra[j]
        upper.append(jnp.where(lane >= sub + r0, top * rs, 0.0))
        inv.append(jnp.where(lane < r0 + 8, low * rs, 0.0))
        merged.append(jnp.where(lane < NB // 2, inv[-1], upper[-1]))
    return upper, inv


def factor_body(count, scale, g_hbm, out_hbm, g_ref, r_ref, w_ref, d_ref, sem):
    def fetch(k):
        at = pl.ds(first_block(k, count), count - k)
        return pltpu.make_async_copy(g_hbm.at[at], g_ref.at[at], sem.at[count + k])

    for k in range(count):
        fetch(k).start()
    r_ref[...] = jnp.zeros_like(r_ref)

    def leave(k):
        at = pl.ds(k * NB, NB)
        return pltpu.make_async_copy(r_ref.at[at], out_hbm.at[at], sem.at[k])

    def take(k, less):
        fetch(k).wait()
        for j in range(k, count):
            value = g_ref[first_block(k, count) + j - k] * scale
            if less is not None:
                value = value - less[:, (j - k) * NB : (j - k + 1) * NB]
            r_ref[k * NB : (k + 1) * NB, j * NB : (j + 1) * NB] = value

    def update(k):
        r0, r1 = k * NB, (k + 1) * NB
        if k % 2 == 0:
            less = [None, None]
            if k > 0:
                both = lax.dot_general(r_ref[0:r0, r0 : r1 + NB], r_ref[0:r0, r0:],
                                       (((0,), (0,)), ((), ())), **DOT)
                less = [both[:NB], both[NB:, NB:]]
            take(k, less[0])
            if k > 0:
                take(k + 1, less[1])
        else:
            if k == 1:
                take(k, None)
            r_ref[r0:r1, r0:] -= lax.dot_general(
                r_ref[r0 - NB : r0, r0:r1], r_ref[r0 - NB : r0, r0:],
                (((0,), (0,)), ((), ())), **DOT)
        d_ref[...] = r_ref[r0:r1, r0:r1]

    def panel(k):
        r0 = k * NB
        r_ref[r0 : r0 + NB, r0 : r0 + NB] = d_ref[...]
        if k + 1 < count:
            r_ref[r0 : r0 + NB, r0 + NB :] = lax.dot_general(
                w_ref[...], r_ref[r0 : r0 + NB, r0 + NB :], (((1,), (0,)), ((), ())), **DOT
            )
        leave(k).start()

    def step(k, _):
        lax.switch(k, [functools.partial(update, i) for i in range(count)])
        rows, inv = factor_block([d_ref[8 * i : 8 * i + 8, :] for i in range(NB // 8)])
        for i in range(NB // 8):
            d_ref[8 * i : 8 * i + 8, :] = rows[i]
            w_ref[8 * i : 8 * i + 8, :] = inv[i]
        lax.switch(k, [functools.partial(panel, i) for i in range(count)])
        return 0

    lax.fori_loop(0, count, step, 0)
    for k in range(count):
        leave(k).wait()


def upper_factor(blocks, count, scale):
    size = count * NB
    return pl.pallas_call(
        functools.partial(factor_body, count, scale),
        out_shape=jax.ShapeDtypeStruct((size, size), F32),
        in_specs=[pl.BlockSpec(memory_space=pltpu.HBM)],
        out_specs=pl.BlockSpec(memory_space=pltpu.HBM),
        scratch_shapes=[pltpu.VMEM(blocks.shape, F32), pltpu.VMEM((size, size), F32), pltpu.VMEM((NB, NB), F32),
                        pltpu.VMEM((NB, NB), F32), pltpu.SemaphoreType.DMA((2 * count,))],
        compiler_params=pltpu.CompilerParams(vmem_limit_bytes=63_000_000),
    )(blocks)


def on_device(signals, channel_node, lag_offsets):
    total_rows = signals.shape[0] * lax.axis_size("tm")
    count = lag_offsets.shape[0] * NODES // NB
    blocks = gram_blocks(signals, channel_node, lag_offsets)
    return upper_factor(blocks, count, 1.0 / total_rows)


def solution(mesh):
    in_specs = (P("tm", "chan"), P("chan"), P())
    out_specs = P()
    return jax.shard_map(
        on_device, mesh=mesh, in_specs=in_specs, out_specs=out_specs, check_vma=False
    )
```
